32 devices in a mesh: ctx: 8 (over y, x, core), fsdp: 4 (over z).
Axes of the slice: x: 2, y: 2, z: 4, core: 2. Of those that a mesh axis runs over, the one named last changes fastest.
Arguments:
- inputs: bfloat16 [4, 1024, 768], P('fsdp', 'ctx'), may hold values from -6 to 6
- w_query_key: bfloat16 [768, 1536], P('fsdp'), may hold values from -0.25 to 0.25
- w_value: bfloat16 [768, 768], P('fsdp'), may hold values from -0.21875 to 0.21875
- w_out: bfloat16 [768, 768], P('fsdp'), may hold values from -2 to 2
- w_up: bfloat16 [768, 3072], P('fsdp'), may hold values from -0.21875 to 0.21875
- w_down: bfloat16 [3072, 768], P('fsdp'), may hold values from -0.109375 to 0.109375
- bias_query: bfloat16 [768], P('fsdp'), may hold values from -4 to 4
- bias_value: bfloat16 [768], P('fsdp'), may hold values from -0.15625 to 0.15625
- bias_out: bfloat16 [768], P('fsdp'), may hold values from -4 to 4
- gain_attn: bfloat16 [768], P('fsdp'), may hold values from 0.5 to 1.5
- shift_attn: bfloat16 [768], P('fsdp'), may hold values from -3 to 3
- bias_up: bfloat16 [3072], P('fsdp'), may hold values from -4 to 4
- bias_down: bfloat16 [768], P('fsdp'), may hold values from -4 to 4
- gain_ffn: bfloat16 [768], P('fsdp'), may hold values from 0.5 to 1.5
- shift_ffn: bfloat16 [768], P('fsdp'), may hold values from -3 to 3
- cotangent: bfloat16 [4, 1024, 768], P('fsdp', 'ctx'), may hold values from -6 to 6
Outputs:
- output: bfloat16 [4, 1024, 768], P('fsdp', 'ctx')
- grad_inputs: float32 [4, 1024, 768], P('fsdp', 'ctx')
- grad_w_query_key: float32 [768, 1536], P(('ctx', 'fsdp'))
- grad_w_value: float32 [768, 768], P(('ctx', 'fsdp'))
- grad_w_out: float32 [768, 768], P(('ctx', 'fsdp'))
- grad_w_up: float32 [768, 3072], P(('ctx', 'fsdp'))
- grad_w_down: float32 [3072, 768], P(('ctx', 'fsdp'))
- grad_bias_query: float32 [768], P(('ctx', 'fsdp'))
- grad_bias_value: float32 [768], P(('ctx', 'fsdp'))
- grad_bias_out: float32 [768], P(('ctx', 'fsdp'))
- grad_gain_attn: float32 [768], P(('ctx', 'fsdp'))
- grad_shift_attn: float32 [768], P(('ctx', 'fsdp'))
- grad_bias_up: float32 [3072], P(('ctx', 'fsdp'))
- grad_bias_down: float32 [768], P(('ctx', 'fsdp'))
- grad_gain_ffn: float32 [768], P(('ctx', 'fsdp'))
- grad_shift_ffn: float32 [768], P(('ctx', 'fsdp'))
The draws below stay inside these ranges and needn't reach their ends.
All inputs are finite; a program needn't handle non-finite values.
Results may differ from the reference program's by a relative error of at most 0.024.
Values may be sent and summed in bfloat16 or wider, within the bound.
No kernel may reach another device: no remote copies, remote signals or barrier semaphores. Data moves between devices by JAX's collectives and lax.ppermute only.
A program may use at most 256 MiB of HBM per device.

```python
import math
import jax
import jax.numpy as jnp
from jax import lax

D = 768
HEADS = 12
HEAD = 64
FF = 3072
SEQS = 4
LEN = 1024


def block_levels(own_key, dims, split, least, largest):
    gain = 1.0
    for position, parts in split:
        heights = jax.random.uniform(jax.random.fold_in(jax.random.fold_in(own_key, 6), position), (parts,), jnp.float32, least / len(split), largest / len(split))
        gain = gain * jnp.repeat(jnp.exp(heights), dims[position] // parts).reshape((-1,) + (1,) * (len(dims) - 1 - position))
    return gain


def scatter_about(stream_key, shape, scale, limit, cuts=(), kind=jnp.bfloat16):
    factor_of = block_levels(stream_key, shape, cuts, -0.22, 0.18) if cuts else 1.0
    values = jax.random.normal(stream_key, shape, jnp.float32) * scale * factor_of
    return jnp.minimum(jnp.maximum(values, -limit), limit).astype(kind)


def setup_inputs(seed: int = 0) -> dict:
    streams_of = jax.random.split(jax.random.key(seed), 17)
    inputs = scatter_about(streams_of[0], (SEQS, LEN, D), 1.0, 6.0, ((0, 4), (1, 8)))
    w_query_key = scatter_about(streams_of[1], (D, 2 * D), (D * 2 // 3) ** -0.5, 0.25, ((0, 4),))
    w_value = scatter_about(streams_of[2], (D, D), D ** -0.5, 0.21875, ((0, 4),))
    w_out = scatter_about(streams_of[3], (D, D), (max(1, 10 * D // LEN)) ** -0.5, 2.0, ((0, 4),))
    w_up = scatter_about(streams_of[4], (D, FF), D ** -0.5, 0.21875, ((0, 4),))
    w_down = scatter_about(streams_of[5], (FF, D), FF ** -0.5, 0.109375, ((0, 4),))
    bias_query = scatter_about(streams_of[6], (D,), 0.3, 4.0, ((0, 4),))
    bias_value = scatter_about(streams_of[7], (D,), (8.0 / D), 0.15625, ((0, 4),))
    bias_out = scatter_about(streams_of[8], (D,), 0.3, 4.0, ((0, 4),))
    gain_attn = jnp.clip(1.0 + 0.1 * jax.random.normal(streams_of[9], (D,), jnp.float32), 0.5, 1.5).astype(jnp.bfloat16)
    shift_attn = scatter_about(streams_of[10], (D,), 0.2, 3.0, ((0, 4),))
    bias_up = scatter_about(streams_of[11], (FF,), 0.3, 4.0, ((0, 4),))
    bias_down = scatter_about(streams_of[12], (D,), 0.3, 4.0, ((0, 4),))
    gain_ffn = jnp.clip(1.0 + 0.1 * jax.random.normal(streams_of[13], (D,), jnp.float32), 0.5, 1.5).astype(jnp.bfloat16)
    shift_ffn = scatter_about(streams_of[14], (D,), 0.2, 3.0, ((0, 4),))
    cotangent = scatter_about(streams_of[15], (SEQS, LEN, D), 1.0, 6.0, ((0, 4), (1, 8)))
    return dict(inputs=inputs, w_query_key=w_query_key, w_value=w_value, w_out=w_out, w_up=w_up, w_down=w_down, bias_query=bias_query, bias_value=bias_value, bias_out=bias_out, gain_attn=gain_attn, shift_attn=shift_attn, bias_up=bias_up, bias_down=bias_down, gain_ffn=gain_ffn, shift_ffn=shift_ffn, cotangent=cotangent)


full_precision = lax.Precision.HIGHEST

@jax.custom_vjp
def low(v):
    return lax.optimization_barrier(v.astype(jnp.bfloat16)).astype(jnp.float32)

@jax.custom_vjp
def low_back(v):
    return v

def low_keep(v):
    return (low(v), None)

def low_pass(kept, grad):
    return (grad,)

def back_keep(v):
    return (v, None)

def back_low(kept, grad):
    return (low(grad),)
low.defvjp(low_keep, low_pass)
low_back.defvjp(back_keep, back_low)

def layer_norm(inputs, norm_gain, norm_shift):
    centre = inputs - lax.optimization_barrier(jnp.mean(inputs, axis=-1, keepdims=True))
    spread = lax.optimization_barrier(jnp.mean(centre * centre, axis=-1, keepdims=True))
    return centre * lax.rsqrt(spread + 1e-05) * norm_gain + norm_shift

def attend_sequence(triple):
    queries, keys, values = triple
    block = math.gcd(LEN, 512)
    blocks = queries.reshape(LEN // block, block, HEADS, HEAD)

    @jax.checkpoint
    def one_block(query_block):
        scores = jnp.einsum('qhd,khd->hqk', query_block, keys, precision=full_precision)
        scores = low_back(scores) * 0.125
        weights = low(jax.nn.softmax(scores, axis=-1))
        return jnp.einsum('hqk,khd->qhd', weights, values, precision=full_precision)
    return lax.map(one_block, blocks).reshape(LEN, HEADS * HEAD)

def forward(inputs, w_query_key, w_value, w_out, w_up, w_down, bias_query, bias_value, bias_out, gain_attn, shift_attn, bias_up, bias_down, gain_ffn, shift_ffn):
    flat = inputs.reshape(SEQS * LEN, D)
    query_key = jnp.dot(flat, w_query_key, precision=full_precision)
    queries = low(low_back(query_key[:, :D] + bias_query))
    keys = low(low_back(query_key[:, D:]))
    values = low(low_back(jnp.dot(flat, w_value, precision=full_precision) + bias_value))
    shaped = (queries.reshape(SEQS, LEN, HEADS, HEAD), keys.reshape(SEQS, LEN, HEADS, HEAD), values.reshape(SEQS, LEN, HEADS, HEAD))
    attended = lax.map(attend_sequence, shaped).reshape(SEQS * LEN, D)
    attended = low(low_back(attended))
    branch = low_back(jnp.dot(attended, w_out, precision=full_precision) + bias_out)
    first = layer_norm(flat + branch, gain_attn, shift_attn)
    hidden = low_back(jnp.dot(low(first), w_up, precision=full_precision) + bias_up)
    activ = low(jax.nn.gelu(hidden, approximate=False))
    second = low_back(jnp.dot(activ, w_down, precision=full_precision) + bias_down)
    output = layer_norm(first + second, gain_ffn, shift_ffn)
    return output.reshape(SEQS, LEN, D)

def reference(inputs, w_query_key, w_value, w_out, w_up, w_down, bias_query, bias_value, bias_out, gain_attn, shift_attn, bias_up, bias_down, gain_ffn, shift_ffn, cotangent):
    floats = [arr.astype(jnp.float32) for arr in (inputs, w_query_key, w_value, w_out, w_up, w_down, bias_query, bias_value, bias_out, gain_attn, shift_attn, bias_up, bias_down, gain_ffn, shift_ffn)]
    output, pullback = jax.vjp(forward, *floats)
    grads = pullback(cotangent.astype(jnp.float32))
    return (output.astype(jnp.bfloat16), grads[0], grads[1], grads[2], grads[3], grads[4], grads[5], grads[6], grads[7], grads[8], grads[9], grads[10], grads[11], grads[12], grads[13], grads[14])
```

```python
import functools
import math

import jax
import jax.numpy as jnp
from jax import lax
from jax.experimental import pallas as pl
from jax.experimental.pallas import tpu as pltpu
from jax.sharding import PartitionSpec as P

HEADS = 12
HEAD = 64


def norm_apply(inputs, norm_gain, norm_shift):
    centre = inputs - jnp.mean(inputs, axis=-1, keepdims=True)
    spread = jnp.mean(centre * centre, axis=-1, keepdims=True)
    return centre * lax.rsqrt(spread + 1e-05) * norm_gain + norm_shift


def left_product(left, right):
    return lax.dot_general(
        left, right, (((0,), (0,)), ((), ())), preferred_element_type=jnp.float32
    )


def right_product(left, right):
    return lax.dot_general(
        left, right, (((1,), (1,)), ((), ())), preferred_element_type=jnp.float32
    )


def column_sums(matrix):
    return jnp.sum(matrix.astype(jnp.float32), axis=0)


def per_device(
    inputs,
    w_query_key,
    w_value,
    w_out,
    w_up,
    w_down,
    bias_query,
    bias_value,
    bias_out,
    gain_attn,
    shift_attn,
    bias_up,
    bias_down,
    gain_ffn,
    shift_ffn,
    cotangent,
):
    gathered = (
        lax.all_gather(w_query_key, "fsdp", axis=0, tiled=True),
        lax.all_gather(w_value, "fsdp", axis=0, tiled=True),
        lax.all_gather(w_out, "fsdp", axis=0, tiled=True),
        lax.all_gather(w_up, "fsdp", axis=0, tiled=True),
        lax.all_gather(w_down, "fsdp", axis=0, tiled=True),
        lax.all_gather(bias_query, "fsdp", axis=0, tiled=True),
        lax.all_gather(bias_value, "fsdp", axis=0, tiled=True),
        lax.all_gather(bias_out, "fsdp", axis=0, tiled=True),
        lax.all_gather(gain_attn, "fsdp", axis=0, tiled=True),
        lax.all_gather(shift_attn, "fsdp", axis=0, tiled=True),
        lax.all_gather(bias_up, "fsdp", axis=0, tiled=True),
        lax.all_gather(bias_down, "fsdp", axis=0, tiled=True),
        lax.all_gather(gain_ffn, "fsdp", axis=0, tiled=True),
        lax.all_gather(shift_ffn, "fsdp", axis=0, tiled=True),
    )
    full_qk, full_value, full_out, full_up, full_down = (
        gathered[0],
        gathered[1],
        gathered[2],
        gathered[3],
        gathered[4],
    )
    smalls = [piece.astype(jnp.float32) for piece in gathered[5:]]
    (
        vec_query,
        vec_value,
        vec_out,
        vec_gain_one,
        vec_shift_one,
        vec_up,
        vec_down,
        vec_gain_two,
        vec_shift_two,
    ) = smalls
    rows = inputs.shape[1]
    width = inputs.shape[2]
    heads = HEADS
    head = HEAD
    tokens = inputs.reshape(rows, width)
    tok_float = tokens.astype(jnp.float32)
    query_key = jnp.dot(tokens, full_qk, preferred_element_type=jnp.float32)
    queries = (query_key[:, :width] + vec_query).astype(jnp.bfloat16)
    keys = query_key[:, width:].astype(jnp.bfloat16)
    values = (jnp.dot(tokens, full_value, preferred_element_type=jnp.float32) + vec_value).astype(
        jnp.bfloat16
    )
    query_heads = queries.reshape(rows, heads, head)
    start_state = (
        jnp.full((heads, rows), -1e30, jnp.float32),
        jnp.zeros((heads, rows), jnp.float32),
        jnp.zeros((rows, heads, head), jnp.float32),
    )
    carry = start_state
    key_piece = lax.all_gather(keys, "ctx", axis=0, tiled=True)
    value_piece = lax.all_gather(values, "ctx", axis=0, tiled=True)
    count = key_piece.shape[0]
    block = math.gcd(count, 2048)
    key_split = key_piece.reshape(count // block, block, heads, head)
    value_split = value_piece.reshape(count // block, block, heads, head)

    def step_block(state, pair):
        running_max, running_sum, running_acc = state
        key_block, value_block = pair
        scores = (
            jnp.einsum("qhd,khd->hqk", query_heads, key_block, preferred_element_type=jnp.float32)
            * 0.125
        )
        new_max = jnp.maximum(running_max, jnp.max(scores, axis=-1))
        factor = jnp.exp(running_max - new_max)
        weights = jnp.exp(scores - new_max[:, :, None])
        running_sum = running_sum * factor + jnp.sum(weights, axis=-1)
        update = jnp.einsum(
            "hqk,khd->qhd",
            weights.astype(jnp.bfloat16),
            value_block,
            preferred_element_type=jnp.float32,
        )
        running_acc = running_acc * jnp.transpose(factor)[:, :, None] + update
        return ((new_max, running_sum, running_acc), None)

    carry, unused = lax.scan(step_block, carry, (key_split, value_split))
    final_max, final_sum, final_acc = carry
    attended_heads = final_acc / jnp.transpose(final_sum)[:, :, None]
    log_total = final_max + jnp.log(final_sum)
    attended_low = attended_heads.reshape(rows, width).astype(jnp.bfloat16)
    branch = jnp.dot(attended_low, full_out, preferred_element_type=jnp.float32) + vec_out
    first, norm_one_pull = jax.vjp(norm_apply, tok_float + branch, vec_gain_one, vec_shift_one)
    first_low = first.astype(jnp.bfloat16)
    hidden = jnp.dot(first_low, full_up, preferred_element_type=jnp.float32) + vec_up
    activ, gelu_pull = jax.vjp(functools.partial(jax.nn.gelu, approximate=False), hidden)
    activ_low = activ.astype(jnp.bfloat16)
    second = jnp.dot(activ_low, full_down, preferred_element_type=jnp.float32) + vec_down
    output, norm_two_pull = jax.vjp(norm_apply, first + second, vec_gain_two, vec_shift_two)
    grad_resid_two, grad_gain_ffn, grad_shift_ffn = norm_two_pull(
        cotangent.reshape(rows, width).astype(jnp.float32)
    )
    second_low = grad_resid_two.astype(jnp.bfloat16)
    grad_w_down = left_product(activ_low, second_low)
    grad_bias_down = column_sums(second_low)
    grad_activ = right_product(second_low, full_down)
    hidden_low = gelu_pull(grad_activ)[0].astype(jnp.bfloat16)
    grad_w_up = left_product(first_low, hidden_low)
    grad_bias_up = column_sums(hidden_low)
    grad_first = grad_resid_two + right_product(hidden_low, full_up)
    grad_resid_one, grad_gain_attn, grad_shift_attn = norm_one_pull(grad_first)
    branch_low = grad_resid_one.astype(jnp.bfloat16)
    grad_w_out = left_product(attended_low, branch_low)
    grad_bias_out = column_sums(branch_low)
    dout_low = right_product(branch_low, full_out).astype(jnp.bfloat16)
    dout_heads = dout_low.reshape(rows, heads, head)
    delta = jnp.einsum("qhd,qhd->hq", dout_heads.astype(jnp.float32), attended_heads)
    all_keys, all_values = (
        lax.all_gather(keys, "ctx", axis=0, tiled=True),
        lax.all_gather(values, "ctx", axis=0, tiled=True),
    )
    total = all_keys.shape[0]
    key_total = all_keys.shape[0]
    block = math.gcd(key_total, 2048)

    def back_block(grad_query, pair):
        key_block, value_block = pair
        scores = (
            jnp.einsum("qhd,khd->hqk", query_heads, key_block, preferred_element_type=jnp.float32)
            * 0.125
        )
        weights = jnp.exp(scores - log_total[:, :, None])
        weight_grad = jnp.einsum(
            "qhd,khd->hqk", dout_heads, value_block, preferred_element_type=jnp.float32
        )
        score_grad = (weights * (weight_grad - delta[:, :, None]) * 0.125).astype(jnp.bfloat16)
        grad_query = grad_query + jnp.einsum(
            "hqk,khd->qhd", score_grad, key_block, preferred_element_type=jnp.float32
        )
        value_grad = jnp.einsum(
            "hqk,qhd->khd",
            weights.astype(jnp.bfloat16),
            dout_heads,
            preferred_element_type=jnp.float32,
        )
        key_grad = jnp.einsum(
            "hqk,qhd->khd", score_grad, query_heads, preferred_element_type=jnp.float32
        )
        return (grad_query, (key_grad, value_grad))

    grad_query, terms = lax.scan(
        back_block,
        jnp.zeros((rows, heads, head), jnp.float32),
        (
            all_keys.reshape(key_total // block, block, heads, head),
            all_values.reshape(key_total // block, block, heads, head),
        ),
    )
    grad_keys, grad_values = (
        lax.psum_scatter(terms[0].reshape(total, width), "ctx", scatter_dimension=0, tiled=True),
        lax.psum_scatter(terms[1].reshape(total, width), "ctx", scatter_dimension=0, tiled=True),
    )
    grad_queries = grad_query.reshape(rows, width)
    query_low = grad_queries.astype(jnp.bfloat16)
    key_low = grad_keys.astype(jnp.bfloat16)
    value_low = grad_values.astype(jnp.bfloat16)
    query_key_low = jnp.concatenate([query_low, key_low], axis=1)
    grad_w_query_key = left_product(tokens, query_key_low)
    grad_w_value = left_product(tokens, value_low)
    grad_bias_query = column_sums(query_low)
    grad_bias_value = column_sums(value_low)
    grad_inputs = (
        grad_resid_one
        + right_product(query_key_low, full_qk)
        + right_product(value_low, full_value)
    )
    summed = (
        lax.psum_scatter(grad_w_query_key, ("ctx", "fsdp"), scatter_dimension=0, tiled=True),
        lax.psum_scatter(grad_w_value, ("ctx", "fsdp"), scatter_dimension=0, tiled=True),
        lax.psum_scatter(grad_w_out, ("ctx", "fsdp"), scatter_dimension=0, tiled=True),
        lax.psum_scatter(grad_w_up, ("ctx", "fsdp"), scatter_dimension=0, tiled=True),
        lax.psum_scatter(grad_w_down, ("ctx", "fsdp"), scatter_dimension=0, tiled=True),
        lax.psum_scatter(grad_bias_query, ("ctx", "fsdp"), scatter_dimension=0, tiled=True),
        lax.psum_scatter(grad_bias_value, ("ctx", "fsdp"), scatter_dimension=0, tiled=True),
        lax.psum_scatter(grad_bias_out, ("ctx", "fsdp"), scatter_dimension=0, tiled=True),
        lax.psum_scatter(grad_gain_attn, ("ctx", "fsdp"), scatter_dimension=0, tiled=True),
        lax.psum_scatter(grad_shift_attn, ("ctx", "fsdp"), scatter_dimension=0, tiled=True),
        lax.psum_scatter(grad_bias_up, ("ctx", "fsdp"), scatter_dimension=0, tiled=True),
        lax.psum_scatter(grad_bias_down, ("ctx", "fsdp"), scatter_dimension=0, tiled=True),
        lax.psum_scatter(grad_gain_ffn, ("ctx", "fsdp"), scatter_dimension=0, tiled=True),
        lax.psum_scatter(grad_shift_ffn, ("ctx", "fsdp"), scatter_dimension=0, tiled=True),
    )
    return (
        output.astype(jnp.bfloat16).reshape(1, rows, width),
        grad_inputs.reshape(1, rows, width),
        summed[0],
        summed[1],
        summed[2],
        summed[3],
        summed[4],
        summed[5],
        summed[6],
        summed[7],
        summed[8],
        summed[9],
        summed[10],
        summed[11],
        summed[12],
        summed[13],
    )


BF = jnp.bfloat16
F32 = jnp.float32


def local_call(body, outs, args, name, scratch=(), flops=0, moved=0):
    spec = pl.BlockSpec(memory_space=pltpu.VMEM)
    moved = moved or sum(a.size * a.dtype.itemsize for a in args)
    return pl.pallas_call(
        body,
        out_shape=tuple(jax.ShapeDtypeStruct(s, d) for s, d in outs),
        in_specs=[spec] * len(args),
        out_specs=tuple(spec for _ in outs),
        scratch_shapes=list(scratch),
        compiler_params=pltpu.CompilerParams(vmem_limit_bytes=48 * 1024 * 1024),
        cost_estimate=pl.CostEstimate(flops=flops, bytes_accessed=moved, transcendentals=0),
        name=name,
    )(*args)


def place():
    c = lax.axis_index("ctx")
    return c // 2, c % 2, lax.axis_index("fsdp")


def mm(a, b):
    return jnp.dot(a, b, preferred_element_type=F32)


def mm_nt(a, b):
    return lax.dot_general(a, b, (((1,), (1,)), ((), ())), preferred_element_type=F32)


def mm_tn(a, b):
    return lax.dot_general(a, b, (((0,), (0,)), ((), ())), preferred_element_type=F32)


def rows_at(start, size, step):
    return pl.ds(pl.multiple_of(start, step), size)


def pack_qkv(w_qk, w_v, *rest):
    vecs, (own, other, tmp) = rest[:9], rest[9:]
    k, h, f = place()
    tmp[...] = jnp.zeros_like(tmp)
    for i in range(8):
        tmp[i : i + 1, 0:192] = vecs[i][...].astype(F32)
    up = vecs[8][...].astype(F32)
    tmp[8:9, :] = up[:, 0:640]
    tmp[9:10, 0:128] = up[:, 640:768]
    small = tmp[...].astype(BF)
    for out, half in ((own, h), (other, 1 - h)):
        rows = rows_at(half * 96, 96, 16)
        out[96:112, :] = small
        out[0:96, 512:640] = jnp.zeros((96, 128), BF)
        for kk in range(4):

            @pl.when(k == kk)
            def _():
                out[0:96, 0:192] = w_qk[rows, 192 * kk : 192 * kk + 192]
                out[0:96, 192:384] = w_qk[rows, 768 + 192 * kk : 960 + 192 * kk]
                out[0:96, 384:576] = w_v[rows, 192 * kk : 192 * kk + 192]


def qkv_body(x0, x1, x2, x3, own, other, p1, p2, p3, m1, m2, m3, q, kv, w, vecs, up, tmp):
    k, h, f = place()
    for s, (mine, mate) in enumerate(((own, other), (p1, m1), (p2, m2), (p3, m3))):
        g = lax.rem(f + 4 - s, 4)
        w[rows_at(192 * g + 96 * h, 96, 16), :] = mine[0:96, :]
        w[rows_at(192 * g + 96 * (1 - h), 96, 16), :] = mate[0:96, :]
        tmp[g] = mine[96:112, :].astype(F32)
    for g in range(4):
        vecs[:, 192 * g : 192 * g + 192] = tmp[g, 0:8, 0:192]
    up[:, 0:640] = tmp[k, 8:9, :]
    up[:, 640:768] = tmp[k, 9:10, 0:128]
    bias_q = tmp[k, 0:1, 0:192]
    bias_v = tmp[k, 1:2, 0:192]
    for j, x in enumerate((x0, x1, x2, x3)):
        r = mm(x[...], w[:, 0:576])
        rows = slice(128 * j, 128 * j + 128)
        rq = (r[:, 0:192] + bias_q).astype(BF)
        rk = r[:, 192:384].astype(BF)
        rv = (r[:, 384:576] + bias_v).astype(BF)
        for i in range(3):
            q[i, rows, :] = rq[:, 64 * i : 64 * i + 64]
            kv[i, rows, :] = rk[:, 64 * i : 64 * i + 64]
            kv[3 + i, rows, :] = rv[:, 64 * i : 64 * i + 64]


def spread_body(p0, p1, p2, p3, up, d0, d1, d2, d3, tmp):
    k, h, f = place()
    for s, p in enumerate((p0, p1, p2, p3)):
        g = lax.rem(f + 4 - s, 4)
        up[g] = p[0:96, :]
        tmp[g] = p[96:216, :].astype(F32)
    for j, d in enumerate((d0, d1, d2, d3)):
        d[0:96, :] = tmp[k ^ j, 0:96, :].astype(BF)
        for g in range(4):
            d[96 + 24 * g : 120 + 24 * g, :] = tmp[g, 96:120, :].astype(BF)


def settle_body(u, d0, d1, d2, d3, mu, e0, e1, e2, e3, w_up, w_down, w_out, tmp):
    k, h, f = place()
    for g in range(4):
        w_up[rows_at(192 * g + 96 * h, 96, 16), :] = u[g]
        w_up[rows_at(192 * g + 96 * (1 - h), 96, 16), :] = mu[g]
    for half, parts in ((h, (d0, d1, d2, d3)), (1 - h, (e0, e1, e2, e3))):
        for j, d in enumerate(parts):
            kk = k ^ j
            w_down[rows_at(192 * kk + 96 * half, 96, 16), :] = d[0:96, :]
            for g in range(4):
                tmp[rows_at(192 * g + 48 * kk + 24 * half, 24, 8), :] = d[96 + 24 * g : 120 + 24 * g, :].astype(F32)
    w_out[...] = tmp[...].astype(BF)


def attend_body(q, kv, mate, packed, att, lse):
    for i in range(3):
        for t in range(4):
            rows = slice(128 * t, 128 * t + 128)
            qt = q[i, rows, :]
            sa = mm_nt(qt, kv[i]) * 0.125
            sb = mm_nt(qt, mate[i]) * 0.125
            top = jnp.maximum(jnp.max(sa, axis=1, keepdims=True), jnp.max(sb, axis=1, keepdims=True))
            ea = jnp.exp(sa - top)
            eb = jnp.exp(sb - top)
            total = jnp.sum(ea, axis=1, keepdims=True) + jnp.sum(eb, axis=1, keepdims=True)
            acc = mm(ea.astype(BF), kv[3 + i]) + mm(eb.astype(BF), mate[3 + i])
            out = acc / total
            att[i, rows, :] = out
            lse[i, rows, :] = top + jnp.log(total)
            col = 192 * (t // 2) + 64 * i
            packed[128 * (t % 2) : 128 * (t % 2) + 128, col : col + 64] = out.astype(BF)


def norm_parts(v):
    centre = v - jnp.mean(v, axis=1, keepdims=True)
    inv = lax.rsqrt(jnp.mean(centre * centre, axis=1, keepdims=True) + 1e-05)
    return centre * inv, inv


def branch_body(a0, a1, a2, a3, x0, x1, x2, x3, w_out, vecs, low, first, hat, inv):
    k, h, f = place()
    parts = (a0, a1, a2, a3)
    for m, x in enumerate((x0, x1, x2, x3)):
        acc = x[...].astype(F32) + vecs[2:3, :]
        for j in range(4):
            b = j ^ m
            a = parts[j][128 * (b % 2) : 128 * (b % 2) + 128, 192 * (b // 2) : 192 * (b // 2) + 192]
            acc = acc + mm(a, w_out[rows_at(192 * (k ^ j), 192, 16), :])
        n, r = norm_parts(acc)
        y = n * vecs[3:4, :] + vecs[4:5, :]
        low[128 * m : 128 * m + 128, :] = y.astype(BF)
        if m == 0:
            first[...] = y
            hat[...] = n
            inv[...] = r


def feed_body(low, w_up, w_down, up, own, s1, s2, s3, act, slope):
    for m, out in ((1, s1), (2, s2), (3, s3), (0, own)):
        rows = slice(128 * m, 128 * m + 128)
        hid = mm(low[rows, :], w_up[...]) + up[...]
        cdf = 0.5 * (1.0 + lax.erf(hid * (2.0**-0.5)))
        pdf = jnp.exp(hid * hid * -0.5) * ((2.0 * math.pi) ** -0.5)
        a = (hid * cdf).astype(BF)
        act[rows, :] = a
        slope[rows, :] = (cdf + hid * pdf).astype(BF)
        out[...] = mm(a, w_down[...]).astype(out.dtype)


def second_body(own, r1, r2, r3, first, vecs, cot, out, grad, low, sums):
    v = own[...] + r1[...].astype(F32) + r2[...].astype(F32) + r3[...].astype(F32)
    n, inv = norm_parts(v + first[...] + vecs[5:6, :])
    out[...] = (n * vecs[6:7, :] + vecs[7:8, :]).astype(BF)
    dy = cot[...].astype(F32)
    g, lowered = norm_back(dy, n, inv, vecs[6:7, :])
    grad[...] = g
    low[...] = lowered
    sums[...] = jnp.zeros_like(sums)
    sums[0:1, :] = jnp.sum(dy * n, axis=0, keepdims=True)
    sums[1:2, :] = jnp.sum(dy, axis=0, keepdims=True)
    sums[2:3, :] = jnp.sum(lowered.astype(F32), axis=0, keepdims=True)


def norm_back(dy, n, inv, gain):
    d = dy * gain
    g = inv * (d - jnp.mean(d, axis=1, keepdims=True) - n * jnp.mean(d * n, axis=1, keepdims=True))
    return g, g.astype(BF)


def feed_back_body(d0, d1, d2, d3, w_up, w_down, slope, own, s1, s2, s3, dhid):
    for m, d, out in ((1, d1, s1), (2, d2, s2), (3, d3, s3), (0, d0, own)):
        rows = slice(128 * m, 128 * m + 128)
        da = mm_nt(d[...], w_down[...])
        dh = (da * slope[rows, :].astype(F32)).astype(BF)
        dhid[rows, :] = dh
        out[...] = mm_nt(dh, w_up[...]).astype(out.dtype)


def feed_grad_body(act, low, d0, d1, d2, d3, dhid, keep, send, full, ds):
    k, h, f = place()
    for m, d in enumerate((d0, d1, d2, d3)):
        ds[128 * m : 128 * m + 128, :] = d[...]
    full[...] = mm_tn(act[...], ds[...])
    keep[0:384, :] = full[rows_at(384 * h, 384, 8), :]
    send[0:384, :] = full[rows_at(384 * (1 - h), 384, 8), :].astype(BF)
    full[...] = mm_tn(low[...], dhid[...])
    for kk in range(4):
        at = slice(384 + 96 * kk, 480 + 96 * kk)
        keep[at, :] = full[rows_at(192 * kk + 96 * h, 96, 8), :]
        send[at, :] = full[rows_at(192 * kk + 96 * (1 - h), 96, 8), :].astype(BF)
    total = jnp.sum(dhid[...].astype(F32), axis=0, keepdims=True)
    lo, hi = total[:, 0:384], total[:, 384:768]
    keep[768:784, :] = jnp.zeros((16, 768), F32)
    keep[768:769, 0:384] = jnp.where(h == 0, lo, hi)
    full[0:16, :] = jnp.zeros((16, 768), F32)
    full[0:1, 0:384] = jnp.where(h == 0, hi, lo)
    send[768:784, :] = full[0:16, :].astype(BF)


def first_back_body(own, r1, r2, r3, grad, hat, inv, vecs, out, low, sums):
    dy = own[...] + r1[...].astype(F32) + r2[...].astype(F32) + r3[...].astype(F32) + grad[...]
    n = hat[...]
    g, lowered = norm_back(dy, n, inv[...], vecs[3:4, :])
    out[...] = g
    low[...] = lowered
    sums[...] = jnp.zeros_like(sums)
    sums[0:1, :] = jnp.sum(dy * n, axis=0, keepdims=True)
    sums[1:2, :] = jnp.sum(dy, axis=0, keepdims=True)
    sums[2:3, :] = jnp.sum(lowered.astype(F32), axis=0, keepdims=True)


def attend_back_body(d0, d1, d2, d3, w_out, q, kv, mate, att, lse, gq, keep, send, dat, pa, pb, sa, sb):
    k, h, f = place()
    wk = w_out[rows_at(192 * k, 192, 16), :]
    for m, d in enumerate((d0, d1, d2, d3)):
        dat[128 * m : 128 * m + 128, :] = mm_nt(d[...], wk).astype(BF)
    for i in range(3):
        for t in range(4):
            rows = slice(128 * t, 128 * t + 128)
            qt = q[i, rows, :]
            do = dat[rows, 64 * i : 64 * i + 64]
            delta = jnp.sum(do.astype(F32) * att[i, rows, :], axis=1, keepdims=True)
            total = lse[i, rows, :]
            gqt = None
            for keys, p_ref, s_ref in ((kv, pa, sa), (mate, pb, sb)):
                p = jnp.exp(mm_nt(qt, keys[i]) * 0.125 - total)
                p_ref[rows, :] = p.astype(BF)
                dp = mm_nt(do, keys[3 + i])
                ds = (p * (dp - delta) * 0.125).astype(BF)
                s_ref[rows, :] = ds
                part = mm(ds, keys[i])
                gqt = part if gqt is None else gqt + part
            gq[i, rows, :] = gqt.astype(BF)
        qi = q[i]
        doi = dat[:, 64 * i : 64 * i + 64]
        keep[i] = mm_tn(sa[...], qi)
        keep[3 + i] = mm_tn(pa[...], doi)
        send[i] = mm_tn(sb[...], qi).astype(BF)
        send[3 + i] = mm_tn(pb[...], doi).astype(BF)


def out_grad_body(packed, d0, d1, d2, d3, keep, send, full, att, ds):
    k, h, f = place()
    for m, d in enumerate((d0, d1, d2, d3)):
        ds[128 * m : 128 * m + 128, :] = d[...]
    att[0:256, :] = packed[:, 0:192]
    att[256:512, :] = packed[:, 192:384]
    full[...] = mm_tn(att[...], ds[...])
    keep[...] = full[rows_at(96 * h, 96, 8), :]
    send[...] = full[rows_at(96 * (1 - h), 96, 8), :].astype(BF)


def inner_grad_body(gq, gk, got, x0, x1, x2, x3, w, sums_a, sums_b, own, s1, s2, s3, keep, send, g, full, cols, xs):
    k, h, f = place()
    for i in range(3):
        g[:, 64 * i : 64 * i + 64] = gq[i]
        g[:, 192 + 64 * i : 256 + 64 * i] = (gk[i] + got[i].astype(F32)).astype(BF)
        g[:, 384 + 64 * i : 448 + 64 * i] = (gk[3 + i] + got[3 + i].astype(F32)).astype(BF)
    for m, x, out in ((1, x1, s1), (2, x2, s2), (3, x3, s3), (0, x0, own)):
        rows = slice(128 * m, 128 * m + 128)
        xs[rows, :] = x[...]
        out[...] = mm_nt(g[rows, :], w[:, 0:576]).astype(out.dtype)
    cols[...] = jnp.zeros_like(cols)
    bias = jnp.sum(g[...].astype(F32), axis=0, keepdims=True)
    for kk in range(4):

        @pl.when(k == kk)
        def _():
            cols[64:65, 192 * kk : 192 * kk + 192] = bias[:, 0:192]
            cols[65:66, 192 * kk : 192 * kk + 192] = bias[:, 384:576]

    cols[66:69, :] = sums_b[0:3, :]
    cols[69:72, :] = sums_a[0:3, :]
    full[:, 0:576] = mm_tn(xs[...], g[...])
    lane = lax.broadcasted_iota(jnp.int32, (768, 128), 1)
    full[:, 512:640] = jnp.where(lane < 64, full[:, 512:640], jnp.transpose(cols[...]))
    for kk in range(4):
        at = slice(96 * kk, 96 * kk + 96)
        keep[at, :] = full[rows_at(192 * kk + 96 * h, 96, 8), :]
        send[at, :] = full[rows_at(192 * kk + 96 * (1 - h), 96, 8), :].astype(BF)


def stage_z_body(keep, got, keep_o, got_o, own, s1, s2, s3, tmp, tmp_o, rows_up, one):
    k, h, f = place()
    tmp[...] = keep[...] + got[...].astype(F32)
    tmp_o[...] = keep_o[...] + got_o[...].astype(F32)
    for g in range(4):
        rows_up[g] = jnp.zeros((8, 768), F32)
        rows_up[g, 0:1, 0:96] = tmp[768:769, 96 * g : 96 * g + 96]
    for s, out in enumerate((own, s1, s2, s3)):
        g = lax.rem(f + s, 4)
        one[0:96, :] = tmp[rows_at(96 * g, 96, 8), :]
        for kk in range(4):
            one[96 + 24 * kk : 120 + 24 * kk, :] = tmp[rows_at(384 + 96 * kk + 24 * g, 24, 8), :]
        one[192:216, :] = tmp_o[rows_at(24 * g, 24, 8), :]
        one[216:224, :] = rows_up[g]
        out[...] = one[...].astype(out.dtype)


def finish_z_body(own, r1, r2, r3, w_down, w_out, up, bias_up):
    v = own[...] + r1[...].astype(F32) + r2[...].astype(F32) + r3[...].astype(F32)
    w_down[...] = v[0:96, :]
    w_out[...] = v[192:216, :]
    for kk in range(4):
        up[kk] = v[96 + 24 * kk : 120 + 24 * kk, :]
    bias_up[...] = v[216:217, 0:96]


def stage_q_body(keep, got, own, s1, s2, s3, tmp):
    k, h, f = place()
    tmp[...] = keep[...] + got[...].astype(F32)
    for s, out in enumerate((own, s1, s2, s3)):
        g = lax.rem(f + s, 4)
        v = [tmp[rows_at(96 * kk + 24 * g, 24, 8), :] for kk in range(4)]
        out[...] = jnp.concatenate(v, axis=0).astype(out.dtype)


def turn_body(own, r1, r2, r3, up, a0, a1, a2, a3, tmp):
    k, h, f = place()
    v = own[...] + r1[...].astype(F32) + r2[...].astype(F32) + r3[...].astype(F32)
    for kk in range(4):
        tmp[kk] = v[24 * kk : 24 * kk + 24, :]
    for j, out in enumerate((a0, a1, a2, a3)):
        kk = k ^ j
        out[:, 0:768] = up[kk].astype(out.dtype)
        out[:, 768:1408] = tmp[kk].astype(out.dtype)


def finish_body(own, r1, r2, r3, w_qk, w_v, w_up, vecs, tmp):
    k, h, f = place()
    total = None
    for j, r in enumerate((own, r1, r2, r3)):
        v = r[...].astype(F32)
        tmp[k ^ j] = v
        part = v[:, 1280:1408]
        total = part if total is None else total + part
    for kk in range(4):
        v = tmp[kk]
        w_up[:, 768 * kk : 768 * kk + 768] = v[:, 0:768]
        w_qk[:, 192 * kk : 192 * kk + 192] = v[:, 768:960]
        w_qk[:, 768 + 192 * kk : 960 + 192 * kk] = v[:, 960:1152]
        w_v[:, 192 * kk : 192 * kk + 192] = v[:, 1152:1344]
    turned = jnp.transpose(jnp.concatenate([total, jnp.zeros((104, 128), F32)], axis=0))
    vecs[...] = turned[64:72, 0:24]


def swap(x):
    return lax.ppermute(x, "ctx", [(i, i ^ 1) for i in range(8)])


def plane(xs):
    return [lax.ppermute(x, "ctx", [(i, i ^ (2 * j)) for i in range(8)]) for j, x in enumerate(xs, 1)]


def along_z(xs):
    return [lax.ppermute(x, "fsdp", [(i, (i + s) % 4) for i in range(4)]) for s, x in enumerate(xs, 1)]


def per_device_blocks(
    inputs, w_query_key, w_value, w_out, w_up, w_down, bias_query, bias_value, bias_out,
    gain_attn, shift_attn, bias_up, bias_down, gain_ffn, shift_ffn, cotangent,
):
    c = lax.axis_index("ctx")
    k, h = c // 2, c % 2
    x0 = inputs.reshape(128, 768)
    cot = cotangent.reshape(128, 768)
    block = ((128, 768), BF)
    vectors = [bias_query, bias_value, bias_out, gain_attn, shift_attn, bias_down, gain_ffn, shift_ffn, bias_up]

    own, other = local_call(
        pack_qkv, [((112, 640), BF)] * 2, [w_query_key, w_value] + [v.reshape(1, -1) for v in vectors], "pack_qkv",
        [pltpu.VMEM((16, 640), F32)],
    )
    xs = [x0] + plane([x0] * 3)
    pz = along_z([own] * 3)
    pm = [swap(p) for p in pz]
    q, kv, w_qkv, vecs, up = local_call(
        qkv_body,
        [((3, 512, 64), BF), ((6, 512, 64), BF), ((768, 640), BF), ((8, 768), F32), ((1, 768), F32)],
        xs + [own, other] + pz + pm, "qkv", [pltpu.VMEM((4, 16, 640), F32)], flops=2 * 512 * 768 * 576,
    )
    mate = swap(kv)

    part = jnp.concatenate(
        [
            lax.dynamic_slice(w_up, (96 * h, 768 * k), (96, 768)),
            lax.dynamic_slice(w_down, (96 * c, 0), (96, 768)),
            lax.dynamic_slice(w_out, (24 * c, 0), (24, 768)),
        ],
        axis=0,
    )
    parts = [part] + along_z([part] * 3)
    u, d0, d1, d2, d3 = local_call(
        spread_body, [((4, 96, 768), BF)] + [((192, 768), BF)] * 4, parts, "spread", [pltpu.VMEM((4, 120, 768), F32)]
    )
    ds = [d0] + plane([d1, d2, d3])
    full_up, full_down, full_out = local_call(
        settle_body, [((768, 768), BF)] * 3, [u] + ds + [swap(u)] + [swap(d) for d in ds], "settle",
        [pltpu.VMEM((768, 768), F32)],
    )

    packed, att, lse = local_call(
        attend_body, [((256, 384), BF), ((3, 512, 64), F32), ((3, 512, 1), F32)], [q, kv, mate], "attend",
        flops=4 * 512 * 1024 * 192,
    )
    atts = [packed] + plane([packed] * 3)
    low, first, hat, inv = local_call(
        branch_body, [((512, 768), BF), ((128, 768), F32), ((128, 768), F32), ((128, 1), F32)],
        atts + xs + [full_out, vecs], "branch", flops=2 * 512 * 768 * 768,
    )
    sec, s1, s2, s3, act, slope = local_call(
        feed_body, [((128, 768), F32), block, block, block, ((512, 768), BF), ((512, 768), BF)],
        [low, full_up, full_down, up], "feed", flops=4 * 512 * 768 * 768,
    )
    rs = plane([s1, s2, s3])
    out, grad_two, dsec, sums_two = local_call(
        second_body, [block, ((128, 768), F32), block, ((8, 768), F32)], [sec] + rs + [first, vecs, cot], "second"
    )
    dsecs = [dsec] + plane([dsec] * 3)
    gfo, s1, s2, s3, dhid = local_call(
        feed_back_body, [((128, 768), F32), block, block, block, ((512, 768), BF)],
        dsecs + [full_up, full_down, slope], "feed_back", flops=4 * 512 * 768 * 768,
    )
    rs = plane([s1, s2, s3])
    keep, send = local_call(
        feed_grad_body, [((784, 768), F32), ((784, 768), BF)], [act, low] + dsecs + [dhid], "feed_grad",
        [pltpu.VMEM((768, 768), F32), pltpu.VMEM((512, 768), BF)], flops=4 * 512 * 768 * 768,
    )
    got = swap(send)
    grad_one, dbr, sums_one = local_call(
        first_back_body, [((128, 768), F32), block, ((8, 768), F32)], [gfo] + rs + [grad_two, hat, inv, vecs], "first_back"
    )
    dbrs = [dbr] + plane([dbr] * 3)
    gq, gkeep, gsend = local_call(
        attend_back_body, [((3, 512, 64), BF), ((6, 512, 64), F32), ((6, 512, 64), BF)],
        dbrs + [full_out, q, kv, mate, att, lse], "attend_back",
        [pltpu.VMEM((512, 192), BF)] + [pltpu.VMEM((512, 512), BF)] * 4, flops=10 * 512 * 1024 * 192,
    )
    ggot = swap(gsend)
    okeep, osend = local_call(
        out_grad_body, [((96, 768), F32), ((96, 768), BF)], [packed] + dbrs, "out_grad",
        [pltpu.VMEM((192, 768), F32), pltpu.VMEM((512, 192), BF), pltpu.VMEM((512, 768), BF)],
        flops=2 * 512 * 192 * 768,
    )
    ogot = swap(osend)
    zown, z1, z2, z3 = local_call(
        stage_z_body, [((224, 768), F32)] + [((224, 768), BF)] * 3, [keep, got, okeep, ogot], "stage_z",
        [pltpu.VMEM((784, 768), F32), pltpu.VMEM((96, 768), F32), pltpu.VMEM((4, 8, 768), F32), pltpu.VMEM((224, 768), F32)],
    )
    zs = along_z([z1, z2, z3])
    g_down, g_out, gup, g_bias_up = local_call(
        finish_z_body, [((96, 768), F32), ((24, 768), F32), ((4, 24, 768), F32), ((1, 96), F32)], [zown] + zs, "finish_z"
    )
    gin, s1, s2, s3, qkeep, qsend = local_call(
        inner_grad_body, [((128, 768), F32), block, block, block, ((384, 640), F32), ((384, 640), BF)],
        [gq, gkeep, ggot] + xs + [w_qkv, sums_two, sums_one], "inner_grad",
        [pltpu.VMEM((512, 576), BF), pltpu.VMEM((768, 640), F32), pltpu.VMEM((128, 768), F32), pltpu.VMEM((512, 768), BF)],
        flops=4 * 512 * 768 * 576,
    )
    rs = plane([s1, s2, s3])
    qgot = swap(qsend)
    qown, q1, q2, q3 = local_call(
        stage_q_body, [((96, 640), F32)] + [((96, 640), BF)] * 3, [qkeep, qgot], "stage_q", [pltpu.VMEM((384, 640), F32)]
    )
    qs = along_z([q1, q2, q3])
    a0, a1, a2, a3 = local_call(
        turn_body, [((24, 1408), F32)] + [((24, 1408), BF)] * 3, [qown] + qs + [gup], "turn", [pltpu.VMEM((4, 24, 640), F32)]
    )
    aa = plane([a1, a2, a3])
    g_qk, g_v, g_up, small = local_call(
        finish_body, [((24, 1536), F32), ((24, 768), F32), ((24, 3072), F32), ((8, 24), F32)], [a0] + aa, "finish",
        [pltpu.VMEM((4, 24, 1408), F32)],
    )
    grad_inputs = grad_one + gin + rs[0].astype(F32) + rs[1].astype(F32) + rs[2].astype(F32)
    return (
        out.reshape(1, 128, 768), grad_inputs.reshape(1, 128, 768), g_qk, g_v, g_out, g_up, g_down,
        small[0], small[1], small[4], small[2], small[3], g_bias_up.reshape(96), small[7], small[5], small[6],
    )


def solution(mesh):
    blocks = mesh.shape["ctx"] == 8 and mesh.shape["fsdp"] == 4
    return jax.shard_map(
        per_device_blocks if blocks else per_device,
        mesh=mesh,
        in_specs=(
            P("fsdp", "ctx", None),
            P("fsdp", None),
            P("fsdp", None),
            P("fsdp", None),
            P("fsdp", None),
            P("fsdp", None),
            P("fsdp"),
            P("fsdp"),
            P("fsdp"),
            P("fsdp"),
            P("fsdp"),
            P("fsdp"),
            P("fsdp"),
            P("fsdp"),
            P("fsdp"),
            P("fsdp", "ctx", None),
        ),
        out_specs=(
            P("fsdp", "ctx", None),
            P("fsdp", "ctx", None),
            P(("ctx", "fsdp"), None),
            P(("ctx", "fsdp"), None),
            P(("ctx", "fsdp"), None),
            P(("ctx", "fsdp"), None),
            P(("ctx", "fsdp"), None),
            P(("ctx", "fsdp")),
            P(("ctx", "fsdp")),
            P(("ctx", "fsdp")),
            P(("ctx", "fsdp")),
            P(("ctx", "fsdp")),
            P(("ctx", "fsdp")),
            P(("ctx", "fsdp")),
            P(("ctx", "fsdp")),
            P(("ctx", "fsdp")),
        ),
        check_vma=False,
    )
```

```python
import functools
import math

import jax
import jax.numpy as jnp
from jax import lax
from jax.experimental import pallas as pl
from jax.experimental.pallas import tpu as pltpu
from jax.sharding import PartitionSpec as P

HEADS = 12
HEAD = 64


def norm_apply(inputs, norm_gain, norm_shift):
    centre = inputs - jnp.mean(inputs, axis=-1, keepdims=True)
    spread = jnp.mean(centre * centre, axis=-1, keepdims=True)
    return centre * lax.rsqrt(spread + 1e-05) * norm_gain + norm_shift


def left_product(left, right):
    return lax.dot_general(
        left, right, (((0,), (0,)), ((), ())), preferred_element_type=jnp.float32
    )


def right_product(left, right):
    return lax.dot_general(
        left, right, (((1,), (1,)), ((), ())), preferred_element_type=jnp.float32
    )


def column_sums(matrix):
    return jnp.sum(matrix.astype(jnp.float32), axis=0)


def per_device(
    inputs,
    w_query_key,
    w_value,
    w_out,
    w_up,
    w_down,
    bias_query,
    bias_value,
    bias_out,
    gain_attn,
    shift_attn,
    bias_up,
    bias_down,
    gain_ffn,
    shift_ffn,
    cotangent,
):
    gathered = (
        lax.all_gather(w_query_key, "fsdp", axis=0, tiled=True),
        lax.all_gather(w_value, "fsdp", axis=0, tiled=True),
        lax.all_gather(w_out, "fsdp", axis=0, tiled=True),
        lax.all_gather(w_up, "fsdp", axis=0, tiled=True),
        lax.all_gather(w_down, "fsdp", axis=0, tiled=True),
        lax.all_gather(bias_query, "fsdp", axis=0, tiled=True),
        lax.all_gather(bias_value, "fsdp", axis=0, tiled=True),
        lax.all_gather(bias_out, "fsdp", axis=0, tiled=True),
        lax.all_gather(gain_attn, "fsdp", axis=0, tiled=True),
        lax.all_gather(shift_attn, "fsdp", axis=0, tiled=True),
        lax.all_gather(bias_up, "fsdp", axis=0, tiled=True),
        lax.all_gather(bias_down, "fsdp", axis=0, tiled=True),
        lax.all_gather(gain_ffn, "fsdp", axis=0, tiled=True),
        lax.all_gather(shift_ffn, "fsdp", axis=0, tiled=True),
    )
    full_qk, full_value, full_out, full_up, full_down = (
        gathered[0],
        gathered[1],
        gathered[2],
        gathered[3],
        gathered[4],
    )
    smalls = [piece.astype(jnp.float32) for piece in gathered[5:]]
    (
        vec_query,
        vec_value,
        vec_out,
        vec_gain_one,
        vec_shift_one,
        vec_up,
        vec_down,
        vec_gain_two,
        vec_shift_two,
    ) = smalls
    rows = inputs.shape[1]
    width = inputs.shape[2]
    heads = HEADS
    head = HEAD
    tokens = inputs.reshape(rows, width)
    tok_float = tokens.astype(jnp.float32)
    query_key = jnp.dot(tokens, full_qk, preferred_element_type=jnp.float32)
    queries = (query_key[:, :width] + vec_query).astype(jnp.bfloat16)
    keys = query_key[:, width:].astype(jnp.bfloat16)
    values = (jnp.dot(tokens, full_value, preferred_element_type=jnp.float32) + vec_value).astype(
        jnp.bfloat16
    )
    query_heads = queries.reshape(rows, heads, head)
    start_state = (
        jnp.full((heads, rows), -1e30, jnp.float32),
        jnp.zeros((heads, rows), jnp.float32),
        jnp.zeros((rows, heads, head), jnp.float32),
    )
    carry = start_state
    key_piece = lax.all_gather(keys, "ctx", axis=0, tiled=True)
    value_piece = lax.all_gather(values, "ctx", axis=0, tiled=True)
    count = key_piece.shape[0]
    block = math.gcd(count, 2048)
    key_split = key_piece.reshape(count // block, block, heads, head)
    value_split = value_piece.reshape(count // block, block, heads, head)

    def step_block(state, pair):
        running_max, running_sum, running_acc = state
        key_block, value_block = pair
        scores = (
            jnp.einsum("qhd,khd->hqk", query_heads, key_block, preferred_element_type=jnp.float32)
            * 0.125
        )
        new_max = jnp.maximum(running_max, jnp.max(scores, axis=-1))
        factor = jnp.exp(running_max - new_max)
        weights = jnp.exp(scores - new_max[:, :, None])
        running_sum = running_sum * factor + jnp.sum(weights, axis=-1)
        update = jnp.einsum(
            "hqk,khd->qhd",
            weights.astype(jnp.bfloat16),
            value_block,
            preferred_element_type=jnp.float32,
        )
        running_acc = running_acc * jnp.transpose(factor)[:, :, None] + update
        return ((new_max, running_sum, running_acc), None)

    carry, unused = lax.scan(step_block, carry, (key_split, value_split))
    final_max, final_sum, final_acc = carry
    attended_heads = final_acc / jnp.transpose(final_sum)[:, :, None]
    log_total = final_max + jnp.log(final_sum)
    attended_low = attended_heads.reshape(rows, width).astype(jnp.bfloat16)
    branch = jnp.dot(attended_low, full_out, preferred_element_type=jnp.float32) + vec_out
    first, norm_one_pull = jax.vjp(norm_apply, tok_float + branch, vec_gain_one, vec_shift_one)
    first_low = first.astype(jnp.bfloat16)
    hidden = jnp.dot(first_low, full_up, preferred_element_type=jnp.float32) + vec_up
    activ, gelu_pull = jax.vjp(functools.partial(jax.nn.gelu, approximate=False), hidden)
    activ_low = activ.astype(jnp.bfloat16)
    second = jnp.dot(activ_low, full_down, preferred_element_type=jnp.float32) + vec_down
    output, norm_two_pull = jax.vjp(norm_apply, first + second, vec_gain_two, vec_shift_two)
    grad_resid_two, grad_gain_ffn, grad_shift_ffn = norm_two_pull(
        cotangent.reshape(rows, width).astype(jnp.float32)
    )
    second_low = grad_resid_two.astype(jnp.bfloat16)
    grad_w_down = left_product(activ_low, second_low)
    grad_bias_down = column_sums(second_low)
    grad_activ = right_product(second_low, full_down)
    hidden_low = gelu_pull(grad_activ)[0].astype(jnp.bfloat16)
    grad_w_up = left_product(first_low, hidden_low)
    grad_bias_up = column_sums(hidden_low)
    grad_first = grad_resid_two + right_product(hidden_low, full_up)
    grad_resid_one, grad_gain_attn, grad_shift_attn = norm_one_pull(grad_first)
    branch_low = grad_resid_one.astype(jnp.bfloat16)
    grad_w_out = left_product(attended_low, branch_low)
    grad_bias_out = column_sums(branch_low)
    dout_low = right_product(branch_low, full_out).astype(jnp.bfloat16)
    dout_heads = dout_low.reshape(rows, heads, head)
    delta = jnp.einsum("qhd,qhd->hq", dout_heads.astype(jnp.float32), attended_heads)
    all_keys, all_values = (
        lax.all_gather(keys, "ctx", axis=0, tiled=True),
        lax.all_gather(values, "ctx", axis=0, tiled=True),
    )
    total = all_keys.shape[0]
    key_total = all_keys.shape[0]
    block = math.gcd(key_total, 2048)

    def back_block(grad_query, pair):
        key_block, value_block = pair
        scores = (
            jnp.einsum("qhd,khd->hqk", query_heads, key_block, preferred_element_type=jnp.float32)
            * 0.125
        )
        weights = jnp.exp(scores - log_total[:, :, None])
        weight_grad = jnp.einsum(
            "qhd,khd->hqk", dout_heads, value_block, preferred_element_type=jnp.float32
        )
        score_grad = (weights * (weight_grad - delta[:, :, None]) * 0.125).astype(jnp.bfloat16)
        grad_query = grad_query + jnp.einsum(
            "hqk,khd->qhd", score_grad, key_block, preferred_element_type=jnp.float32
        )
        value_grad = jnp.einsum(
            "hqk,qhd->khd",
            weights.astype(jnp.bfloat16),
            dout_heads,
            preferred_element_type=jnp.float32,
        )
        key_grad = jnp.einsum(
            "hqk,qhd->khd", score_grad, query_heads, preferred_element_type=jnp.float32
        )
        return (grad_query, (key_grad, value_grad))

    grad_query, terms = lax.scan(
        back_block,
        jnp.zeros((rows, heads, head), jnp.float32),
        (
            all_keys.reshape(key_total // block, block, heads, head),
            all_values.reshape(key_total // block, block, heads, head),
        ),
    )
    grad_keys, grad_values = (
        lax.psum_scatter(terms[0].reshape(total, width), "ctx", scatter_dimension=0, tiled=True),
        lax.psum_scatter(terms[1].reshape(total, width), "ctx", scatter_dimension=0, tiled=True),
    )
    grad_queries = grad_query.reshape(rows, width)
    query_low = grad_queries.astype(jnp.bfloat16)
    key_low = grad_keys.astype(jnp.bfloat16)
    value_low = grad_values.astype(jnp.bfloat16)
    query_key_low = jnp.concatenate([query_low, key_low], axis=1)
    grad_w_query_key = left_product(tokens, query_key_low)
    grad_w_value = left_product(tokens, value_low)
    grad_bias_query = column_sums(query_low)
    grad_bias_value = column_sums(value_low)
    grad_inputs = (
        grad_resid_one
        + right_product(query_key_low, full_qk)
        + right_product(value_low, full_value)
    )
    summed = (
        lax.psum_scatter(grad_w_query_key, ("ctx", "fsdp"), scatter_dimension=0, tiled=True),
        lax.psum_scatter(grad_w_value, ("ctx", "fsdp"), scatter_dimension=0, tiled=True),
        lax.psum_scatter(grad_w_out, ("ctx", "fsdp"), scatter_dimension=0, tiled=True),
        lax.psum_scatter(grad_w_up, ("ctx", "fsdp"), scatter_dimension=0, tiled=True),
        lax.psum_scatter(grad_w_down, ("ctx", "fsdp"), scatter_dimension=0, tiled=True),
        lax.psum_scatter(grad_bias_query, ("ctx", "fsdp"), scatter_dimension=0, tiled=True),
        lax.psum_scatter(grad_bias_value, ("ctx", "fsdp"), scatter_dimension=0, tiled=True),
        lax.psum_scatter(grad_bias_out, ("ctx", "fsdp"), scatter_dimension=0, tiled=True),
        lax.psum_scatter(grad_gain_attn, ("ctx", "fsdp"), scatter_dimension=0, tiled=True),
        lax.psum_scatter(grad_shift_attn, ("ctx", "fsdp"), scatter_dimension=0, tiled=True),
        lax.psum_scatter(grad_bias_up, ("ctx", "fsdp"), scatter_dimension=0, tiled=True),
        lax.psum_scatter(grad_bias_down, ("ctx", "fsdp"), scatter_dimension=0, tiled=True),
        lax.psum_scatter(grad_gain_ffn, ("ctx", "fsdp"), scatter_dimension=0, tiled=True),
        lax.psum_scatter(grad_shift_ffn, ("ctx", "fsdp"), scatter_dimension=0, tiled=True),
    )
    return (
        output.astype(jnp.bfloat16).reshape(1, rows, width),
        grad_inputs.reshape(1, rows, width),
        summed[0],
        summed[1],
        summed[2],
        summed[3],
        summed[4],
        summed[5],
        summed[6],
        summed[7],
        summed[8],
        summed[9],
        summed[10],
        summed[11],
        summed[12],
        summed[13],
    )


BF = jnp.bfloat16
F32 = jnp.float32


def local_call(body, outs, args, name, scratch=(), flops=0, mib=16, final=(), raw=0):
    vmem, hbm = pl.BlockSpec(memory_space=pltpu.VMEM), pl.BlockSpec(memory_space=pltpu.HBM)
    held = [pltpu.with_memory_space_constraint(a, pltpu.HBM if i < raw else pltpu.VMEM) for i, a in enumerate(args)]
    return pl.pallas_call(
        body,
        out_shape=tuple(jax.ShapeDtypeStruct(s, d) if i in final else pltpu.VMEM(s, d) for i, (s, d) in enumerate(outs)),
        in_specs=[hbm] * raw + [vmem] * (len(args) - raw),
        out_specs=tuple(vmem for _ in outs),
        scratch_shapes=list(scratch),
        compiler_params=pltpu.CompilerParams(vmem_limit_bytes=mib * 1024 * 1024),
        cost_estimate=pl.CostEstimate(flops=0, bytes_accessed=0, transcendentals=0),
        name=name,
    )(*held)


def fetch(sems, *pairs):
    copies = [pltpu.make_async_copy(src, dst, sems.at[i]) for i, (src, dst) in enumerate(pairs)]
    for copy in copies:
        copy.start()
    for copy in copies:
        copy.wait()


def place():
    c = lax.axis_index("ctx")
    return c // 2, c % 2, lax.axis_index("fsdp")


def chip(k, h, j):
    return k ^ (j if j in (0, 3) else 1 + h if j == 1 else 2 - h)


def mm(a, b):
    return jnp.dot(a, b, preferred_element_type=F32)


def mm_nt(a, b):
    return lax.dot_general(a, b, (((1,), (1,)), ((), ())), preferred_element_type=F32)


def mm_tn(a, b):
    return lax.dot_general(a, b, (((0,), (0,)), ((), ())), preferred_element_type=F32)


def rows_at(start, size, step):
    return pl.ds(pl.multiple_of(start, step), size)


def pack_qkv(w_qk_hbm, w_v_hbm, w_out_hbm, *rest):
    raw, (own, other, w_qk, w_v, w_out), vecs, (tmp, wide, sems) = rest[:9], rest[9:14], rest[14:23], rest[23:]
    k, h, f = place()
    fetch(sems, (w_qk_hbm, w_qk), (w_v_hbm, w_v), (w_out_hbm, w_out), *zip(raw, vecs))
    tmp[...] = jnp.zeros_like(tmp)
    for i in range(8):
        at = slice(192 * (i % 4), 192 * (i % 4) + 192)
        tmp[96 + i // 4 : 97 + i // 4, at] = vecs[i][...].astype(F32).reshape(1, 192)
    tmp[98:99, :] = vecs[8][...].astype(F32).reshape(1, 768)
    wide[...] = w_out[...].astype(F32)
    for out, half in ((own, h), (other, 1 - h)):
        rows = rows_at(half * 96, 96, 16)
        for t in range(4):
            tmp[24 * t : 24 * t + 24, 576:768] = wide[rows_at(48 * k + 24 * half, 24, 8), 192 * t : 192 * t + 192]
        out[...] = tmp[...].astype(BF)
        for kk in range(4):

            @pl.when(k == kk)
            def _():
                out[0:96, 0:192] = w_qk[rows, 192 * kk : 192 * kk + 192]
                out[0:96, 192:384] = w_qk[rows, 768 + 192 * kk : 960 + 192 * kk]
                out[0:96, 384:576] = w_v[rows, 192 * kk : 192 * kk + 192]


def pack_feed(w_up_hbm, w_down_hbm, token, out, w_up, w_down, sems):
    k, h, f = place()
    c = 2 * k + h
    fetch(sems, (w_up_hbm, w_up), (w_down_hbm.at[rows_at(96 * c, 96, 16), :], w_down))
    out[192:288, :] = w_down[:, 0:384]
    out[288:384, :] = w_down[:, 384:768]
    for cc in range(8):

        @pl.when(c == cc)
        def _():
            for g in range(4):
                out[0:192, 96 * g : 96 * g + 96] = w_up[:, 768 * g + 96 * cc : 768 * g + 96 * cc + 96]


def qkv_body(x0, x1, x2, x3, own, other, p1, p2, p3, m1, m2, m3, q, kv, w, vecs, up, tmp, vec, row):
    k, h, f = place()
    for s, (mine, mate) in enumerate(((own, other), (p1, m1), (p2, m2), (p3, m3))):
        g = f ^ s
        w[rows_at(192 * g + 96 * h, 96, 16), :] = mine[0:96, 0:576]
        w[rows_at(192 * g + 96 * (1 - h), 96, 16), :] = mate[0:96, 0:576]
        tmp[g] = mine[96:112, :].astype(F32)
    for g in range(4):
        for i in range(8):
            at = 192 * (i % 4)
            vecs[i : i + 1, 192 * g : 192 * g + 192] = tmp[g, i // 4 : i // 4 + 1, at : at + 192]
    for kk in range(4):

        @pl.when(k == kk)
        def _():
            for half in range(2):
                for g in range(4):
                    at = 192 * kk + 96 * half
                    row[0:1, 384 * half + 96 * g : 384 * half + 96 * g + 96] = tmp[g, 2:3, at : at + 96]

    up[...] = row[0:1, :]
    for i in range(2):
        vec[i : i + 1, :] = tmp[k, 0:1, 192 * i : 192 * i + 192]
    for j, x in enumerate((x0, x1, x2, x3)):
        r = mm(x[...], w[...])
        rows = slice(128 * j, 128 * j + 128)
        q[rows, :] = (r[:, 0:192] + vec[0:1, :]).astype(BF)
        kv[rows, 0:192] = r[:, 192:384].astype(BF)
        kv[rows, 192:384] = (r[:, 384:576] + vec[1:2, :]).astype(BF)


def gather_out_body(p0, p1, p2, p3, d):
    for s, p in enumerate((p0, p1, p2, p3)):
        d[:, 192 * s : 192 * s + 192] = p[0:96, 576:768]


def settle_out_body(d0, d1, d2, d3, e1, e2, e3, m0, m1, m2, m3, w_out, tmp):
    k, h, f = place()
    for half, parts in ((h, (d0, d1, d2, d3)), (1 - h, (None, e1, e2, e3))):
        for j, d in enumerate(parts):
            for s in range(4):
                rows = rows_at(192 * (f ^ s) + 48 * chip(k, half, j) + 24 * half, 24, 8)
                if d is None:
                    piece = (m0, m1, m2, m3)[s][0:96, 576:768].astype(F32)
                else:
                    piece = d[:, 192 * s : 192 * s + 192].astype(F32)
                for t in range(4):
                    tmp[rows, 192 * t : 192 * t + 192] = piece[24 * t : 24 * t + 24, :]
    w_out[...] = tmp[...].astype(BF)


def settle_feed_body(p0, p1, p2, p3, e0, e1, e2, e3, w_up, w_down):
    k, h, f = place()
    for half, parts in ((h, (p0, p1, p2, p3)), (1 - h, (e0, e1, e2, e3))):
        lanes = pl.ds(pl.multiple_of(384 * half, 128), 384)
        for s, part in enumerate(parts):
            g = f ^ s
            w_up[rows_at(192 * g, 192, 16), lanes] = part[0:192, :]
            rows = rows_at(384 * half + 96 * g, 96, 16)
            w_down[rows, 0:384] = part[192:288, :]
            w_down[rows, 384:768] = part[288:384, :]


def attend_body(q, kv, mate, packed, att, lse):
    for i in range(3):
        for t in range(4):
            rows = slice(128 * t, 128 * t + 128)
            qt = q[rows, 64 * i : 64 * i + 64]
            sa = mm_nt(qt, kv[:, 64 * i : 64 * i + 64]) * 0.125
            sb = mm_nt(qt, mate[:, 64 * i : 64 * i + 64]) * 0.125
            top = jnp.maximum(jnp.max(sa, axis=1, keepdims=True), jnp.max(sb, axis=1, keepdims=True))
            ea = jnp.exp(sa - top)
            eb = jnp.exp(sb - top)
            total = jnp.sum(ea, axis=1, keepdims=True) + jnp.sum(eb, axis=1, keepdims=True)
            acc = mm(ea.astype(BF), kv[:, 192 + 64 * i : 256 + 64 * i]) + mm(eb.astype(BF), mate[:, 192 + 64 * i : 256 + 64 * i])
            out = acc / total
            att[i, rows, :] = out
            lse[i, rows, :] = top + jnp.log(total)
            col = 192 * (t // 2) + 64 * i
            packed[128 * (t % 2) : 128 * (t % 2) + 128, col : col + 64] = out.astype(BF)


def norm_parts(v):
    centre = v - jnp.mean(v, axis=1, keepdims=True)
    inv = lax.rsqrt(jnp.mean(centre * centre, axis=1, keepdims=True) + 1e-05)
    return centre * inv, inv


def branch_body(a0, a1, a2, a3, x0, x1, x2, x3, w_out, vecs, low, first, hat, inv):
    k, h, f = place()
    parts = (a0, a1, a2, a3)
    for m, x in enumerate((x0, x1, x2, x3)):
        acc = x[...].astype(F32) + vecs[2:3, :]
        for j in range(4):
            b = j ^ m
            a = parts[j][128 * (b % 2) : 128 * (b % 2) + 128, 192 * (b // 2) : 192 * (b // 2) + 192]
            acc = acc + mm(a, w_out[rows_at(192 * chip(k, h, j), 192, 16), :])
        n, r = norm_parts(acc)
        y = n * vecs[3:4, :] + vecs[4:5, :]
        low[128 * m : 128 * m + 128, :] = y.astype(BF)
        if m == 0:
            first[...] = y
            hat[...] = n
            inv[...] = r


def feed_body(low, w_up, w_down, up, own, s1, s2, s3, act, slope):
    for m, out in ((1, s1), (2, s2), (3, s3), (0, own)):
        rows = slice(128 * m, 128 * m + 128)
        hid = mm(low[rows, :], w_up[...]) + up[...]
        cdf = 0.5 * (1.0 + lax.erf(hid * (2.0**-0.5)))
        pdf = jnp.exp(hid * hid * -0.5) * ((2.0 * math.pi) ** -0.5)
        a = (hid * cdf).astype(BF)
        act[rows, :] = a
        slope[rows, :] = (cdf + hid * pdf).astype(BF)
        out[...] = mm(a, w_down[...]).astype(out.dtype)


def second_body(own, r1, r2, r3, first, vecs, cot, out, grad, low, sums):
    v = own[...] + r1[...].astype(F32) + r2[...].astype(F32) + r3[...].astype(F32)
    n, inv = norm_parts(v + first[...] + vecs[5:6, :])
    out[...] = (n * vecs[6:7, :] + vecs[7:8, :]).astype(BF)
    dy = cot[...].astype(F32)
    g, lowered = norm_back(dy, n, inv, vecs[6:7, :])
    grad[...] = g
    low[...] = lowered
    sums[...] = jnp.zeros_like(sums)
    sums[0:1, :] = jnp.sum(dy * n, axis=0, keepdims=True)
    sums[1:2, :] = jnp.sum(dy, axis=0, keepdims=True)
    sums[2:3, :] = jnp.sum(lowered.astype(F32), axis=0, keepdims=True)


def norm_back(dy, n, inv, gain):
    d = dy * gain
    g = inv * (d - jnp.mean(d, axis=1, keepdims=True) - n * jnp.mean(d * n, axis=1, keepdims=True))
    return g, g.astype(BF)


def feed_back_body(d0, d1, d2, d3, w_up, w_down, slope, own, s1, s2, s3, dhid):
    for m, d, out in ((1, d1, s1), (2, d2, s2), (3, d3, s3), (0, d0, own)):
        rows = slice(128 * m, 128 * m + 128)
        da = mm_nt(d[...], w_down[...])
        dh = (da * slope[rows, :].astype(F32)).astype(BF)
        dhid[rows, :] = dh
        out[...] = mm_nt(dh, w_up[...]).astype(out.dtype)


def down_grad_body(act, d0, d1, d2, d3, keep, send, full, ds):
    k, h, f = place()
    for m, d in enumerate((d0, d1, d2, d3)):
        ds[128 * m : 128 * m + 128, :] = d[...]
    full[...] = mm_tn(act[...], ds[...])
    keep[...] = full[rows_at(384 * h, 384, 8), :]
    send[...] = full[rows_at(384 * (1 - h), 384, 8), :].astype(BF)


def up_grad_body(low, dhid, keep, send, full):
    k, h, f = place()
    full[...] = mm_tn(low[...], dhid[...])
    for kk in range(4):
        at = slice(96 * kk, 96 * kk + 96)
        keep[at, :] = full[rows_at(192 * kk + 96 * h, 96, 8), :]
        send[at, :] = full[rows_at(192 * kk + 96 * (1 - h), 96, 8), :].astype(BF)
    total = jnp.sum(dhid[...].astype(F32), axis=0, keepdims=True)
    lo, hi = total[:, 0:384], total[:, 384:768]
    keep[384:400, :] = jnp.zeros((16, 768), F32)
    keep[384:385, 0:384] = jnp.where(h == 0, lo, hi)
    full[0:16, :] = jnp.zeros((16, 768), F32)
    full[0:1, 0:384] = jnp.where(h == 0, hi, lo)
    send[384:400, :] = full[0:16, :].astype(BF)


def first_back_body(own, r1, r2, r3, grad, hat, inv, vecs, out, low, sums):
    dy = own[...] + r1[...].astype(F32) + r2[...].astype(F32) + r3[...].astype(F32) + grad[...]
    n = hat[...]
    g, lowered = norm_back(dy, n, inv[...], vecs[3:4, :])
    out[...] = g
    low[...] = lowered
    sums[...] = jnp.zeros_like(sums)
    sums[0:1, :] = jnp.sum(dy * n, axis=0, keepdims=True)
    sums[1:2, :] = jnp.sum(dy, axis=0, keepdims=True)
    sums[2:3, :] = jnp.sum(lowered.astype(F32), axis=0, keepdims=True)


def attend_back_body(d0, d1, d2, d3, w_out, q, kv, mate, att, lse, gq, keep, send, dat, pa, pb, sa, sb):
    k, h, f = place()
    wk = w_out[rows_at(192 * k, 192, 16), :]
    for m, d in enumerate((d0, d1, d2, d3)):
        dat[128 * m : 128 * m + 128, :] = mm_nt(d[...], wk).astype(BF)
    for i in range(3):
        lanes, vlanes = slice(64 * i, 64 * i + 64), slice(192 + 64 * i, 256 + 64 * i)
        for t in range(4):
            rows = slice(128 * t, 128 * t + 128)
            qt = q[rows, lanes]
            do = dat[rows, lanes]
            delta = jnp.sum(do.astype(F32) * att[i, rows, :], axis=1, keepdims=True)
            total = lse[i, rows, :]
            gqt = None
            for keys, p_ref, s_ref in ((kv, pa, sa), (mate, pb, sb)):
                p = jnp.exp(mm_nt(qt, keys[:, lanes]) * 0.125 - total)
                p_ref[rows, :] = p.astype(BF)
                dp = mm_nt(do, keys[:, vlanes])
                ds = (p * (dp - delta) * 0.125).astype(BF)
                s_ref[rows, :] = ds
                part = mm(ds, keys[:, lanes])
                gqt = part if gqt is None else gqt + part
            gq[rows, lanes] = gqt.astype(BF)
        qi = q[:, lanes]
        doi = dat[:, lanes]
        keep[:, lanes] = mm_tn(sa[...], qi)
        keep[:, vlanes] = mm_tn(pa[...], doi)
        send[:, lanes] = mm_tn(sb[...], qi).astype(BF)
        send[:, vlanes] = mm_tn(pb[...], doi).astype(BF)


def out_grad_body(packed, d0, d1, d2, d3, keep, send, full, att, ds):
    k, h, f = place()
    for m, d in enumerate((d0, d1, d2, d3)):
        ds[128 * m : 128 * m + 128, :] = d[...]
    att[0:256, :] = packed[:, 0:192]
    att[256:512, :] = packed[:, 192:384]
    full[...] = mm_tn(att[...], ds[...])
    keep[...] = full[rows_at(96 * h, 96, 8), :]
    send[...] = full[rows_at(96 * (1 - h), 96, 8), :].astype(BF)


def inner_weight_body(gq, gk, got, x0, x1, x2, x3, sums_a, sums_b, g, keep, send, full, cols, xs):
    k, h, f = place()
    g[:, 0:192] = gq[...]
    g[:, 192:576] = (gk[...] + got[...].astype(F32)).astype(BF)
    for m, x in enumerate((x0, x1, x2, x3)):
        xs[128 * m : 128 * m + 128, :] = x[...]
    cols[...] = jnp.zeros_like(cols)
    bias = jnp.sum(g[...].astype(F32), axis=0, keepdims=True)
    for kk in range(4):

        @pl.when(k == kk)
        def _():
            cols[64:65, 192 * kk : 192 * kk + 192] = bias[:, 0:192]
            cols[65:66, 192 * kk : 192 * kk + 192] = bias[:, 384:576]

    cols[66:69, :] = sums_b[0:3, :]
    cols[69:72, :] = sums_a[0:3, :]
    full[:, 0:576] = mm_tn(xs[...], g[...])
    lane = lax.broadcasted_iota(jnp.int32, (768, 128), 1)
    full[:, 512:640] = jnp.where(lane < 64, full[:, 512:640], jnp.transpose(cols[...]))
    for kk in range(4):
        at = slice(96 * kk, 96 * kk + 96)
        keep[at, :] = full[rows_at(192 * kk + 96 * h, 96, 8), :]
        send[at, :] = full[rows_at(192 * kk + 96 * (1 - h), 96, 8), :].astype(BF)


def inner_input_body(g, w, own, s1, s2, s3):
    for m, out in ((1, s1), (2, s2), (3, s3), (0, own)):
        out[...] = mm_nt(g[128 * m : 128 * m + 128, :], w[...]).astype(out.dtype)


def stage_down_body(keep, got, held, sent, tmp):
    k, h, f = place()
    tmp[...] = keep[...] + got[...].astype(F32)
    for s in range(4):
        out = (held, sent)[s % 2]
        out[96 * (s // 2) : 96 * (s // 2) + 96, :] = tmp[rows_at(96 * (f ^ s), 96, 8), :].astype(out.dtype)


def stage_up_body(keep, got, held, sent, tmp, one):
    k, h, f = place()
    tmp[...] = keep[...] + got[...].astype(F32)
    for g in range(4):
        one[g] = jnp.zeros((16, 768), F32)
        one[g, 0:1, 0:96] = tmp[384:385, 96 * g : 96 * g + 96]
    for s in range(4):
        out, g = (held, sent)[s % 2], f ^ s
        v = [tmp[rows_at(96 * kk + 24 * g, 24, 8), :] for kk in range(4)] + [one[g]]
        out[112 * (s // 2) : 112 * (s // 2) + 112, :] = jnp.concatenate(v, axis=0).astype(out.dtype)


def stage_q_body(keep, got, held, sent, tmp):
    k, h, f = place()
    tmp[...] = keep[...] + got[...].astype(F32)
    for s in range(4):
        out = (held, sent)[s % 2]
        v = [tmp[rows_at(96 * kk + 24 * (f ^ s), 24, 8), :] for kk in range(4)]
        out[96 * (s // 2) : 96 * (s // 2) + 96, :] = jnp.concatenate(v, axis=0).astype(out.dtype)


def stage_out_body(keep, got, held, sent, tmp):
    k, h, f = place()
    tmp[...] = keep[...] + got[...].astype(F32)
    for half, out in enumerate((held, sent)):
        v = [tmp[rows_at(24 * (f ^ s), 24, 8), :] for s in (half, half + 2)]
        out[...] = jnp.concatenate(v, axis=0).astype(out.dtype)


def half_body(held, got, own, far):
    n = own.shape[0]
    own[...] = held[0:n, :] + got[0:n, :].astype(F32)
    far[...] = (held[n : 2 * n, :] + got[n : 2 * n, :].astype(F32)).astype(BF)


def half_out_body(held, got, own, far):
    v = held[...] + got[...].astype(F32)
    own[...] = v[0:24, :]
    far[...] = v[24:48, :].astype(BF)


def join_down_body(own, r, up, u, out, up_sum):
    out[0:96, :] = (own[...] + r[...].astype(F32)).astype(BF)
    v = up[...] + u[...].astype(F32)
    up_sum[...] = v[0:96, :]
    out[96:112, :] = v[96:112, :].astype(BF)


def turn_body(own, r, up, a0, a1, a2, a3, tmp):
    k, h, f = place()
    v = own[...] + r[...].astype(F32)
    u = up[...]
    for kk in range(4):
        tmp[kk, :, 0:768] = u[24 * kk : 24 * kk + 24, :]
        tmp[kk, :, 768:1408] = v[24 * kk : 24 * kk + 24, :]
    for j, out in enumerate((a0, a1, a2, a3)):
        out[...] = tmp[chip(k, h, j)].astype(out.dtype)


def finish_body(own, r1, r2, r3, down, out, o1, w_qk, w_v, w_up, w_down, w_out, *rest):
    vecs, bias_up, tmp = rest[:8], rest[8], rest[9]
    k, h, f = place()
    total = None
    for j, r in enumerate((own, r1, r2, r3)):
        v = r[...].astype(F32)
        tmp[chip(k, h, j)] = v
        part = v[:, 1280:1408]
        total = part if total is None else total + part
    for kk in range(4):
        v = tmp[kk]
        for half in range(2):
            for g in range(4):
                at = 768 * g + 192 * kk + 96 * half
                w_up[:, at : at + 96] = v[:, 384 * half + 96 * g : 384 * half + 96 * g + 96]
        w_qk[:, 192 * kk : 192 * kk + 192] = v[:, 768:960]
        w_qk[:, 768 + 192 * kk : 960 + 192 * kk] = v[:, 960:1152]
        w_v[:, 192 * kk : 192 * kk + 192] = v[:, 1152:1344]
    turned = jnp.transpose(jnp.concatenate([total, jnp.zeros((104, 128), F32)], axis=0))
    for i in range(8):
        vecs[i][...] = turned[64 + i : 65 + i, 0:24].reshape(24)
    w_down[...] = down[0:96, :].astype(F32)
    bias_up[...] = down[96:112, :].astype(F32)[0:1, 0:96].reshape(96)
    w_out[...] = out[...] + o1[...].astype(F32)


def swap(x):
    return lax.ppermute(x, "ctx", [(i, i ^ 1) for i in range(8)])


def to_chip(x, j):
    return lax.ppermute(x, "ctx", [(i, i ^ (2 * chip(0, i % 2, j))) for i in range(8)])


def to_plane(x, s):
    return lax.ppermute(x, "fsdp", [(i, i ^ s) for i in range(4)])


def plane(xs):
    return [to_chip(x, j) for j, x in enumerate(xs, 1)]


def gather_plane(x):
    a = to_chip(x, 1)
    return [x, a, to_chip(x, 2), to_chip(a, 2)]


def gather_z(x):
    return [x, to_plane(x, 1), to_plane(x, 2)]


def sum_z(body, mid, outs, args, name, scratch):
    rows, lanes = outs
    held, sent = local_call(body, [((2 * rows, lanes), F32), ((2 * rows, lanes), BF)], args, "stage_" + name, scratch)
    own, far = local_call(mid, [((rows, lanes), F32), ((rows, lanes), BF)], [held, to_plane(sent, 1)], "half_" + name)
    return sent, far, own, to_plane(far, 2)


def after(value, *others):
    return lax.optimization_barrier((value, *others))[0]


def per_device_blocks(
    inputs, w_query_key, w_value, w_out, w_up, w_down, bias_query, bias_value, bias_out,
    gain_attn, shift_attn, bias_up, bias_down, gain_ffn, shift_ffn, cotangent,
):
    c = lax.axis_index("ctx")
    x0 = inputs.reshape(128, 768)
    cot = cotangent.reshape(128, 768)
    block, wide = ((128, 768), BF), ((128, 768), F32)
    vectors = [bias_query, bias_value, bias_out, gain_attn, shift_attn, bias_down, gain_ffn, shift_ffn, bias_up]

    own, other = local_call(
        pack_qkv, [((112, 768), BF)] * 2, [w_query_key, w_value, w_out] + vectors, "pack_qkv",
        [pltpu.VMEM((192, 1536), BF), pltpu.VMEM((192, 768), BF), pltpu.VMEM((192, 768), BF)]
        + [pltpu.VMEM((192,), BF)] * 8
        + [pltpu.VMEM((768,), BF), pltpu.VMEM((112, 768), F32), pltpu.VMEM((192, 768), F32), pltpu.SemaphoreType.DMA((12,))],
        raw=12,
    )
    pz = gather_z(own)[1:]
    pz.append(to_plane(pz[1], 1))
    xs = gather_plane(x0)
    (part,) = local_call(
        pack_feed, [((384, 384), BF)], [w_up, w_down, own], "pack_feed",
        [pltpu.VMEM((192, 3072), BF), pltpu.VMEM((96, 768), BF), pltpu.SemaphoreType.DMA((2,))],
        raw=2,
    )
    pm = [swap(after(p, part)) for p in pz]
    q, kv, w_qkv, vecs, up = local_call(
        qkv_body,
        [((512, 192), BF), ((512, 384), BF), ((768, 576), BF), ((8, 768), F32), ((1, 768), F32)],
        xs + [own, other] + pz + pm, "qkv",
        [pltpu.VMEM((4, 16, 768), F32), pltpu.VMEM((8, 192), F32), pltpu.VMEM((8, 768), F32)],
        flops=2 * 512 * 768 * 576,
    )
    mate = swap(kv)

    (piece,) = local_call(gather_out_body, [((96, 768), BF)], [after(own, q)] + pz, "gather_out")
    ds = gather_plane(piece)
    parts = gather_z(part)
    packed, att, lse = local_call(
        attend_body, [((256, 384), BF), ((3, 512, 64), F32), ((3, 512, 1), F32)], [q, kv, mate], "attend",
        flops=4 * 512 * 1024 * 192,
    )
    atts = gather_plane(packed)
    parts.append(to_plane(after(parts[2], packed), 1))
    (full_out,) = local_call(
        settle_out_body, [((768, 768), BF)], ds + [swap(after(d, packed)) for d in ds[1:]] + [other] + pm, "settle_out",
        [pltpu.VMEM((768, 768), F32)],
    )
    full_up, full_down = local_call(
        settle_feed_body, [((768, 768), BF)] * 2, parts + [swap(p) for p in parts], "settle_feed"
    )
    low, first, hat, inv = local_call(
        branch_body, [((512, 768), BF), wide, wide, ((128, 1), F32)], atts + xs + [full_out, vecs], "branch",
        flops=2 * 512 * 768 * 768,
    )
    sec, s1, s2, s3, act, slope = local_call(
        feed_body, [wide, block, block, block, ((512, 768), BF), ((512, 768), BF)],
        [low, full_up, full_down, up], "feed", flops=4 * 512 * 768 * 768,
    )
    rs = plane([s1, s2, s3])
    out, grad_two, dsec, sums_two = local_call(
        second_body, [block, wide, block, ((8, 768), F32)], [sec] + rs + [first, vecs, cot], "second", final=(0,)
    )
    dsecs = gather_plane(dsec)
    dkeep, dsend = local_call(
        down_grad_body, [((384, 768), F32), ((384, 768), BF)], [act] + dsecs, "down_grad",
        [pltpu.VMEM((768, 768), F32), pltpu.VMEM((512, 768), BF)], flops=2 * 512 * 768 * 768,
    )
    gfo, s1, s2, s3, dhid = local_call(
        feed_back_body, [wide, block, block, block, ((512, 768), BF)],
        dsecs + [full_up, full_down, slope], "feed_back", flops=4 * 512 * 768 * 768,
    )
    rs = plane([s1, s2, s3])
    ukeep, usend = local_call(
        up_grad_body, [((400, 768), F32), ((400, 768), BF)], [low, dhid], "up_grad",
        [pltpu.VMEM((768, 768), F32)], flops=2 * 512 * 768 * 768,
    )
    dsent, dfar, down, down_far = sum_z(
        stage_down_body, half_body, (96, 768), [dkeep, swap(dsend)], "down", [pltpu.VMEM((384, 768), F32)]
    )
    usent, ufar, up_own, up_far = sum_z(
        stage_up_body, half_body, (112, 768), [ukeep, swap(usend)], "up",
        [pltpu.VMEM((400, 768), F32), pltpu.VMEM((4, 16, 768), F32)],
    )
    down, up_sum = local_call(
        join_down_body, [((112, 768), BF), ((96, 768), F32)], [down, down_far, up_own, up_far], "join_down"
    )
    down = lax.ppermute(down, ("ctx", "fsdp"), [(4 * i + z, 8 * z + i) for i in range(8) for z in range(4)])
    grad_one, dbr, sums_one = local_call(
        first_back_body, [wide, block, ((8, 768), F32)], [after(gfo, dsent, ukeep)] + rs + [grad_two, hat, inv, vecs], "first_back"
    )
    dbrs = gather_plane(dbr)
    gq, gkeep, gsend = local_call(
        attend_back_body, [((512, 192), BF), ((512, 384), F32), ((512, 384), BF)],
        dbrs + [full_out, after(q, usent, dfar), kv, mate, att, lse], "attend_back",
        [pltpu.VMEM((512, 192), BF)] + [pltpu.VMEM((512, 512), BF)] * 4, flops=10 * 512 * 1024 * 192,
    )
    ggot = swap(gsend)
    g, qkeep, qsend = local_call(
        inner_weight_body, [((512, 576), BF), ((384, 640), F32), ((384, 640), BF)],
        [after(gq, ufar), gkeep, ggot] + xs + [sums_two, sums_one], "inner_weight",
        [pltpu.VMEM((768, 640), F32), pltpu.VMEM((128, 768), F32), pltpu.VMEM((512, 768), BF)], flops=2 * 512 * 768 * 576,
    )
    qsent, _, qown, qfar = sum_z(
        stage_q_body, half_body, (96, 640), [qkeep, swap(qsend)], "q", [pltpu.VMEM((384, 640), F32)]
    )
    gin, s1, s2, s3 = local_call(
        inner_input_body, [wide, block, block, block], [after(g, qsent), w_qkv], "inner_input", flops=2 * 512 * 768 * 576
    )
    rs = plane([s1, s2, s3])
    okeep, osend = local_call(
        out_grad_body, [((96, 768), F32), ((96, 768), BF)], [after(packed, qsent)] + dbrs, "out_grad",
        [pltpu.VMEM((192, 768), F32), pltpu.VMEM((512, 192), BF), pltpu.VMEM((512, 768), BF)],
        flops=2 * 512 * 192 * 768,
    )
    _, _, oown, ofar = sum_z(
        stage_out_body, half_out_body, (24, 768), [okeep, swap(osend)], "out", [pltpu.VMEM((96, 768), F32)]
    )
    a0, a1, a2, a3 = local_call(
        turn_body, [((24, 1408), F32)] + [((24, 1408), BF)] * 3, [after(qown, *rs), qfar, up_sum], "turn", [pltpu.VMEM((4, 24, 1408), F32)]
    )
    aa = plane([a1, a2, a3])
    g_qk, g_v, g_up, g_down, g_out, *small = local_call(
        finish_body,
        [((24, 1536), F32), ((24, 768), F32), ((24, 3072), F32), ((96, 768), F32), ((24, 768), F32)]
        + [((24,), F32)] * 8
        + [((96,), F32)],
        [a0] + aa + [down, oown, ofar], "finish", [pltpu.VMEM((4, 24, 1408), F32)], final=range(14),
    )
    grad_inputs = grad_one + gin + rs[0].astype(F32) + rs[1].astype(F32) + rs[2].astype(F32)
    return (
        out.reshape(1, 128, 768), grad_inputs.reshape(1, 128, 768), g_qk, g_v, g_out, g_up, g_down,
        small[0], small[1], small[4], small[2], small[3], small[8], small[7], small[5], small[6],
    )


def solution(mesh):
    blocks = mesh.shape["ctx"] == 8 and mesh.shape["fsdp"] == 4
    return jax.shard_map(
        per_device_blocks if blocks else per_device,
        mesh=mesh,
        in_specs=(
            P("fsdp", "ctx", None),
            P("fsdp", None),
            P("fsdp", None),
            P("fsdp", None),
            P("fsdp", None),
            P("fsdp", None),
            P("fsdp"),
            P("fsdp"),
            P("fsdp"),
            P("fsdp"),
            P("fsdp"),
            P("fsdp"),
            P("fsdp"),
            P("fsdp"),
            P("fsdp"),
            P("fsdp", "ctx", None),
        ),
        out_specs=(
            P("fsdp", "ctx", None),
            P("fsdp", "ctx", None),
            P(("ctx", "fsdp"), None),
            P(("ctx", "fsdp"), None),
            P(("ctx", "fsdp"), None),
            P(("ctx", "fsdp"), None),
            P(("ctx", "fsdp"), None),
            P(("ctx", "fsdp")),
            P(("ctx", "fsdp")),
            P(("ctx", "fsdp")),
            P(("ctx", "fsdp")),
            P(("ctx", "fsdp")),
            P(("ctx", "fsdp")),
            P(("ctx", "fsdp")),
            P(("ctx", "fsdp")),
            P(("ctx", "fsdp")),
        ),
        check_vma=False,
    )
```

```python
import functools
import math

import jax
import jax.numpy as jnp
from jax import lax
from jax.experimental import pallas as pl
from jax.experimental.pallas import tpu as pltpu
from jax.sharding import PartitionSpec as P

HEADS = 12
HEAD = 64


def norm_apply(inputs, norm_gain, norm_shift):
    centre = inputs - jnp.mean(inputs, axis=-1, keepdims=True)
    spread = jnp.mean(centre * centre, axis=-1, keepdims=True)
    return centre * lax.rsqrt(spread + 1e-05) * norm_gain + norm_shift


def left_product(left, right):
    return lax.dot_general(
        left, right, (((0,), (0,)), ((), ())), preferred_element_type=jnp.float32
    )


def right_product(left, right):
    return lax.dot_general(
        left, right, (((1,), (1,)), ((), ())), preferred_element_type=jnp.float32
    )


def column_sums(matrix):
    return jnp.sum(matrix.astype(jnp.float32), axis=0)


def per_device(
    inputs,
    w_query_key,
    w_value,
    w_out,
    w_up,
    w_down,
    bias_query,
    bias_value,
    bias_out,
    gain_attn,
    shift_attn,
    bias_up,
    bias_down,
    gain_ffn,
    shift_ffn,
    cotangent,
):
    gathered = (
        lax.all_gather(w_query_key, "fsdp", axis=0, tiled=True),
        lax.all_gather(w_value, "fsdp", axis=0, tiled=True),
        lax.all_gather(w_out, "fsdp", axis=0, tiled=True),
        lax.all_gather(w_up, "fsdp", axis=0, tiled=True),
        lax.all_gather(w_down, "fsdp", axis=0, tiled=True),
        lax.all_gather(bias_query, "fsdp", axis=0, tiled=True),
        lax.all_gather(bias_value, "fsdp", axis=0, tiled=True),
        lax.all_gather(bias_out, "fsdp", axis=0, tiled=True),
        lax.all_gather(gain_attn, "fsdp", axis=0, tiled=True),
        lax.all_gather(shift_attn, "fsdp", axis=0, tiled=True),
        lax.all_gather(bias_up, "fsdp", axis=0, tiled=True),
        lax.all_gather(bias_down, "fsdp", axis=0, tiled=True),
        lax.all_gather(gain_ffn, "fsdp", axis=0, tiled=True),
        lax.all_gather(shift_ffn, "fsdp", axis=0, tiled=True),
    )
    full_qk, full_value, full_out, full_up, full_down = (
        gathered[0],
        gathered[1],
        gathered[2],
        gathered[3],
        gathered[4],
    )
    smalls = [piece.astype(jnp.float32) for piece in gathered[5:]]
    (
        vec_query,
        vec_value,
        vec_out,
        vec_gain_one,
        vec_shift_one,
        vec_up,
        vec_down,
        vec_gain_two,
        vec_shift_two,
    ) = smalls
    rows = inputs.shape[1]
    width = inputs.shape[2]
    heads = HEADS
    head = HEAD
    tokens = inputs.reshape(rows, width)
    tok_float = tokens.astype(jnp.float32)
    query_key = jnp.dot(tokens, full_qk, preferred_element_type=jnp.float32)
    queries = (query_key[:, :width] + vec_query).astype(jnp.bfloat16)
    keys = query_key[:, width:].astype(jnp.bfloat16)
    values = (jnp.dot(tokens, full_value, preferred_element_type=jnp.float32) + vec_value).astype(
        jnp.bfloat16
    )
    query_heads = queries.reshape(rows, heads, head)
    start_state = (
        jnp.full((heads, rows), -1e30, jnp.float32),
        jnp.zeros((heads, rows), jnp.float32),
        jnp.zeros((rows, heads, head), jnp.float32),
    )
    carry = start_state
    key_piece = lax.all_gather(keys, "ctx", axis=0, tiled=True)
    value_piece = lax.all_gather(values, "ctx", axis=0, tiled=True)
    count = key_piece.shape[0]
    block = math.gcd(count, 2048)
    key_split = key_piece.reshape(count // block, block, heads, head)
    value_split = value_piece.reshape(count // block, block, heads, head)

    def step_block(state, pair):
        running_max, running_sum, running_acc = state
        key_block, value_block = pair
        scores = (
            jnp.einsum("qhd,khd->hqk", query_heads, key_block, preferred_element_type=jnp.float32)
            * 0.125
        )
        new_max = jnp.maximum(running_max, jnp.max(scores, axis=-1))
        factor = jnp.exp(running_max - new_max)
        weights = jnp.exp(scores - new_max[:, :, None])
        running_sum = running_sum * factor + jnp.sum(weights, axis=-1)
        update = jnp.einsum(
            "hqk,khd->qhd",
            weights.astype(jnp.bfloat16),
            value_block,
            preferred_element_type=jnp.float32,
        )
        running_acc = running_acc * jnp.transpose(factor)[:, :, None] + update
        return ((new_max, running_sum, running_acc), None)

    carry, unused = lax.scan(step_block, carry, (key_split, value_split))
    final_max, final_sum, final_acc = carry
    attended_heads = final_acc / jnp.transpose(final_sum)[:, :, None]
    log_total = final_max + jnp.log(final_sum)
    attended_low = attended_heads.reshape(rows, width).astype(jnp.bfloat16)
    branch = jnp.dot(attended_low, full_out, preferred_element_type=jnp.float32) + vec_out
    first, norm_one_pull = jax.vjp(norm_apply, tok_float + branch, vec_gain_one, vec_shift_one)
    first_low = first.astype(jnp.bfloat16)
    hidden = jnp.dot(first_low, full_up, preferred_element_type=jnp.float32) + vec_up
    activ, gelu_pull = jax.vjp(functools.partial(jax.nn.gelu, approximate=False), hidden)
    activ_low = activ.astype(jnp.bfloat16)
    second = jnp.dot(activ_low, full_down, preferred_element_type=jnp.float32) + vec_down
    output, norm_two_pull = jax.vjp(norm_apply, first + second, vec_gain_two, vec_shift_two)
    grad_resid_two, grad_gain_ffn, grad_shift_ffn = norm_two_pull(
        cotangent.reshape(rows, width).astype(jnp.float32)
    )
    second_low = grad_resid_two.astype(jnp.bfloat16)
    grad_w_down = left_product(activ_low, second_low)
    grad_bias_down = column_sums(second_low)
    grad_activ = right_product(second_low, full_down)
    hidden_low = gelu_pull(grad_activ)[0].astype(jnp.bfloat16)
    grad_w_up = left_product(first_low, hidden_low)
    grad_bias_up = column_sums(hidden_low)
    grad_first = grad_resid_two + right_product(hidden_low, full_up)
    grad_resid_one, grad_gain_attn, grad_shift_attn = norm_one_pull(grad_first)
    branch_low = grad_resid_one.astype(jnp.bfloat16)
    grad_w_out = left_product(attended_low, branch_low)
    grad_bias_out = column_sums(branch_low)
    dout_low = right_product(branch_low, full_out).astype(jnp.bfloat16)
    dout_heads = dout_low.reshape(rows, heads, head)
    delta = jnp.einsum("qhd,qhd->hq", dout_heads.astype(jnp.float32), attended_heads)
    all_keys, all_values = (
        lax.all_gather(keys, "ctx", axis=0, tiled=True),
        lax.all_gather(values, "ctx", axis=0, tiled=True),
    )
    total = all_keys.shape[0]
    key_total = all_keys.shape[0]
    block = math.gcd(key_total, 2048)

    def back_block(grad_query, pair):
        key_block, value_block = pair
        scores = (
            jnp.einsum("qhd,khd->hqk", query_heads, key_block, preferred_element_type=jnp.float32)
            * 0.125
        )
        weights = jnp.exp(scores - log_total[:, :, None])
        weight_grad = jnp.einsum(
            "qhd,khd->hqk", dout_heads, value_block, preferred_element_type=jnp.float32
        )
        score_grad = (weights * (weight_grad - delta[:, :, None]) * 0.125).astype(jnp.bfloat16)
        grad_query = grad_query + jnp.einsum(
            "hqk,khd->qhd", score_grad, key_block, preferred_element_type=jnp.float32
        )
        value_grad = jnp.einsum(
            "hqk,qhd->khd",
            weights.astype(jnp.bfloat16),
            dout_heads,
            preferred_element_type=jnp.float32,
        )
        key_grad = jnp.einsum(
            "hqk,qhd->khd", score_grad, query_heads, preferred_element_type=jnp.float32
        )
        return (grad_query, (key_grad, value_grad))

    grad_query, terms = lax.scan(
        back_block,
        jnp.zeros((rows, heads, head), jnp.float32),
        (
            all_keys.reshape(key_total // block, block, heads, head),
            all_values.reshape(key_total // block, block, heads, head),
        ),
    )
    grad_keys, grad_values = (
        lax.psum_scatter(terms[0].reshape(total, width), "ctx", scatter_dimension=0, tiled=True),
        lax.psum_scatter(terms[1].reshape(total, width), "ctx", scatter_dimension=0, tiled=True),
    )
    grad_queries = grad_query.reshape(rows, width)
    query_low = grad_queries.astype(jnp.bfloat16)
    key_low = grad_keys.astype(jnp.bfloat16)
    value_low = grad_values.astype(jnp.bfloat16)
    query_key_low = jnp.concatenate([query_low, key_low], axis=1)
    grad_w_query_key = left_product(tokens, query_key_low)
    grad_w_value = left_product(tokens, value_low)
    grad_bias_query = column_sums(query_low)
    grad_bias_value = column_sums(value_low)
    grad_inputs = (
        grad_resid_one
        + right_product(query_key_low, full_qk)
        + right_product(value_low, full_value)
    )
    summed = (
        lax.psum_scatter(grad_w_query_key, ("ctx", "fsdp"), scatter_dimension=0, tiled=True),
        lax.psum_scatter(grad_w_value, ("ctx", "fsdp"), scatter_dimension=0, tiled=True),
        lax.psum_scatter(grad_w_out, ("ctx", "fsdp"), scatter_dimension=0, tiled=True),
        lax.psum_scatter(grad_w_up, ("ctx", "fsdp"), scatter_dimension=0, tiled=True),
        lax.psum_scatter(grad_w_down, ("ctx", "fsdp"), scatter_dimension=0, tiled=True),
        lax.psum_scatter(grad_bias_query, ("ctx", "fsdp"), scatter_dimension=0, tiled=True),
        lax.psum_scatter(grad_bias_value, ("ctx", "fsdp"), scatter_dimension=0, tiled=True),
        lax.psum_scatter(grad_bias_out, ("ctx", "fsdp"), scatter_dimension=0, tiled=True),
        lax.psum_scatter(grad_gain_attn, ("ctx", "fsdp"), scatter_dimension=0, tiled=True),
        lax.psum_scatter(grad_shift_attn, ("ctx", "fsdp"), scatter_dimension=0, tiled=True),
        lax.psum_scatter(grad_bias_up, ("ctx", "fsdp"), scatter_dimension=0, tiled=True),
        lax.psum_scatter(grad_bias_down, ("ctx", "fsdp"), scatter_dimension=0, tiled=True),
        lax.psum_scatter(grad_gain_ffn, ("ctx", "fsdp"), scatter_dimension=0, tiled=True),
        lax.psum_scatter(grad_shift_ffn, ("ctx", "fsdp"), scatter_dimension=0, tiled=True),
    )
    return (
        output.astype(jnp.bfloat16).reshape(1, rows, width),
        grad_inputs.reshape(1, rows, width),
        summed[0],
        summed[1],
        summed[2],
        summed[3],
        summed[4],
        summed[5],
        summed[6],
        summed[7],
        summed[8],
        summed[9],
        summed[10],
        summed[11],
        summed[12],
        summed[13],
    )


BF = jnp.bfloat16
F32 = jnp.float32


COST = {'qkv': 0.5, 'branch': 7.9, 'feed': 3, 'second': 7.5, 'feed_back': 16, 'first_back': 9, 'attend_back': 16, 'inner_weight': 2.2, 'feed_grad': 0.5, 'turn': 4, 'join_down': 4, 'out_grad': 2.0, 'input_sum': 1, 'stage_q': 1, 'gather_out': 10, 'pack_feed': 3.5, 'half_feed_grad': 7, 'settle_feed': 0.5}
GATES = ('both_att', 'input_qsent', 'out_back', 'out_qfar', 'out_qsent', 'piece_q', 'pm_part', 'pm_x', 'relay_att', 'relay_piece', 'turn_gin')


def local_call(body, outs, args, name, scratch=(), mib=16, final=(), raw=0):
    vmem, hbm = pl.BlockSpec(memory_space=pltpu.VMEM), pl.BlockSpec(memory_space=pltpu.HBM)
    held = [pltpu.with_memory_space_constraint(a, pltpu.HBM if i < raw else pltpu.VMEM) for i, a in enumerate(args)]
    return pl.pallas_call(
        body,
        out_shape=tuple(jax.ShapeDtypeStruct(s, d) if i in final else pltpu.VMEM(s, d) for i, (s, d) in enumerate(outs)),
        in_specs=[hbm] * raw + [vmem] * (len(args) - raw),
        out_specs=tuple(vmem for _ in outs),
        scratch_shapes=list(scratch),
        compiler_params=pltpu.CompilerParams(vmem_limit_bytes=mib * 1024 * 1024),
        cost_estimate=pl.CostEstimate(flops=int(COST.get(name, 0) * 524e6), bytes_accessed=0, transcendentals=0),
        name=name,
    )(*held)


def fetch(sems, *pairs):
    copies = [pltpu.make_async_copy(src, dst, sems.at[i]) for i, (src, dst) in enumerate(pairs)]
    for copy in copies:
        copy.start()
    for copy in copies:
        copy.wait()


def place():
    c = lax.axis_index("ctx")
    return c // 2, c % 2, lax.axis_index("fsdp")


def chip(k, j):
    return k ^ j


def mm(a, b):
    return jnp.dot(a, b, preferred_element_type=F32)


def mm_nt(a, b):
    return lax.dot_general(a, b, (((1,), (1,)), ((), ())), preferred_element_type=F32)


def mm_tn(a, b):
    return lax.dot_general(a, b, (((0,), (0,)), ((), ())), preferred_element_type=F32)


def rows_at(start, size, step):
    return pl.ds(pl.multiple_of(start, step), size)


def pack_qkv(w_qk_hbm, w_v_hbm, w_out_hbm, *rest):
    raw, (own, other, w_qk, w_v, w_out), vecs, (tmp, wide, sems) = rest[:9], rest[9:14], rest[14:23], rest[23:]
    k, h, f = place()
    fetch(sems, (w_qk_hbm, w_qk), (w_v_hbm, w_v), (w_out_hbm, w_out), *zip(raw, vecs))
    tmp[...] = jnp.zeros_like(tmp)
    for i in range(8):
        at = slice(192 * (i % 4), 192 * (i % 4) + 192)
        tmp[96 + i // 4 : 97 + i // 4, at] = vecs[i][...].astype(F32).reshape(1, 192)
    tmp[98:99, :] = vecs[8][...].astype(F32).reshape(1, 768)
    wide[...] = w_out[...].astype(F32)
    for out, half in ((own, h), (other, 1 - h)):
        rows = rows_at(half * 96, 96, 16)
        for t in range(4):
            tmp[24 * t : 24 * t + 24, 576:768] = wide[rows_at(48 * k + 24 * half, 24, 8), 192 * t : 192 * t + 192]
        out[...] = tmp[...].astype(BF)
        for kk in range(4):

            @pl.when(k == kk)
            def _():
                out[0:96, 0:192] = w_qk[rows, 192 * kk : 192 * kk + 192]
                out[0:96, 192:384] = w_qk[rows, 768 + 192 * kk : 960 + 192 * kk]
                out[0:96, 384:576] = w_v[rows, 192 * kk : 192 * kk + 192]


def pack_feed(w_up_hbm, w_down_hbm, token, own, other, w_up, w_down, sems):
    k, h, f = place()
    fetch(sems, (w_up_hbm, w_up), (w_down_hbm.at[rows_at(192 * k, 192, 16), :], w_down))
    for kk in range(4):
        for half in range(2):

            @pl.when(k == kk)
            def _():
                for which, out in enumerate((own, other)):

                    @pl.when(h == (half + which) % 2)
                    def _():
                        for g in range(4):
                            at = 768 * g + 192 * kk + 96 * half
                            out[0:192, 96 * g : 96 * g + 96] = w_up[:, at : at + 96]
                        out[192:288, :] = w_down[96 * half : 96 * half + 96, 0:384]
                        out[288:384, :] = w_down[96 * half : 96 * half + 96, 384:768]


def qkv_body(x0, x1, x2, x3, own, other, p1, p2, p3, m1, m2, m3, q, kv, w, vecs, up, tmp, vec, row):
    k, h, f = place()
    for s, (mine, mate) in enumerate(((own, other), (p1, m1), (p2, m2), (p3, m3))):
        g = f ^ s
        w[rows_at(192 * g + 96 * h, 96, 16), :] = mine[0:96, 0:576]
        w[rows_at(192 * g + 96 * (1 - h), 96, 16), :] = mate[0:96, 0:576]
        tmp[g] = mine[96:112, :].astype(F32)
    for g in range(4):
        for i in range(8):
            at = 192 * (i % 4)
            vecs[i : i + 1, 192 * g : 192 * g + 192] = tmp[g, i // 4 : i // 4 + 1, at : at + 192]
    for kk in range(4):

        @pl.when(k == kk)
        def _():
            for half in range(2):
                for g in range(4):
                    at = 192 * kk + 96 * half
                    row[0:1, 384 * half + 96 * g : 384 * half + 96 * g + 96] = tmp[g, 2:3, at : at + 96]

    up[...] = row[0:1, :]
    for i in range(2):
        vec[i : i + 1, :] = tmp[k, 0:1, 192 * i : 192 * i + 192]
    for j, x in enumerate((x0, x1, x2, x3)):
        r = mm(x[...], w[...])
        rows = slice(128 * j, 128 * j + 128)
        q[rows, :] = (r[:, 0:192] + vec[0:1, :]).astype(BF)
        kv[rows, 0:192] = r[:, 192:384].astype(BF)
        kv[rows, 192:384] = (r[:, 384:576] + vec[1:2, :]).astype(BF)


def gather_out_body(p0, p1, p2, p3, d):
    for s, p in enumerate((p0, p1, p2, p3)):
        d[:, 192 * s : 192 * s + 192] = p[0:96, 576:768]


def settle_out_body(d0, d1, d2, d3, e1, e2, e3, m0, m1, m2, m3, w_out, tmp):
    k, h, f = place()
    for half, parts in ((h, (d0, d1, d2, d3)), (1 - h, (None, e1, e2, e3))):
        for j, d in enumerate(parts):
            for s in range(4):
                rows = rows_at(192 * (f ^ s) + 48 * chip(k, j) + 24 * half, 24, 8)
                if d is None:
                    piece = (m0, m1, m2, m3)[s][0:96, 576:768].astype(F32)
                else:
                    piece = d[:, 192 * s : 192 * s + 192].astype(F32)
                for t in range(4):
                    tmp[rows, 192 * t : 192 * t + 192] = piece[24 * t : 24 * t + 24, :]
    w_out[...] = tmp[...].astype(BF)


def settle_feed_body(p0, p1, p2, p3, e0, e1, e2, e3, w_up, w_down):
    k, h, f = place()
    for half, parts in ((h, (p0, p1, p2, p3)), (1 - h, (e0, e1, e2, e3))):
        lanes = pl.ds(pl.multiple_of(384 * half, 128), 384)
        for s, part in enumerate(parts):
            g = f ^ s
            w_up[rows_at(192 * g, 192, 16), lanes] = part[0:192, :]
            rows = rows_at(384 * half + 96 * g, 96, 16)
            w_down[rows, 0:384] = part[192:288, :]
            w_down[rows, 384:768] = part[288:384, :]


def attend_body(q, kv, mate, packed, att, lse):
    for i in range(3):
        lanes, vlanes = slice(64 * i, 64 * i + 64), slice(192 + 64 * i, 256 + 64 * i)
        for t in range(4):
            rows = slice(128 * t, 128 * t + 128)
            qt = q[rows, lanes]
            sa = mm_nt(qt, kv[:, lanes]) * 0.125
            sb = mm_nt(qt, mate[:, lanes]) * 0.125
            top = jnp.maximum(jnp.max(sa, axis=1, keepdims=True), jnp.max(sb, axis=1, keepdims=True))
            ea = jnp.exp(sa - top)
            eb = jnp.exp(sb - top)
            total = jnp.sum(ea, axis=1, keepdims=True) + jnp.sum(eb, axis=1, keepdims=True)
            acc = mm(ea.astype(BF), kv[:, vlanes]) + mm(eb.astype(BF), mate[:, vlanes])
            out = acc / total
            att[i, rows, :] = out
            lse[i, rows, :] = top + jnp.log(total)
            col = 192 * (t // 2) + 64 * i
            packed[128 * (t % 2) : 128 * (t % 2) + 128, col : col + 64] = out.astype(BF)


def norm_parts(v):
    centre = v - jnp.mean(v, axis=1, keepdims=True)
    inv = lax.rsqrt(jnp.mean(centre * centre, axis=1, keepdims=True) + 1e-05)
    return centre * inv, inv


def branch_body(a0, a1, a2, a3, x0, x1, x2, x3, w_out, vecs, low, first, hat, inv):
    k, h, f = place()
    parts = (a0, a1, a2, a3)
    for m, x in enumerate((x0, x1, x2, x3)):
        acc = x[...].astype(F32) + vecs[2:3, :]
        for j in range(4):
            b = j ^ m
            a = parts[j][128 * (b % 2) : 128 * (b % 2) + 128, 192 * (b // 2) : 192 * (b // 2) + 192]
            acc = acc + mm(a, w_out[rows_at(192 * chip(k, j), 192, 16), :])
        n, r = norm_parts(acc)
        y = n * vecs[3:4, :] + vecs[4:5, :]
        low[128 * m : 128 * m + 128, :] = y.astype(BF)
        if m == 0:
            first[...] = y
            hat[...] = n
            inv[...] = r


def feed_body(low, w_up, w_down, up, own, s1, s2, s3, act, slope):
    for m, out in ((1, s1), (2, s2), (3, s3), (0, own)):
        rows = slice(128 * m, 128 * m + 128)
        hid = mm(low[rows, :], w_up[...]) + up[...]
        cdf = 0.5 * (1.0 + lax.erf(hid * (2.0**-0.5)))
        pdf = jnp.exp(hid * hid * -0.5) * ((2.0 * math.pi) ** -0.5)
        a = (hid * cdf).astype(BF)
        act[rows, :] = a
        slope[rows, :] = (cdf + hid * pdf).astype(BF)
        out[...] = mm(a, w_down[...]).astype(out.dtype)


def second_body(own, r1, r2, r3, first, vecs, cot, out, grad, low, sums):
    v = own[...] + r1[...].astype(F32) + r2[...].astype(F32) + r3[...].astype(F32)
    n, inv = norm_parts(v + first[...] + vecs[5:6, :])
    out[...] = (n * vecs[6:7, :] + vecs[7:8, :]).astype(BF)
    dy = cot[...].astype(F32)
    g, lowered = norm_back(dy, n, inv, vecs[6:7, :])
    grad[...] = g
    low[...] = lowered
    sums[...] = jnp.zeros_like(sums)
    sums[0:1, :] = jnp.sum(dy * n, axis=0, keepdims=True)
    sums[1:2, :] = jnp.sum(dy, axis=0, keepdims=True)
    sums[2:3, :] = jnp.sum(lowered.astype(F32), axis=0, keepdims=True)


def norm_back(dy, n, inv, gain):
    d = dy * gain
    g = inv * (d - jnp.mean(d, axis=1, keepdims=True) - n * jnp.mean(d * n, axis=1, keepdims=True))
    return g, g.astype(BF)


def feed_back_body(d0, d1, d2, d3, w_up, w_down, slope, own, s1, s2, s3, dhid):
    for m, d, out in ((1, d1, s1), (2, d2, s2), (3, d3, s3), (0, d0, own)):
        rows = slice(128 * m, 128 * m + 128)
        da = mm_nt(d[...], w_down[...])
        dh = (da * slope[rows, :].astype(F32)).astype(BF)
        dhid[rows, :] = dh
        out[...] = mm_nt(dh, w_up[...]).astype(out.dtype)


def feed_grad_body(act, low, d0, d1, d2, d3, dhid, keep, send_a, send_b, send_c, send_d, full, ds):
    k, h, f = place()
    for m, d in enumerate((d0, d1, d2, d3)):
        ds[128 * m : 128 * m + 128, :] = d[...]
    full[...] = mm_tn(act[...], ds[...])
    keep[0:384, :] = full[rows_at(384 * h, 384, 8), :]
    send_a[...] = full[rows_at(384 * (1 - h), 192, 8), :].astype(BF)
    send_b[...] = full[rows_at(384 * (1 - h) + 192, 192, 8), :].astype(BF)
    full[...] = mm_tn(low[...], dhid[...])
    for kk in range(4):
        keep[384 + 96 * kk : 480 + 96 * kk, :] = full[rows_at(192 * kk + 96 * h, 96, 8), :]
        out = (send_c, send_d)[kk // 2]
        out[96 * (kk % 2) : 96 * (kk % 2) + 96, :] = full[rows_at(192 * kk + 96 * (1 - h), 96, 8), :].astype(BF)
    total = jnp.sum(dhid[...].astype(F32), axis=0, keepdims=True)
    lo, hi = total[:, 0:384], total[:, 384:768]
    keep[768:784, :] = jnp.zeros((16, 768), F32)
    keep[768:769, 0:384] = jnp.where(h == 0, lo, hi)
    full[0:16, :] = jnp.zeros((16, 768), F32)
    full[0:1, 0:384] = jnp.where(h == 0, hi, lo)
    send_d[192:208, :] = full[0:16, :].astype(BF)


def first_back_body(own, r1, r2, r3, grad, hat, inv, vecs, out, low, sums):
    dy = own[...] + r1[...].astype(F32) + r2[...].astype(F32) + r3[...].astype(F32) + grad[...]
    n = hat[...]
    g, lowered = norm_back(dy, n, inv[...], vecs[3:4, :])
    out[...] = g
    low[...] = lowered
    sums[...] = jnp.zeros_like(sums)
    sums[0:1, :] = jnp.sum(dy * n, axis=0, keepdims=True)
    sums[1:2, :] = jnp.sum(dy, axis=0, keepdims=True)
    sums[2:3, :] = jnp.sum(lowered.astype(F32), axis=0, keepdims=True)


def attend_back_body(d0, d1, d2, d3, w_out, q, kv, mate, att, lse, gq, keep, send_k, send_v, dat, pa, pb, sa, sb):
    k, h, f = place()
    wk = w_out[rows_at(192 * k, 192, 16), :]
    for m, d in enumerate((d0, d1, d2, d3)):
        dat[128 * m : 128 * m + 128, :] = mm_nt(d[...], wk).astype(BF)
    for i in range(3):
        lanes, vlanes = slice(64 * i, 64 * i + 64), slice(192 + 64 * i, 256 + 64 * i)
        for t in range(4):
            rows = slice(128 * t, 128 * t + 128)
            qt = q[rows, lanes]
            do = dat[rows, lanes]
            delta = jnp.sum(do.astype(F32) * att[i, rows, :], axis=1, keepdims=True)
            total = lse[i, rows, :]
            gqt = None
            for keys, p_ref, s_ref in ((kv, pa, sa), (mate, pb, sb)):
                p = jnp.exp(mm_nt(qt, keys[:, lanes]) * 0.125 - total)
                p_ref[rows, :] = p.astype(BF)
                dp = mm_nt(do, keys[:, vlanes])
                ds = (p * (dp - delta) * 0.125).astype(BF)
                s_ref[rows, :] = ds
                part = mm(ds, keys[:, lanes])
                gqt = part if gqt is None else gqt + part
            gq[rows, lanes] = gqt.astype(BF)
        qi = q[:, lanes]
        doi = dat[:, lanes]
        keep[:, lanes] = mm_tn(sa[...], qi)
        keep[:, vlanes] = mm_tn(pa[...], doi)
        send_k[:, lanes] = mm_tn(sb[...], qi).astype(BF)
        send_v[:, lanes] = mm_tn(pb[...], doi).astype(BF)


def out_grad_body(packed, d0, d1, d2, d3, keep, send, full, att, ds):
    k, h, f = place()
    for m, d in enumerate((d0, d1, d2, d3)):
        ds[128 * m : 128 * m + 128, :] = d[...]
    att[0:256, :] = packed[:, 0:192]
    att[256:512, :] = packed[:, 192:384]
    full[...] = mm_tn(att[...], ds[...])
    keep[...] = full[rows_at(96 * h, 96, 8), :]
    send[...] = full[rows_at(96 * (1 - h), 96, 8), :].astype(BF)


def inner_weight_body(gq, gk, got_k, got_v, x0, x1, x2, x3, sums_a, sums_b, g, keep, send_a, send_b, full, cols, xs):
    k, h, f = place()
    g[:, 0:192] = gq[...]
    g[:, 192:384] = (gk[:, 0:192] + got_k[...].astype(F32)).astype(BF)
    g[:, 384:576] = (gk[:, 192:384] + got_v[...].astype(F32)).astype(BF)
    for m, x in enumerate((x0, x1, x2, x3)):
        xs[128 * m : 128 * m + 128, :] = x[...]
    cols[...] = jnp.zeros_like(cols)
    bias = jnp.sum(g[...].astype(F32), axis=0, keepdims=True)
    for kk in range(4):

        @pl.when(k == kk)
        def _():
            cols[64:65, 192 * kk : 192 * kk + 192] = bias[:, 0:192]
            cols[65:66, 192 * kk : 192 * kk + 192] = bias[:, 384:576]

    cols[66:69, :] = sums_b[0:3, :]
    cols[69:72, :] = sums_a[0:3, :]
    full[:, 0:576] = mm_tn(xs[...], g[...])
    lane = lax.broadcasted_iota(jnp.int32, (768, 128), 1)
    full[:, 512:640] = jnp.where(lane < 64, full[:, 512:640], jnp.transpose(cols[...]))
    for kk in range(4):
        at = slice(96 * kk, 96 * kk + 96)
        keep[at, :] = full[rows_at(192 * kk + 96 * h, 96, 8), :]
        out = (send_a, send_b)[kk // 2]
        out[96 * (kk % 2) : 96 * (kk % 2) + 96, :] = full[rows_at(192 * kk + 96 * (1 - h), 96, 8), :].astype(BF)


def inner_input_body(g, w, own, s1, s2, s3):
    for m, out in ((1, s1), (2, s2), (3, s3), (0, own)):
        out[...] = mm_nt(g[128 * m : 128 * m + 128, :], w[...]).astype(out.dtype)


def input_sum_body(grad, own, r1, r2, r3, out):
    out[...] = grad[...] + own[...] + r1[...].astype(F32) + r2[...].astype(F32) + r3[...].astype(F32)


def stage_feed_body(keep, got_a, got_b, got_c, got_d, held, sent, tmp, one):
    k, h, f = place()
    for at, n, got in ((0, 192, got_a), (192, 192, got_b), (384, 192, got_c), (576, 208, got_d)):
        tmp[at : at + n, :] = keep[at : at + n, :] + got[...].astype(F32)
    for g in range(4):
        one[g] = jnp.zeros((16, 768), F32)
        one[g, 0:1, 0:96] = tmp[768:769, 96 * g : 96 * g + 96]
    for s in range(4):
        out, g = (held, sent)[s % 2], f ^ s
        v = [tmp[rows_at(96 * g, 96, 8), :], one[g]] + [tmp[rows_at(384 + 96 * kk + 24 * g, 24, 8), :] for kk in range(4)]
        out[208 * (s // 2) : 208 * (s // 2) + 208, :] = jnp.concatenate(v, axis=0).astype(out.dtype)


def stage_q_body(keep, got_a, got_b, held, sent, tmp):
    k, h, f = place()
    tmp[0:192, :] = keep[0:192, :] + got_a[...].astype(F32)
    tmp[192:384, :] = keep[192:384, :] + got_b[...].astype(F32)
    for s in range(4):
        out = (held, sent)[s % 2]
        v = [tmp[rows_at(96 * kk + 24 * (f ^ s), 24, 8), :] for kk in range(4)]
        out[96 * (s // 2) : 96 * (s // 2) + 96, :] = jnp.concatenate(v, axis=0).astype(out.dtype)


def stage_out_body(keep, got, held, sent, tmp):
    k, h, f = place()
    tmp[...] = keep[...] + got[...].astype(F32)
    for half, out in enumerate((held, sent)):
        v = [tmp[rows_at(24 * (f ^ s), 24, 8), :] for s in (half, half + 2)]
        out[...] = jnp.concatenate(v, axis=0).astype(out.dtype)


def half_body(held, got, own, far):
    n = own.shape[0]
    own[...] = held[0:n, :] + got[0:n, :].astype(F32)
    far[...] = (held[n : 2 * n, :] + got[n : 2 * n, :].astype(F32)).astype(BF)


def half_out_body(held, got, own, far):
    v = held[...] + got[...].astype(F32)
    own[...] = v[0:24, :]
    far[...] = v[24:48, :].astype(BF)


def join_down_body(own, r, down, up):
    v = own[...] + r[...].astype(F32)
    down[...] = v[0:112, :].astype(BF)
    up[...] = v[112:208, :]


def turn_body(own, r, up, a0, a1, a2, a3, tmp):
    k, h, f = place()
    v = own[...] + r[...].astype(F32)
    u = up[...]
    for kk in range(4):
        tmp[kk, :, 0:768] = u[24 * kk : 24 * kk + 24, :]
        tmp[kk, :, 768:1408] = v[24 * kk : 24 * kk + 24, :]
    for j, out in enumerate((a0, a1, a2, a3)):
        out[...] = tmp[chip(k, j)].astype(out.dtype)


def finish_down_body(down, out, o1, w_down, w_out, bias_up):
    w_down[...] = down[0:96, :].astype(F32)
    bias_up[...] = down[96:112, :].astype(F32)[0:1, 0:96].reshape(96)
    w_out[...] = out[...] + o1[...].astype(F32)


def finish_body(own, r1, r2, r3, w_qk, w_v, w_up, *rest):
    vecs, tmp = rest[:8], rest[8]
    k, h, f = place()
    total = None
    for j, r in enumerate((own, r1, r2, r3)):
        v = r[...].astype(F32)
        tmp[chip(k, j)] = v
        part = v[:, 1280:1408]
        total = part if total is None else total + part
    for kk in range(4):
        v = tmp[kk]
        for half in range(2):
            for g in range(4):
                at = 768 * g + 192 * kk + 96 * half
                w_up[:, at : at + 96] = v[:, 384 * half + 96 * g : 384 * half + 96 * g + 96]
        w_qk[:, 192 * kk : 192 * kk + 192] = v[:, 768:960]
        w_qk[:, 768 + 192 * kk : 960 + 192 * kk] = v[:, 960:1152]
        w_v[:, 192 * kk : 192 * kk + 192] = v[:, 1152:1344]
    turned = jnp.transpose(jnp.concatenate([total, jnp.zeros((104, 128), F32)], axis=0))
    for i in range(8):
        vecs[i][...] = turned[64 + i : 65 + i, 0:24].reshape(24)


def swap(x):
    return lax.ppermute(x, "ctx", [(i, i ^ 1) for i in range(8)])


def to_chip(x, j):
    return lax.ppermute(x, "ctx", [(i, i ^ (2 * j)) for i in range(8)])


def to_plane(x, s):
    return lax.ppermute(x, "fsdp", [(i, i ^ s) for i in range(4)])


def plane(xs):
    return [to_chip(x, j) for j, x in enumerate(xs, 1)]


def gather_plane(x, name=""):
    if "relay_" + name in GATES:
        a = to_chip(x, 1)
        return [x, a, to_chip(x, 2), to_chip(a, 2)]
    return [x, *plane([x] * 3)]


def gate(name, value, *others):
    return after(value, *others) if name in GATES else value


def gather_z(x):
    return [x, to_plane(x, 1), to_plane(x, 2)]


def sum_z(body, mid, outs, args, name, scratch, gate=()):
    rows, lanes = outs
    held, sent = local_call(body, [((2 * rows, lanes), F32), ((2 * rows, lanes), BF)], args, "stage_" + name, scratch)
    own, far = local_call(mid, [((rows, lanes), F32), ((rows, lanes), BF)], [after(held, *gate), to_plane(sent, 1)], "half_" + name)
    return sent, far, own, to_plane(far, 2)


def after(value, *others):
    return lax.optimization_barrier((value, *others))[0]


def per_device_blocks(
    inputs, w_query_key, w_value, w_out, w_up, w_down, bias_query, bias_value, bias_out,
    gain_attn, shift_attn, bias_up, bias_down, gain_ffn, shift_ffn, cotangent,
):
    c = lax.axis_index("ctx")
    x0 = inputs.reshape(128, 768)
    cot = cotangent.reshape(128, 768)
    block, wide = ((128, 768), BF), ((128, 768), F32)
    vectors = [bias_query, bias_value, bias_out, gain_attn, shift_attn, bias_down, gain_ffn, shift_ffn, bias_up]

    own, other = local_call(
        pack_qkv, [((112, 768), BF)] * 2, [w_query_key, w_value, w_out] + vectors, "pack_qkv",
        [pltpu.VMEM((192, 1536), BF), pltpu.VMEM((192, 768), BF), pltpu.VMEM((192, 768), BF)]
        + [pltpu.VMEM((192,), BF)] * 8
        + [pltpu.VMEM((768,), BF), pltpu.VMEM((112, 768), F32), pltpu.VMEM((192, 768), F32), pltpu.SemaphoreType.DMA((12,))],
        raw=12,
    )
    pz = gather_z(own)[1:]
    pz.append(to_plane(pz[1], 1))
    xs = gather_plane(x0, "x")
    part, mate_part = local_call(
        pack_feed, [((384, 384), BF)] * 2, [w_up, w_down, own], "pack_feed",
        [pltpu.VMEM((192, 3072), BF), pltpu.VMEM((192, 768), BF), pltpu.SemaphoreType.DMA((2,))],
        raw=2,
    )
    parts = gather_z(part)
    pm = [swap(gate("pm_x", gate("pm_far", gate("pm_part", p, part), parts[2]), *xs[1:])) for p in pz]
    q, kv, w_qkv, vecs, up = local_call(
        qkv_body,
        [((512, 192), BF), ((512, 384), BF), ((768, 576), BF), ((8, 768), F32), ((1, 768), F32)],
        xs + [own, other] + pz + pm, "qkv",
        [pltpu.VMEM((4, 16, 768), F32), pltpu.VMEM((8, 192), F32), pltpu.VMEM((8, 768), F32)],
    )
    kv = [kv, swap(kv)]
    (piece,) = local_call(gather_out_body, [((96, 768), BF)], [own] + pz, "gather_out")
    ds = gather_plane(gate("piece_q", piece, q), "piece")
    both = gate("both_q", parts[2], q)
    packed, att, lse = local_call(
        attend_body, [((256, 384), BF), ((3, 512, 64), F32), ((3, 512, 1), F32)], [q] + kv, "attend"
    )
    both = gate("both_att", both, packed)
    parts.append(to_plane(both, 1))
    atts = gather_plane(packed, "att")
    (full_out,) = local_call(
        settle_out_body, [((768, 768), BF)], ds + [swap(gate("ds_att", d, packed)) for d in ds[1:]] + [other] + pm, "settle_out",
        [pltpu.VMEM((768, 768), F32)],
    )
    full_up, full_down = local_call(
        settle_feed_body, [((768, 768), BF)] * 2, parts + [mate_part] + [swap(p) for p in parts[1:]], "settle_feed"
    )
    low, first, hat, inv = local_call(
        branch_body, [((512, 768), BF), wide, wide, ((128, 1), F32)], atts + xs + [full_out, vecs], "branch"
    )
    sec, s1, s2, s3, act, slope = local_call(
        feed_body, [wide, block, block, block, ((512, 768), BF), ((512, 768), BF)], [low, full_up, full_down, up], "feed",

    )
    out, grad_two, dsec, sums_two = local_call(
        second_body, [block, wide, block, ((8, 768), F32)], [sec] + plane([s1, s2, s3]) + [first, vecs, cot], "second", final=(0,)
    )
    dsecs = gather_plane(dsec, "dsec")
    gfo, s1, s2, s3, dhid = local_call(
        feed_back_body, [wide, block, block, block, ((512, 768), BF)], dsecs + [full_up, full_down, slope], "feed_back",

    )
    gfo = [gfo] + plane([s1, s2, s3])
    fkeep, *fsend = local_call(
        feed_grad_body, [((784, 768), F32)] + [((192, 768), BF)] * 3 + [((208, 768), BF)], [act, low] + dsecs + [dhid],
        "feed_grad", [pltpu.VMEM((768, 768), F32), pltpu.VMEM((512, 768), BF)],
    )
    fsent, ffar, fown, fgot = sum_z(
        stage_feed_body, half_body, (208, 768), [fkeep] + [swap(x) for x in fsend], "feed_grad",
        [pltpu.VMEM((784, 768), F32), pltpu.VMEM((4, 16, 768), F32)],
    )
    down, up_sum = local_call(join_down_body, [((112, 768), BF), ((96, 768), F32)], [fown, fgot], "join_down")
    down = lax.ppermute(down, ("ctx", "fsdp"), [(4 * i + z, 8 * z + i) for i in range(8) for z in range(4)])
    grad_one, dbr, sums_one = local_call(
        first_back_body, [wide, block, ((8, 768), F32)], [gate("first_back_fsent", gfo[0], fsent)] + gfo[1:] + [grad_two, hat, inv, vecs], "first_back"
    )
    dbrs = gather_plane(dbr, "dbr")
    gq, gkeep, gk_send, gv_send = local_call(
        attend_back_body, [((512, 192), BF), ((512, 384), F32), ((512, 192), BF), ((512, 192), BF)],
        dbrs + [full_out, gate("back_ffar", gate("back_fsent", q, fsent), ffar)] + kv + [att, lse], "attend_back",
        [pltpu.VMEM((512, 192), BF)] + [pltpu.VMEM((512, 512), BF)] * 4,
    )
    gk_got, gv_got = swap(gate("gk_ffar", gk_send, ffar)), swap(gv_send)
    g, qkeep, qsend_a, qsend_b = local_call(
        inner_weight_body, [((512, 576), BF), ((384, 640), F32), ((192, 640), BF), ((192, 640), BF)],
        [gate("weight_ffar", gq, ffar), gkeep, gk_got, gv_got] + xs + [sums_two, sums_one], "inner_weight",
        [pltpu.VMEM((768, 640), F32), pltpu.VMEM((128, 768), F32), pltpu.VMEM((512, 768), BF)],
    )
    qsent, qfar_sent, qown, qfar = sum_z(
        stage_q_body, half_body, (96, 640), [qkeep, swap(qsend_a), swap(qsend_b)], "q", [pltpu.VMEM((384, 640), F32)],
        [up_sum] if "q_join" in GATES else [],
    )
    gin, s1, s2, s3 = local_call(inner_input_body, [wide, block, block, block], [gate("input_qsent", g, qsent), w_qkv], "inner_input")
    gin = [gin] + plane([s1, s2, s3])
    okeep, osend = local_call(
        out_grad_body, [((96, 768), F32), ((96, 768), BF)], [gate("out_back", packed, gq)] + dbrs, "out_grad",
        [pltpu.VMEM((192, 768), F32), pltpu.VMEM((512, 192), BF), pltpu.VMEM((512, 768), BF)],
    )
    _, _, oown, ofar = sum_z(
        stage_out_body, half_out_body, (24, 768), [gate("out_qsent", okeep, qsent), swap(gate("osend_qsend", osend, qsend_a))], "out", [pltpu.VMEM((96, 768), F32)],
        [qfar_sent] if "out_qfar" in GATES else [],
    )
    a0, a1, a2, a3 = local_call(
        turn_body, [((24, 1408), F32)] + [((24, 1408), BF)] * 3, [gate("turn_gin", gate("turn_down", qown, down), *gin[1:]), qfar, up_sum], "turn", scratch=[pltpu.VMEM((4, 24, 1408), F32)]
    )
    aa = plane([a1, a2, a3])
    g_qk, g_v, g_up, *small = local_call(
        finish_body, [((24, 1536), F32), ((24, 768), F32), ((24, 3072), F32)] + [((24,), F32)] * 8, [a0] + aa, "finish",
        [pltpu.VMEM((4, 24, 1408), F32)], final=range(11),
    )
    g_down, g_out, g_bias_up = local_call(
        finish_down_body, [((96, 768), F32), ((24, 768), F32), ((96,), F32)], [down, oown, ofar], "finish_down",
        final=range(3),
    )
    (grad_inputs,) = local_call(input_sum_body, [wide], [gate("input_down", grad_one, down)] + gin, "input_sum", final=(0,))
    return (
        out.reshape(1, 128, 768), grad_inputs.reshape(1, 128, 768), g_qk, g_v, g_out, g_up, g_down,
        small[0], small[1], small[4], small[2], small[3], g_bias_up, small[7], small[5], small[6],
    )


def solution(mesh):
    blocks = mesh.shape["ctx"] == 8 and mesh.shape["fsdp"] == 4
    return jax.shard_map(
        per_device_blocks if blocks else per_device,
        mesh=mesh,
        in_specs=(
            P("fsdp", "ctx", None),
            P("fsdp", None),
            P("fsdp", None),
            P("fsdp", None),
            P("fsdp", None),
            P("fsdp", None),
            P("fsdp"),
            P("fsdp"),
            P("fsdp"),
            P("fsdp"),
            P("fsdp"),
            P("fsdp"),
            P("fsdp"),
            P("fsdp"),
            P("fsdp"),
            P("fsdp", "ctx", None),
        ),
        out_specs=(
            P("fsdp", "ctx", None),
            P("fsdp", "ctx", None),
            P(("ctx", "fsdp"), None),
            P(("ctx", "fsdp"), None),
            P(("ctx", "fsdp"), None),
            P(("ctx", "fsdp"), None),
            P(("ctx", "fsdp"), None),
            P(("ctx", "fsdp")),
            P(("ctx", "fsdp")),
            P(("ctx", "fsdp")),
            P(("ctx", "fsdp")),
            P(("ctx", "fsdp")),
            P(("ctx", "fsdp")),
            P(("ctx", "fsdp")),
            P(("ctx", "fsdp")),
            P(("ctx", "fsdp")),
        ),
        check_vma=False,
    )
```

```python
import functools
import math

import jax
import jax.numpy as jnp
from jax import lax
from jax.experimental import pallas as pl
from jax.experimental.pallas import tpu as pltpu
from jax.sharding import PartitionSpec as P

HEADS = 12
HEAD = 64


def norm_apply(inputs, norm_gain, norm_shift):
    centre = inputs - jnp.mean(inputs, axis=-1, keepdims=True)
    spread = jnp.mean(centre * centre, axis=-1, keepdims=True)
    return centre * lax.rsqrt(spread + 1e-05) * norm_gain + norm_shift


def left_product(left, right):
    return lax.dot_general(
        left, right, (((0,), (0,)), ((), ())), preferred_element_type=jnp.float32
    )


def right_product(left, right):
    return lax.dot_general(
        left, right, (((1,), (1,)), ((), ())), preferred_element_type=jnp.float32
    )


def column_sums(matrix):
    return jnp.sum(matrix.astype(jnp.float32), axis=0)


def per_device(
    inputs,
    w_query_key,
    w_value,
    w_out,
    w_up,
    w_down,
    bias_query,
    bias_value,
    bias_out,
    gain_attn,
    shift_attn,
    bias_up,
    bias_down,
    gain_ffn,
    shift_ffn,
    cotangent,
):
    gathered = (
        lax.all_gather(w_query_key, "fsdp", axis=0, tiled=True),
        lax.all_gather(w_value, "fsdp", axis=0, tiled=True),
        lax.all_gather(w_out, "fsdp", axis=0, tiled=True),
        lax.all_gather(w_up, "fsdp", axis=0, tiled=True),
        lax.all_gather(w_down, "fsdp", axis=0, tiled=True),
        lax.all_gather(bias_query, "fsdp", axis=0, tiled=True),
        lax.all_gather(bias_value, "fsdp", axis=0, tiled=True),
        lax.all_gather(bias_out, "fsdp", axis=0, tiled=True),
        lax.all_gather(gain_attn, "fsdp", axis=0, tiled=True),
        lax.all_gather(shift_attn, "fsdp", axis=0, tiled=True),
        lax.all_gather(bias_up, "fsdp", axis=0, tiled=True),
        lax.all_gather(bias_down, "fsdp", axis=0, tiled=True),
        lax.all_gather(gain_ffn, "fsdp", axis=0, tiled=True),
        lax.all_gather(shift_ffn, "fsdp", axis=0, tiled=True),
    )
    full_qk, full_value, full_out, full_up, full_down = (
        gathered[0],
        gathered[1],
        gathered[2],
        gathered[3],
        gathered[4],
    )
    smalls = [piece.astype(jnp.float32) for piece in gathered[5:]]
    (
        vec_query,
        vec_value,
        vec_out,
        vec_gain_one,
        vec_shift_one,
        vec_up,
        vec_down,
        vec_gain_two,
        vec_shift_two,
    ) = smalls
    rows = inputs.shape[1]
    width = inputs.shape[2]
    heads = HEADS
    head = HEAD
    tokens = inputs.reshape(rows, width)
    tok_float = tokens.astype(jnp.float32)
    query_key = jnp.dot(tokens, full_qk, preferred_element_type=jnp.float32)
    queries = (query_key[:, :width] + vec_query).astype(jnp.bfloat16)
    keys = query_key[:, width:].astype(jnp.bfloat16)
    values = (jnp.dot(tokens, full_value, preferred_element_type=jnp.float32) + vec_value).astype(
        jnp.bfloat16
    )
    query_heads = queries.reshape(rows, heads, head)
    start_state = (
        jnp.full((heads, rows), -1e30, jnp.float32),
        jnp.zeros((heads, rows), jnp.float32),
        jnp.zeros((rows, heads, head), jnp.float32),
    )
    carry = start_state
    key_piece = lax.all_gather(keys, "ctx", axis=0, tiled=True)
    value_piece = lax.all_gather(values, "ctx", axis=0, tiled=True)
    count = key_piece.shape[0]
    block = math.gcd(count, 2048)
    key_split = key_piece.reshape(count // block, block, heads, head)
    value_split = value_piece.reshape(count // block, block, heads, head)

    def step_block(state, pair):
        running_max, running_sum, running_acc = state
        key_block, value_block = pair
        scores = (
            jnp.einsum("qhd,khd->hqk", query_heads, key_block, preferred_element_type=jnp.float32)
            * 0.125
        )
        new_max = jnp.maximum(running_max, jnp.max(scores, axis=-1))
        factor = jnp.exp(running_max - new_max)
        weights = jnp.exp(scores - new_max[:, :, None])
        running_sum = running_sum * factor + jnp.sum(weights, axis=-1)
        update = jnp.einsum(
            "hqk,khd->qhd",
            weights.astype(jnp.bfloat16),
            value_block,
            preferred_element_type=jnp.float32,
        )
        running_acc = running_acc * jnp.transpose(factor)[:, :, None] + update
        return ((new_max, running_sum, running_acc), None)

    carry, unused = lax.scan(step_block, carry, (key_split, value_split))
    final_max, final_sum, final_acc = carry
    attended_heads = final_acc / jnp.transpose(final_sum)[:, :, None]
    log_total = final_max + jnp.log(final_sum)
    attended_low = attended_heads.reshape(rows, width).astype(jnp.bfloat16)
    branch = jnp.dot(attended_low, full_out, preferred_element_type=jnp.float32) + vec_out
    first, norm_one_pull = jax.vjp(norm_apply, tok_float + branch, vec_gain_one, vec_shift_one)
    first_low = first.astype(jnp.bfloat16)
    hidden = jnp.dot(first_low, full_up, preferred_element_type=jnp.float32) + vec_up
    activ, gelu_pull = jax.vjp(functools.partial(jax.nn.gelu, approximate=False), hidden)
    activ_low = activ.astype(jnp.bfloat16)
    second = jnp.dot(activ_low, full_down, preferred_element_type=jnp.float32) + vec_down
    output, norm_two_pull = jax.vjp(norm_apply, first + second, vec_gain_two, vec_shift_two)
    grad_resid_two, grad_gain_ffn, grad_shift_ffn = norm_two_pull(
        cotangent.reshape(rows, width).astype(jnp.float32)
    )
    second_low = grad_resid_two.astype(jnp.bfloat16)
    grad_w_down = left_product(activ_low, second_low)
    grad_bias_down = column_sums(second_low)
    grad_activ = right_product(second_low, full_down)
    hidden_low = gelu_pull(grad_activ)[0].astype(jnp.bfloat16)
    grad_w_up = left_product(first_low, hidden_low)
    grad_bias_up = column_sums(hidden_low)
    grad_first = grad_resid_two + right_product(hidden_low, full_up)
    grad_resid_one, grad_gain_attn, grad_shift_attn = norm_one_pull(grad_first)
    branch_low = grad_resid_one.astype(jnp.bfloat16)
    grad_w_out = left_product(attended_low, branch_low)
    grad_bias_out = column_sums(branch_low)
    dout_low = right_product(branch_low, full_out).astype(jnp.bfloat16)
    dout_heads = dout_low.reshape(rows, heads, head)
    delta = jnp.einsum("qhd,qhd->hq", dout_heads.astype(jnp.float32), attended_heads)
    all_keys, all_values = (
        lax.all_gather(keys, "ctx", axis=0, tiled=True),
        lax.all_gather(values, "ctx", axis=0, tiled=True),
    )
    total = all_keys.shape[0]
    key_total = all_keys.shape[0]
    block = math.gcd(key_total, 2048)

    def back_block(grad_query, pair):
        key_block, value_block = pair
        scores = (
            jnp.einsum("qhd,khd->hqk", query_heads, key_block, preferred_element_type=jnp.float32)
            * 0.125
        )
        weights = jnp.exp(scores - log_total[:, :, None])
        weight_grad = jnp.einsum(
            "qhd,khd->hqk", dout_heads, value_block, preferred_element_type=jnp.float32
        )
        score_grad = (weights * (weight_grad - delta[:, :, None]) * 0.125).astype(jnp.bfloat16)
        grad_query = grad_query + jnp.einsum(
            "hqk,khd->qhd", score_grad, key_block, preferred_element_type=jnp.float32
        )
        value_grad = jnp.einsum(
            "hqk,qhd->khd",
            weights.astype(jnp.bfloat16),
            dout_heads,
            preferred_element_type=jnp.float32,
        )
        key_grad = jnp.einsum(
            "hqk,qhd->khd", score_grad, query_heads, preferred_element_type=jnp.float32
        )
        return (grad_query, (key_grad, value_grad))

    grad_query, terms = lax.scan(
        back_block,
        jnp.zeros((rows, heads, head), jnp.float32),
        (
            all_keys.reshape(key_total // block, block, heads, head),
            all_values.reshape(key_total // block, block, heads, head),
        ),
    )
    grad_keys, grad_values = (
        lax.psum_scatter(terms[0].reshape(total, width), "ctx", scatter_dimension=0, tiled=True),
        lax.psum_scatter(terms[1].reshape(total, width), "ctx", scatter_dimension=0, tiled=True),
    )
    grad_queries = grad_query.reshape(rows, width)
    query_low = grad_queries.astype(jnp.bfloat16)
    key_low = grad_keys.astype(jnp.bfloat16)
    value_low = grad_values.astype(jnp.bfloat16)
    query_key_low = jnp.concatenate([query_low, key_low], axis=1)
    grad_w_query_key = left_product(tokens, query_key_low)
    grad_w_value = left_product(tokens, value_low)
    grad_bias_query = column_sums(query_low)
    grad_bias_value = column_sums(value_low)
    grad_inputs = (
        grad_resid_one
        + right_product(query_key_low, full_qk)
        + right_product(value_low, full_value)
    )
    summed = (
        lax.psum_scatter(grad_w_query_key, ("ctx", "fsdp"), scatter_dimension=0, tiled=True),
        lax.psum_scatter(grad_w_value, ("ctx", "fsdp"), scatter_dimension=0, tiled=True),
        lax.psum_scatter(grad_w_out, ("ctx", "fsdp"), scatter_dimension=0, tiled=True),
        lax.psum_scatter(grad_w_up, ("ctx", "fsdp"), scatter_dimension=0, tiled=True),
        lax.psum_scatter(grad_w_down, ("ctx", "fsdp"), scatter_dimension=0, tiled=True),
        lax.psum_scatter(grad_bias_query, ("ctx", "fsdp"), scatter_dimension=0, tiled=True),
        lax.psum_scatter(grad_bias_value, ("ctx", "fsdp"), scatter_dimension=0, tiled=True),
        lax.psum_scatter(grad_bias_out, ("ctx", "fsdp"), scatter_dimension=0, tiled=True),
        lax.psum_scatter(grad_gain_attn, ("ctx", "fsdp"), scatter_dimension=0, tiled=True),
        lax.psum_scatter(grad_shift_attn, ("ctx", "fsdp"), scatter_dimension=0, tiled=True),
        lax.psum_scatter(grad_bias_up, ("ctx", "fsdp"), scatter_dimension=0, tiled=True),
        lax.psum_scatter(grad_bias_down, ("ctx", "fsdp"), scatter_dimension=0, tiled=True),
        lax.psum_scatter(grad_gain_ffn, ("ctx", "fsdp"), scatter_dimension=0, tiled=True),
        lax.psum_scatter(grad_shift_ffn, ("ctx", "fsdp"), scatter_dimension=0, tiled=True),
    )
    return (
        output.astype(jnp.bfloat16).reshape(1, rows, width),
        grad_inputs.reshape(1, rows, width),
        summed[0],
        summed[1],
        summed[2],
        summed[3],
        summed[4],
        summed[5],
        summed[6],
        summed[7],
        summed[8],
        summed[9],
        summed[10],
        summed[11],
        summed[12],
        summed[13],
    )


BF = jnp.bfloat16
F32 = jnp.float32


COST = dict(qkv=5, attend=7, branch=15, feed=7, second=5.5, feed_back=20, first_back=14, attend_back=5, inner_input=4, feed_grad=0.5, turn=5, join_down=14, out_grad=8.0, stage_q=4, gather_out=13.5, pack_feed=2, stage_out=7, settle_out=0.5, settle_feed=12, half_up=7, stage_down=14, half_q=0.5, stage_up=4, stage_feed_grad=3, finish_down=10)


def local_call(body, outs, args, name, scratch=(), mib=16, final=(), raw=0):
    vmem, hbm = pl.BlockSpec(memory_space=pltpu.VMEM), pl.BlockSpec(memory_space=pltpu.HBM)
    held = [pltpu.with_memory_space_constraint(a, pltpu.HBM if i < raw else pltpu.VMEM) for i, a in enumerate(args)]
    return pl.pallas_call(
        body,
        out_shape=tuple(jax.ShapeDtypeStruct(s, d) if i in final else pltpu.VMEM(s, d) for i, (s, d) in enumerate(outs)),
        in_specs=[hbm] * raw + [vmem] * (len(args) - raw),
        out_specs=tuple(vmem for _ in outs),
        scratch_shapes=list(scratch),
        compiler_params=pltpu.CompilerParams(vmem_limit_bytes=mib * 1024 * 1024),
        cost_estimate=pl.CostEstimate(flops=int(COST.get(name, 0) * 524e6), bytes_accessed=0, transcendentals=0),
        name=name,
    )(*held)


def fetch(sems, *pairs):
    copies = [pltpu.make_async_copy(src, dst, sems.at[i]) for i, (src, dst) in enumerate(pairs)]
    for copy in copies:
        copy.start()
    for copy in copies:
        copy.wait()


def place():
    c = lax.axis_index("ctx")
    return c // 2, c % 2, lax.axis_index("fsdp")


def chip(k, j):
    return k ^ j


def mm(a, b):
    return jnp.dot(a, b, preferred_element_type=F32)


def mm_nt(a, b):
    return lax.dot_general(a, b, (((1,), (1,)), ((), ())), preferred_element_type=F32)


def mm_tn(a, b):
    return lax.dot_general(a, b, (((0,), (0,)), ((), ())), preferred_element_type=F32)


def rows_at(start, size, step):
    return pl.ds(pl.multiple_of(start, step), size)


def pack_qkv(w_qk_hbm, w_v_hbm, w_out_hbm, *rest):
    raw, (own, other, w_qk, w_v, w_out), vecs, (tmp, wide, sems) = rest[:9], rest[9:14], rest[14:23], rest[23:]
    k, h, f = place()
    fetch(sems, (w_qk_hbm, w_qk), (w_v_hbm, w_v), (w_out_hbm, w_out), *zip(raw, vecs))
    tmp[...] = jnp.zeros_like(tmp)
    for i in range(8):
        at = slice(192 * (i % 4), 192 * (i % 4) + 192)
        tmp[96 + i // 4 : 97 + i // 4, at] = vecs[i][...].astype(F32).reshape(1, 192)
    tmp[98:99, :] = vecs[8][...].astype(F32).reshape(1, 768)
    wide[...] = w_out[...].astype(F32)
    for out, half in ((own, h), (other, 1 - h)):
        rows = rows_at(half * 96, 96, 16)
        for t in range(4):
            tmp[24 * t : 24 * t + 24, 576:768] = wide[rows_at(48 * k + 24 * half, 24, 8), 192 * t : 192 * t + 192]
        out[...] = tmp[...].astype(BF)
        for kk in range(4):

            @pl.when(k == kk)
            def _():
                out[0:96, 0:192] = w_qk[rows, 192 * kk : 192 * kk + 192]
                out[0:96, 192:384] = w_qk[rows, 768 + 192 * kk : 960 + 192 * kk]
                out[0:96, 384:576] = w_v[rows, 192 * kk : 192 * kk + 192]


def pack_feed(w_up_hbm, w_down_hbm, token, own, other, w_up, w_down, sems):
    k, h, f = place()
    fetch(sems, (w_up_hbm, w_up), (w_down_hbm.at[rows_at(192 * k, 192, 16), :], w_down))
    for kk in range(4):
        for half in range(2):

            @pl.when(k == kk)
            def _():
                for which, out in enumerate((own, other)):

                    @pl.when(h == (half + which) % 2)
                    def _():
                        for g in range(4):
                            at = 768 * g + 192 * kk + 96 * half
                            out[0:192, 96 * g : 96 * g + 96] = w_up[:, at : at + 96]
                        out[192:288, :] = w_down[96 * half : 96 * half + 96, 0:384]
                        out[288:384, :] = w_down[96 * half : 96 * half + 96, 384:768]


def qkv_body(x0, x1, x2, x3, own, other, p1, p2, p3, m1, m2, m3, q, kv, w, vecs, up, tmp, vec, row, xs):
    k, h, f = place()
    for s, (mine, mate) in enumerate(((own, other), (p1, m1), (p2, m2), (p3, m3))):
        g = f ^ s
        w[rows_at(192 * g + 96 * h, 96, 16), :] = mine[0:96, 0:576]
        w[rows_at(192 * g + 96 * (1 - h), 96, 16), :] = mate[0:96, 0:576]
        tmp[g] = mine[96:112, :].astype(F32)
    for g in range(4):
        for i in range(8):
            at = 192 * (i % 4)
            vecs[i : i + 1, 192 * g : 192 * g + 192] = tmp[g, i // 4 : i // 4 + 1, at : at + 192]
    for kk in range(4):

        @pl.when(k == kk)
        def _():
            for half in range(2):
                for g in range(4):
                    at = 192 * kk + 96 * half
                    row[0:1, 384 * half + 96 * g : 384 * half + 96 * g + 96] = tmp[g, 2:3, at : at + 96]

    up[...] = row[0:1, :]
    for i in range(2):
        vec[i : i + 1, :] = tmp[k, 0:1, 192 * i : 192 * i + 192]
    for j, x in enumerate((x0, x1, x2, x3)):
        xs[128 * j : 128 * j + 128, :] = x[...]
    r = mm(xs[...], w[...])
    q[...] = ((r[:, 0:192] + vec[0:1, :]) * 0.125).astype(BF)
    kv[:, 0:192] = r[:, 192:384].astype(BF)
    kv[:, 192:384] = (r[:, 384:576] + vec[1:2, :]).astype(BF)


def gather_out_body(p0, p1, p2, p3, d):
    for s, p in enumerate((p0, p1, p2, p3)):
        d[:, 192 * s : 192 * s + 192] = p[0:96, 576:768]


def settle_out_body(d0, d1, d2, d3, e1, e2, e3, m0, m1, m2, m3, w_out, tmp):
    k, h, f = place()
    for half, parts in ((h, (d0, d1, d2, d3)), (1 - h, (None, e1, e2, e3))):
        for j, d in enumerate(parts):
            for s in range(4):
                rows = rows_at(192 * (f ^ s) + 48 * chip(k, j) + 24 * half, 24, 8)
                if d is None:
                    piece = (m0, m1, m2, m3)[s][0:96, 576:768].astype(F32)
                else:
                    piece = d[:, 192 * s : 192 * s + 192].astype(F32)
                for t in range(4):
                    tmp[rows, 192 * t : 192 * t + 192] = piece[24 * t : 24 * t + 24, :]
    w_out[...] = tmp[...].astype(BF)


def settle_feed_body(p0, p1, p2, p3, e0, e1, e2, e3, w_up, w_down):
    k, h, f = place()
    for half, parts in ((h, (p0, p1, p2, p3)), (1 - h, (e0, e1, e2, e3))):
        lanes = pl.ds(pl.multiple_of(384 * half, 128), 384)
        for s, part in enumerate(parts):
            g = f ^ s
            w_up[rows_at(192 * g, 192, 16), lanes] = part[0:192, :]
            rows = rows_at(384 * half + 96 * g, 96, 16)
            w_down[rows, 0:384] = part[192:288, :]
            w_down[rows, 384:768] = part[288:384, :]


def attend_body(q, kv, mate, packed, att, lse):
    for i in range(3):
        lanes, vlanes = slice(64 * i, 64 * i + 64), slice(192 + 64 * i, 256 + 64 * i)
        sa = mm_nt(q[:, lanes], kv[:, lanes])
        sb = mm_nt(q[:, lanes], mate[:, lanes])
        top = jnp.maximum(jnp.max(sa, axis=1, keepdims=True), jnp.max(sb, axis=1, keepdims=True))
        ea = jnp.exp(sa - top)
        eb = jnp.exp(sb - top)
        total = jnp.sum(ea, axis=1, keepdims=True) + jnp.sum(eb, axis=1, keepdims=True)
        out = (mm(ea.astype(BF), kv[:, vlanes]) + mm(eb.astype(BF), mate[:, vlanes])) / total
        att[i] = out
        lse[i] = top + jnp.log(total)
        low = out.astype(BF)
        packed[:, lanes] = low[0:256, :]
        packed[:, vlanes] = low[256:512, :]


def norm_parts(v):
    centre = v - jnp.mean(v, axis=1, keepdims=True)
    inv = lax.rsqrt(jnp.mean(centre * centre, axis=1, keepdims=True) + 1e-05)
    return centre * inv, inv


def branch_body(a0, a1, a2, a3, x0, x1, x2, x3, w_out, vecs, low, first, hat, inv, att, xs):
    k, h, f = place()
    parts = (a0, a1, a2, a3)
    for m, x in enumerate((x0, x1, x2, x3)):
        xs[128 * m : 128 * m + 128, :] = x[...]
        for j in range(4):
            b = j ^ m
            rows, lanes = 128 * (b % 2), 192 * (b // 2)
            att[j, 128 * m : 128 * m + 128, :] = parts[j][rows : rows + 128, lanes : lanes + 192]
    acc = xs[...].astype(F32) + vecs[2:3, :]
    for j in range(4):
        acc = acc + mm(att[j], w_out[rows_at(192 * chip(k, j), 192, 16), :])
    n, r = norm_parts(acc)
    y = n * vecs[3:4, :] + vecs[4:5, :]
    low[...] = y.astype(BF)
    first[...] = y[0:128, :]
    hat[...] = n[0:128, :]
    inv[...] = r[0:128, :]


def feed_body(low, w_up, w_down, up, own, s1, s2, s3, act, slope):
    hid = mm(low[...], w_up[...]) + up[...]
    cdf = 0.5 * (1.0 + lax.erf(hid * (2.0**-0.5)))
    pdf = jnp.exp(hid * hid * -0.5) * ((2.0 * math.pi) ** -0.5)
    a = (hid * cdf).astype(BF)
    act[...] = a
    slope[...] = (cdf + hid * pdf).astype(BF)
    part = mm(a, w_down[...])
    for m, out in enumerate((own, s1, s2, s3)):
        out[...] = part[128 * m : 128 * m + 128, :].astype(out.dtype)


def second_body(own, r1, r2, r3, first, vecs, cot, out, grad, low, sums):
    v = own[...] + r1[...].astype(F32) + r2[...].astype(F32) + r3[...].astype(F32)
    n, inv = norm_parts(v + first[...] + vecs[5:6, :])
    out[...] = (n * vecs[6:7, :] + vecs[7:8, :]).astype(BF)
    dy = cot[...].astype(F32)
    g, lowered = norm_back(dy, n, inv, vecs[6:7, :])
    grad[...] = g
    low[...] = lowered
    sums[...] = jnp.zeros_like(sums)
    sums[0:1, :] = jnp.sum(dy * n, axis=0, keepdims=True)
    sums[1:2, :] = jnp.sum(dy, axis=0, keepdims=True)
    sums[2:3, :] = jnp.sum(lowered.astype(F32), axis=0, keepdims=True)


def norm_back(dy, n, inv, gain):
    d = dy * gain
    g = inv * (d - jnp.mean(d, axis=1, keepdims=True) - n * jnp.mean(d * n, axis=1, keepdims=True))
    return g, g.astype(BF)


def feed_back_body(
    d0, d1, d2, d3, w_up, w_down, slope, act, low, own, s1, s2, s3, keep, send, ds, dhid, full
):
    k, h, f = place()
    for m, d in enumerate((d0, d1, d2, d3)):
        ds[128 * m : 128 * m + 128, :] = d[...]
    dhid[...] = (mm_nt(ds[...], w_down[...]) * slope[...].astype(F32)).astype(BF)
    part = mm_nt(dhid[...], w_up[...])
    for m, out in enumerate((own, s1, s2, s3)):
        out[...] = part[128 * m : 128 * m + 128, :].astype(out.dtype)
    full[...] = mm_tn(act[...], ds[...])
    keep[0:384, :] = full[rows_at(384 * h, 384, 8), :]
    send[0:384, :] = full[rows_at(384 * (1 - h), 384, 8), :].astype(BF)
    full[...] = mm_tn(low[...], dhid[...])
    for kk in range(4):
        at = slice(384 + 96 * kk, 480 + 96 * kk)
        keep[at, :] = full[rows_at(192 * kk + 96 * h, 96, 8), :]
        send[at, :] = full[rows_at(192 * kk + 96 * (1 - h), 96, 8), :].astype(BF)
    total = jnp.sum(dhid[...].astype(F32), axis=0, keepdims=True)
    lo, hi = total[:, 0:384], total[:, 384:768]
    keep[768:784, :] = jnp.zeros((16, 768), F32)
    keep[768:769, 0:384] = jnp.where(h == 0, lo, hi)
    full[0:16, :] = jnp.zeros((16, 768), F32)
    full[0:1, 0:384] = jnp.where(h == 0, hi, lo)
    send[768:784, :] = full[0:16, :].astype(BF)


def first_back_body(own, r1, r2, r3, grad, hat, inv, vecs, w_out, out, low, t0, t1, t2, t3, sums):
    k, h, f = place()
    dy = own[...] + r1[...].astype(F32) + r2[...].astype(F32) + r3[...].astype(F32) + grad[...]
    n = hat[...]
    g, lowered = norm_back(dy, n, inv[...], vecs[3:4, :])
    out[...] = g
    low[...] = lowered
    for j, t in enumerate((t0, t1, t2, t3)):
        t[...] = mm_nt(lowered, w_out[rows_at(192 * chip(k, j), 192, 16), :]).astype(BF)
    sums[...] = jnp.zeros_like(sums)
    sums[0:1, :] = jnp.sum(dy * n, axis=0, keepdims=True)
    sums[1:2, :] = jnp.sum(dy, axis=0, keepdims=True)
    sums[2:3, :] = jnp.sum(lowered.astype(F32), axis=0, keepdims=True)


def attend_back_body(d0, d1, d2, d3, q, kv, mate, att, lse, gq, keep, send_k, send_v, dat):
    for m, d in enumerate((d0, d1, d2, d3)):
        dat[128 * m : 128 * m + 128, :] = d[...]
    for i in range(3):
        lanes, vlanes = slice(64 * i, 64 * i + 64), slice(192 + 64 * i, 256 + 64 * i)
        qi = q[:, lanes]
        do = dat[:, lanes]
        delta = jnp.sum(do.astype(F32) * att[i], axis=1, keepdims=True)
        total = lse[i]
        gqi = None
        for keys in (kv, mate):
            p = jnp.exp(mm_nt(qi, keys[:, lanes]) - total)
            ds = (p * (mm_nt(do, keys[:, vlanes]) - delta)).astype(BF)
            part = mm(ds, keys[:, lanes])
            gqi = part if gqi is None else gqi + part
            gk, gv = mm_tn(ds, qi), mm_tn(p.astype(BF), do)
            if keys is kv:
                keep[:, lanes] = gk
                keep[:, vlanes] = gv
            else:
                send_k[:, lanes] = gk.astype(BF)
                send_v[:, lanes] = gv.astype(BF)
        gq[:, lanes] = (gqi * 0.125).astype(BF)


def out_grad_body(packed, d0, d1, d2, d3, keep, send, full, att, ds):
    k, h, f = place()
    for m, d in enumerate((d0, d1, d2, d3)):
        ds[128 * m : 128 * m + 128, :] = d[...]
    att[0:256, :] = packed[:, 0:192]
    att[256:512, :] = packed[:, 192:384]
    full[...] = mm_tn(att[...], ds[...])
    keep[...] = full[rows_at(96 * h, 96, 8), :]
    send[...] = full[rows_at(96 * (1 - h), 96, 8), :].astype(BF)


def inner_weight_body(gq, gk, got_k, got_v, x0, x1, x2, x3, sums_a, sums_b, g, keep, send_a, send_b, full, cols, xs):
    k, h, f = place()
    g[:, 0:192] = gq[...]
    g[:, 192:384] = (gk[:, 0:192] + got_k[...].astype(F32)).astype(BF)
    g[:, 384:576] = (gk[:, 192:384] + got_v[...].astype(F32)).astype(BF)
    for m, x in enumerate((x0, x1, x2, x3)):
        xs[128 * m : 128 * m + 128, :] = x[...]
    cols[...] = jnp.zeros_like(cols)
    bias = jnp.sum(g[...].astype(F32), axis=0, keepdims=True)
    for kk in range(4):

        @pl.when(k == kk)
        def _():
            cols[64:65, 192 * kk : 192 * kk + 192] = bias[:, 0:192]
            cols[65:66, 192 * kk : 192 * kk + 192] = bias[:, 384:576]

    cols[66:69, :] = sums_b[0:3, :]
    cols[69:72, :] = sums_a[0:3, :]
    full[:, 0:576] = mm_tn(xs[...], g[...])
    lane = lax.broadcasted_iota(jnp.int32, (768, 128), 1)
    full[:, 512:640] = jnp.where(lane < 64, full[:, 512:640], jnp.transpose(cols[...]))
    for kk in range(4):
        at = slice(96 * kk, 96 * kk + 96)
        keep[at, :] = full[rows_at(192 * kk + 96 * h, 96, 8), :]
        out = (send_a, send_b)[kk // 2]
        out[96 * (kk % 2) : 96 * (kk % 2) + 96, :] = full[rows_at(192 * kk + 96 * (1 - h), 96, 8), :].astype(BF)


def inner_input_body(g, w, own, s1, s2, s3):
    part = mm_nt(g[...], w[...])
    for m, out in enumerate((own, s1, s2, s3)):
        out[...] = part[128 * m : 128 * m + 128, :].astype(out.dtype)


def input_sum_body(grad, own, r1, r2, r3, out):
    out[...] = grad[...] + own[...] + r1[...].astype(F32) + r2[...].astype(F32) + r3[...].astype(F32)


def stage_feed_body(keep, got, held, sent, tmp, one):
    k, h, f = place()
    tmp[...] = keep[...] + got[...].astype(F32)
    for g in range(4):
        one[g] = jnp.zeros((16, 768), F32)
        one[g, 0:1, 0:96] = tmp[768:769, 96 * g : 96 * g + 96]
    for s in range(4):
        out, g = (held, sent)[s % 2], f ^ s
        v = [tmp[rows_at(96 * g, 96, 8), :], one[g]] + [tmp[rows_at(384 + 96 * kk + 24 * g, 24, 8), :] for kk in range(4)]
        out[208 * (s // 2) : 208 * (s // 2) + 208, :] = jnp.concatenate(v, axis=0).astype(out.dtype)


def stage_q_body(keep, got_a, got_b, held, sent, tmp):
    k, h, f = place()
    tmp[0:192, :] = keep[0:192, :] + got_a[...].astype(F32)
    tmp[192:384, :] = keep[192:384, :] + got_b[...].astype(F32)
    for s in range(4):
        out = (held, sent)[s % 2]
        v = [tmp[rows_at(96 * kk + 24 * (f ^ s), 24, 8), :] for kk in range(4)]
        out[96 * (s // 2) : 96 * (s // 2) + 96, :] = jnp.concatenate(v, axis=0).astype(out.dtype)


def stage_out_body(keep, got, held, sent, tmp):
    k, h, f = place()
    tmp[...] = keep[...] + got[...].astype(F32)
    for half, out in enumerate((held, sent)):
        v = [tmp[rows_at(24 * (f ^ s), 24, 8), :] for s in (half, half + 2)]
        out[...] = jnp.concatenate(v, axis=0).astype(out.dtype)


def half_body(held, got, own, far):
    n = own.shape[0]
    own[...] = held[0:n, :] + got[0:n, :].astype(F32)
    far[...] = (held[n : 2 * n, :] + got[n : 2 * n, :].astype(F32)).astype(BF)


def half_out_body(held, got, own, far):
    v = held[...] + got[...].astype(F32)
    own[...] = v[0:24, :]
    far[...] = v[24:48, :].astype(BF)


def join_down_body(own, r, down, up):
    v = own[...] + r[...].astype(F32)
    down[...] = v[0:112, :].astype(BF)
    up[...] = v[112:208, :]


def turn_body(own, r, up, a0, a1, a2, a3, tmp):
    k, h, f = place()
    v = own[...] + r[...].astype(F32)
    u = up[...]
    for kk in range(4):
        tmp[kk, :, 0:768] = u[24 * kk : 24 * kk + 24, :]
        tmp[kk, :, 768:1408] = v[24 * kk : 24 * kk + 24, :]
    for j, out in enumerate((a0, a1, a2, a3)):
        out[...] = tmp[chip(k, j)].astype(out.dtype)


def finish_down_body(down, out, o1, w_down, w_out, bias_up):
    w_down[...] = down[0:96, :].astype(F32)
    bias_up[...] = down[96:112, :].astype(F32)[0:1, 0:96].reshape(96)
    w_out[...] = out[...] + o1[...].astype(F32)


def finish_body(own, r1, r2, r3, w_qk, w_v, w_up, *rest):
    vecs, tmp = rest[:8], rest[8]
    k, h, f = place()
    total = None
    for j, r in enumerate((own, r1, r2, r3)):
        v = r[...].astype(F32)
        tmp[chip(k, j)] = v
        part = v[:, 1280:1408]
        total = part if total is None else total + part
    for kk in range(4):
        v = tmp[kk]
        for half in range(2):
            for g in range(4):
                at = 768 * g + 192 * kk + 96 * half
                w_up[:, at : at + 96] = v[:, 384 * half + 96 * g : 384 * half + 96 * g + 96]
        w_qk[:, 192 * kk : 192 * kk + 192] = v[:, 768:960]
        w_qk[:, 768 + 192 * kk : 960 + 192 * kk] = v[:, 960:1152]
        w_v[:, 192 * kk : 192 * kk + 192] = v[:, 1152:1344]
    turned = jnp.transpose(jnp.concatenate([total, jnp.zeros((104, 128), F32)], axis=0))
    for i in range(8):
        vecs[i][...] = turned[64 + i : 65 + i, 0:24].reshape(24)


def swap(x):
    return lax.ppermute(x, "ctx", [(i, i ^ 1) for i in range(8)])


def to_chip(x, j):
    return lax.ppermute(x, "ctx", [(i, i ^ (2 * j)) for i in range(8)])


def to_plane(x, s):
    return lax.ppermute(x, "fsdp", [(i, i ^ s) for i in range(4)])


def send_plane(xs):
    return [to_chip(x, j) for j, x in enumerate(xs, 1)]


def send_back(xs):
    return [to_chip(x, 3 - j) for j, x in enumerate(xs[::-1])][::-1]


def gather_plane(x):
    return [x, *send_plane([x] * 3)]


def gather_back(x):
    return [x, *send_back([x] * 3)]


def relay_plane(x):
    a = to_chip(x, 1)
    return [x, a, to_chip(x, 2), to_chip(a, 2)]


def gather_z(x):
    return [x, to_plane(x, 1), to_plane(x, 2)]


def sum_z(body, mid, outs, args, name, scratch, gate=()):
    rows, lanes = outs
    held, sent = local_call(body, [((2 * rows, lanes), F32), ((2 * rows, lanes), BF)], args, "stage_" + name, scratch)
    own, far = local_call(mid, [((rows, lanes), F32), ((rows, lanes), BF)], [after(held, *gate), to_plane(sent, 1)], "half_" + name)
    return sent, far, own, to_plane(far, 2)


def after(value, *others):
    return lax.optimization_barrier((value, *others))[0]


def per_device_blocks(
    inputs, w_query_key, w_value, w_out, w_up, w_down, bias_query, bias_value, bias_out,
    gain_attn, shift_attn, bias_up, bias_down, gain_ffn, shift_ffn, cotangent,
):
    c = lax.axis_index("ctx")
    x0 = inputs.reshape(128, 768)
    cot = cotangent.reshape(128, 768)
    block, wide = ((128, 768), BF), ((128, 768), F32)
    vectors = [bias_query, bias_value, bias_out, gain_attn, shift_attn, bias_down, gain_ffn, shift_ffn, bias_up]

    own, other = local_call(
        pack_qkv, [((112, 768), BF)] * 2, [w_query_key, w_value, w_out] + vectors, "pack_qkv",
        [pltpu.VMEM((192, 1536), BF), pltpu.VMEM((192, 768), BF), pltpu.VMEM((192, 768), BF)]
        + [pltpu.VMEM((192,), BF)] * 8
        + [pltpu.VMEM((768,), BF), pltpu.VMEM((112, 768), F32), pltpu.VMEM((192, 768), F32), pltpu.SemaphoreType.DMA((12,))],
        raw=12,
    )
    pz = gather_z(own)[1:]
    pz.append(to_plane(pz[1], 1))
    xs = gather_plane(x0)
    part, mate_part = local_call(
        pack_feed, [((384, 384), BF)] * 2, [w_up, w_down, own], "pack_feed",
        [pltpu.VMEM((192, 3072), BF), pltpu.VMEM((192, 768), BF), pltpu.SemaphoreType.DMA((2,))],
        raw=2,
    )
    parts = gather_z(after(part, pz[1]))
    pm = [swap(after(after(p, part), *xs[1:])) for p in pz]
    q, kv, w_qkv, vecs, up = local_call(
        qkv_body,
        [((512, 192), BF), ((512, 384), BF), ((768, 576), BF), ((8, 768), F32), ((1, 768), F32)],
        xs + [own, other] + pz + pm, "qkv",
        [pltpu.VMEM((4, 16, 768), F32), pltpu.VMEM((8, 192), F32), pltpu.VMEM((8, 768), F32), pltpu.VMEM((512, 768), BF)],
    )
    kv = [kv, swap(kv)]
    (piece,) = local_call(gather_out_body, [((96, 768), BF)], [own] + pz, "gather_out")
    ds = relay_plane(piece)
    both = parts[2]
    packed, att, lse = local_call(
        attend_body, [((256, 384), BF), ((3, 512, 64), F32), ((3, 512, 1), F32)], [q] + kv, "attend"
    )
    both = after(both, packed)
    parts.append(to_plane(both, 1))
    atts = relay_plane(packed)
    full_out, = local_call(settle_out_body, [((768, 768), BF)], ds + [swap(d) for d in ds[1:]] + [other] + pm, 'settle_out', [pltpu.VMEM((768, 768), F32)])
    full_up, full_down = local_call(
        settle_feed_body, [((768, 768), BF)] * 2, parts + [mate_part] + [swap(p) for p in parts[1:]], "settle_feed"
    )
    low, first, hat, inv = local_call(
        branch_body, [((512, 768), BF), wide, wide, ((128, 1), F32)], atts + xs + [full_out, vecs], "branch",
        [pltpu.VMEM((4, 512, 192), BF), pltpu.VMEM((512, 768), BF)]
    )
    sec, s1, s2, s3, act, slope = local_call(
        feed_body, [wide, block, block, block, ((512, 768), BF), ((512, 768), BF)], [low, full_up, full_down, up], "feed",

    )
    out, grad_two, dsec, sums_two = local_call(
        second_body, [block, wide, block, ((8, 768), F32)], [sec] + send_plane([s1, s2, s3]) + [first, vecs, cot], "second", final=(0,)
    )
    dsecs = gather_back(dsec)
    gfo, s1, s2, s3, fkeep, fsend = local_call(
        feed_back_body, [wide, block, block, block, ((784, 768), F32), ((784, 768), BF)],
        dsecs + [full_up, full_down, slope, act, low], "feed_back",
        [pltpu.VMEM((512, 768), BF)] * 2 + [pltpu.VMEM((768, 768), F32)],
    )
    gfo = [gfo] + send_back([s1, s2, s3])
    fsent, ffar, fown, fgot = sum_z(
        stage_feed_body, half_body, (208, 768), [fkeep, swap(fsend)], "feed_grad",
        [pltpu.VMEM((784, 768), F32), pltpu.VMEM((4, 16, 768), F32)],
    )
    down, up_sum = local_call(join_down_body, [((112, 768), BF), ((96, 768), F32)], [fown, fgot], "join_down")
    down = lax.ppermute(down, ("ctx", "fsdp"), [(4 * i + z, 8 * z + i) for i in range(8) for z in range(4)])
    grad_one, dbr, t0, t1, t2, t3, sums_one = local_call(first_back_body, [wide, block] + [((128, 192), BF)] * 4 + [((8, 768), F32)], [after(gfo[0], fsent)] + gfo[1:] + [grad_two, hat, inv, vecs, full_out], 'first_back')
    dats = [t0] + send_plane([t1, t2, t3])
    gq, gkeep, gk_send, gv_send = local_call(attend_back_body, [((512, 192), BF), ((512, 384), F32), ((512, 192), BF), ((512, 192), BF)], dats + [after(q, ffar)] + kv + [att, lse], 'attend_back', [pltpu.VMEM((512, 192), BF)], mib=24)
    dbrs = relay_plane(after(dbr, gq))
    gk_got, gv_got = (swap(after(gk_send, ffar)), swap(gv_send))
    g, qkeep, qsend_a, qsend_b = local_call(inner_weight_body, [((512, 576), BF), ((384, 640), F32), ((192, 640), BF), ((192, 640), BF)], [gq, gkeep, gk_got, gv_got] + xs + [sums_two, sums_one], 'inner_weight', [pltpu.VMEM((768, 640), F32), pltpu.VMEM((128, 768), F32), pltpu.VMEM((512, 768), BF)])
    qsent, qfar_sent, qown, qfar = sum_z(stage_q_body, half_body, (96, 640), [qkeep, swap(qsend_a), swap(qsend_b)], 'q', [pltpu.VMEM((384, 640), F32)], [])
    gin, s1, s2, s3 = local_call(inner_input_body, [wide, block, block, block], [after(g, qsent), w_qkv], 'inner_input')
    gin = [gin] + send_plane([s1, s2, s3])
    okeep, osend = local_call(
        out_grad_body, [((96, 768), F32), ((96, 768), BF)], [packed] + dbrs, "out_grad",
        [pltpu.VMEM((192, 768), F32), pltpu.VMEM((512, 192), BF), pltpu.VMEM((512, 768), BF)],
    )
    _, _, oown, ofar = sum_z(stage_out_body, half_out_body, (24, 768), [after(okeep, qsent), swap(after(after(osend, qsend_a), qsent))], 'out', [pltpu.VMEM((96, 768), F32)], [] + [gin[1]])
    a0, a1, a2, a3 = local_call(turn_body, [((24, 1408), F32)] + [((24, 1408), BF)] * 3, [after(qown, down), qfar, up_sum], 'turn', scratch=[pltpu.VMEM((4, 24, 1408), F32)])
    aa = send_plane([a1, a2, a3])
    g_qk, g_v, g_up, *small = local_call(
        finish_body, [((24, 1536), F32), ((24, 768), F32), ((24, 3072), F32)] + [((24,), F32)] * 8, [a0] + aa, "finish",
        [pltpu.VMEM((4, 24, 1408), F32)], final=range(11),
    )
    g_down, g_out, g_bias_up = local_call(
        finish_down_body, [((96, 768), F32), ((24, 768), F32), ((96,), F32)], [down, oown, ofar], "finish_down",
        final=range(3),
    )
    grad_inputs, = local_call(input_sum_body, [wide], [grad_one] + gin, 'input_sum', final=(0,))
    return (
        out.reshape(1, 128, 768), grad_inputs.reshape(1, 128, 768), g_qk, g_v, g_out, g_up, g_down,
        small[0], small[1], small[4], small[2], small[3], g_bias_up, small[7], small[5], small[6],
    )


def solution(mesh):
    blocks = mesh.shape["ctx"] == 8 and mesh.shape["fsdp"] == 4
    return jax.shard_map(
        per_device_blocks if blocks else per_device,
        mesh=mesh,
        in_specs=(
            P("fsdp", "ctx", None),
            P("fsdp", None),
            P("fsdp", None),
            P("fsdp", None),
            P("fsdp", None),
            P("fsdp", None),
            P("fsdp"),
            P("fsdp"),
            P("fsdp"),
            P("fsdp"),
            P("fsdp"),
            P("fsdp"),
            P("fsdp"),
            P("fsdp"),
            P("fsdp"),
            P("fsdp", "ctx", None),
        ),
        out_specs=(
            P("fsdp", "ctx", None),
            P("fsdp", "ctx", None),
            P(("ctx", "fsdp"), None),
            P(("ctx", "fsdp"), None),
            P(("ctx", "fsdp"), None),
            P(("ctx", "fsdp"), None),
            P(("ctx", "fsdp"), None),
            P(("ctx", "fsdp")),
            P(("ctx", "fsdp")),
            P(("ctx", "fsdp")),
            P(("ctx", "fsdp")),
            P(("ctx", "fsdp")),
            P(("ctx", "fsdp")),
            P(("ctx", "fsdp")),
            P(("ctx", "fsdp")),
            P(("ctx", "fsdp")),
        ),
        check_vma=False,
    )
```

```python
import functools
import math

import jax
import jax.numpy as jnp
from jax import lax
from jax.experimental import pallas as pl
from jax.experimental.pallas import tpu as pltpu
from jax.sharding import PartitionSpec as P

HEADS = 12
HEAD = 64


def norm_apply(inputs, norm_gain, norm_shift):
    centre = inputs - jnp.mean(inputs, axis=-1, keepdims=True)
    spread = jnp.mean(centre * centre, axis=-1, keepdims=True)
    return centre * lax.rsqrt(spread + 1e-05) * norm_gain + norm_shift


def left_product(left, right):
    return lax.dot_general(
        left, right, (((0,), (0,)), ((), ())), preferred_element_type=jnp.float32
    )


def right_product(left, right):
    return lax.dot_general(
        left, right, (((1,), (1,)), ((), ())), preferred_element_type=jnp.float32
    )


def column_sums(matrix):
    return jnp.sum(matrix.astype(jnp.float32), axis=0)


def per_device(
    inputs,
    w_query_key,
    w_value,
    w_out,
    w_up,
    w_down,
    bias_query,
    bias_value,
    bias_out,
    gain_attn,
    shift_attn,
    bias_up,
    bias_down,
    gain_ffn,
    shift_ffn,
    cotangent,
):
    gathered = (
        lax.all_gather(w_query_key, "fsdp", axis=0, tiled=True),
        lax.all_gather(w_value, "fsdp", axis=0, tiled=True),
        lax.all_gather(w_out, "fsdp", axis=0, tiled=True),
        lax.all_gather(w_up, "fsdp", axis=0, tiled=True),
        lax.all_gather(w_down, "fsdp", axis=0, tiled=True),
        lax.all_gather(bias_query, "fsdp", axis=0, tiled=True),
        lax.all_gather(bias_value, "fsdp", axis=0, tiled=True),
        lax.all_gather(bias_out, "fsdp", axis=0, tiled=True),
        lax.all_gather(gain_attn, "fsdp", axis=0, tiled=True),
        lax.all_gather(shift_attn, "fsdp", axis=0, tiled=True),
        lax.all_gather(bias_up, "fsdp", axis=0, tiled=True),
        lax.all_gather(bias_down, "fsdp", axis=0, tiled=True),
        lax.all_gather(gain_ffn, "fsdp", axis=0, tiled=True),
        lax.all_gather(shift_ffn, "fsdp", axis=0, tiled=True),
    )
    full_qk, full_value, full_out, full_up, full_down = (
        gathered[0],
        gathered[1],
        gathered[2],
        gathered[3],
        gathered[4],
    )
    smalls = [piece.astype(jnp.float32) for piece in gathered[5:]]
    (
        vec_query,
        vec_value,
        vec_out,
        vec_gain_one,
        vec_shift_one,
        vec_up,
        vec_down,
        vec_gain_two,
        vec_shift_two,
    ) = smalls
    rows = inputs.shape[1]
    width = inputs.shape[2]
    heads = HEADS
    head = HEAD
    tokens = inputs.reshape(rows, width)
    tok_float = tokens.astype(jnp.float32)
    query_key = jnp.dot(tokens, full_qk, preferred_element_type=jnp.float32)
    queries = (query_key[:, :width] + vec_query).astype(jnp.bfloat16)
    keys = query_key[:, width:].astype(jnp.bfloat16)
    values = (jnp.dot(tokens, full_value, preferred_element_type=jnp.float32) + vec_value).astype(
        jnp.bfloat16
    )
    query_heads = queries.reshape(rows, heads, head)
    start_state = (
        jnp.full((heads, rows), -1e30, jnp.float32),
        jnp.zeros((heads, rows), jnp.float32),
        jnp.zeros((rows, heads, head), jnp.float32),
    )
    carry = start_state
    key_piece = lax.all_gather(keys, "ctx", axis=0, tiled=True)
    value_piece = lax.all_gather(values, "ctx", axis=0, tiled=True)
    count = key_piece.shape[0]
    block = math.gcd(count, 2048)
    key_split = key_piece.reshape(count // block, block, heads, head)
    value_split = value_piece.reshape(count // block, block, heads, head)

    def step_block(state, pair):
        running_max, running_sum, running_acc = state
        key_block, value_block = pair
        scores = (
            jnp.einsum("qhd,khd->hqk", query_heads, key_block, preferred_element_type=jnp.float32)
            * 0.125
        )
        new_max = jnp.maximum(running_max, jnp.max(scores, axis=-1))
        factor = jnp.exp(running_max - new_max)
        weights = jnp.exp(scores - new_max[:, :, None])
        running_sum = running_sum * factor + jnp.sum(weights, axis=-1)
        update = jnp.einsum(
            "hqk,khd->qhd",
            weights.astype(jnp.bfloat16),
            value_block,
            preferred_element_type=jnp.float32,
        )
        running_acc = running_acc * jnp.transpose(factor)[:, :, None] + update
        return ((new_max, running_sum, running_acc), None)

    carry, unused = lax.scan(step_block, carry, (key_split, value_split))
    final_max, final_sum, final_acc = carry
    attended_heads = final_acc / jnp.transpose(final_sum)[:, :, None]
    log_total = final_max + jnp.log(final_sum)
    attended_low = attended_heads.reshape(rows, width).astype(jnp.bfloat16)
    branch = jnp.dot(attended_low, full_out, preferred_element_type=jnp.float32) + vec_out
    first, norm_one_pull = jax.vjp(norm_apply, tok_float + branch, vec_gain_one, vec_shift_one)
    first_low = first.astype(jnp.bfloat16)
    hidden = jnp.dot(first_low, full_up, preferred_element_type=jnp.float32) + vec_up
    activ, gelu_pull = jax.vjp(functools.partial(jax.nn.gelu, approximate=False), hidden)
    activ_low = activ.astype(jnp.bfloat16)
    second = jnp.dot(activ_low, full_down, preferred_element_type=jnp.float32) + vec_down
    output, norm_two_pull = jax.vjp(norm_apply, first + second, vec_gain_two, vec_shift_two)
    grad_resid_two, grad_gain_ffn, grad_shift_ffn = norm_two_pull(
        cotangent.reshape(rows, width).astype(jnp.float32)
    )
    second_low = grad_resid_two.astype(jnp.bfloat16)
    grad_w_down = left_product(activ_low, second_low)
    grad_bias_down = column_sums(second_low)
    grad_activ = right_product(second_low, full_down)
    hidden_low = gelu_pull(grad_activ)[0].astype(jnp.bfloat16)
    grad_w_up = left_product(first_low, hidden_low)
    grad_bias_up = column_sums(hidden_low)
    grad_first = grad_resid_two + right_product(hidden_low, full_up)
    grad_resid_one, grad_gain_attn, grad_shift_attn = norm_one_pull(grad_first)
    branch_low = grad_resid_one.astype(jnp.bfloat16)
    grad_w_out = left_product(attended_low, branch_low)
    grad_bias_out = column_sums(branch_low)
    dout_low = right_product(branch_low, full_out).astype(jnp.bfloat16)
    dout_heads = dout_low.reshape(rows, heads, head)
    delta = jnp.einsum("qhd,qhd->hq", dout_heads.astype(jnp.float32), attended_heads)
    all_keys, all_values = (
        lax.all_gather(keys, "ctx", axis=0, tiled=True),
        lax.all_gather(values, "ctx", axis=0, tiled=True),
    )
    total = all_keys.shape[0]
    key_total = all_keys.shape[0]
    block = math.gcd(key_total, 2048)

    def back_block(grad_query, pair):
        key_block, value_block = pair
        scores = (
            jnp.einsum("qhd,khd->hqk", query_heads, key_block, preferred_element_type=jnp.float32)
            * 0.125
        )
        weights = jnp.exp(scores - log_total[:, :, None])
        weight_grad = jnp.einsum(
            "qhd,khd->hqk", dout_heads, value_block, preferred_element_type=jnp.float32
        )
        score_grad = (weights * (weight_grad - delta[:, :, None]) * 0.125).astype(jnp.bfloat16)
        grad_query = grad_query + jnp.einsum(
            "hqk,khd->qhd", score_grad, key_block, preferred_element_type=jnp.float32
        )
        value_grad = jnp.einsum(
            "hqk,qhd->khd",
            weights.astype(jnp.bfloat16),
            dout_heads,
            preferred_element_type=jnp.float32,
        )
        key_grad = jnp.einsum(
            "hqk,qhd->khd", score_grad, query_heads, preferred_element_type=jnp.float32
        )
        return (grad_query, (key_grad, value_grad))

    grad_query, terms = lax.scan(
        back_block,
        jnp.zeros((rows, heads, head), jnp.float32),
        (
            all_keys.reshape(key_total // block, block, heads, head),
            all_values.reshape(key_total // block, block, heads, head),
        ),
    )
    grad_keys, grad_values = (
        lax.psum_scatter(terms[0].reshape(total, width), "ctx", scatter_dimension=0, tiled=True),
        lax.psum_scatter(terms[1].reshape(total, width), "ctx", scatter_dimension=0, tiled=True),
    )
    grad_queries = grad_query.reshape(rows, width)
    query_low = grad_queries.astype(jnp.bfloat16)
    key_low = grad_keys.astype(jnp.bfloat16)
    value_low = grad_values.astype(jnp.bfloat16)
    query_key_low = jnp.concatenate([query_low, key_low], axis=1)
    grad_w_query_key = left_product(tokens, query_key_low)
    grad_w_value = left_product(tokens, value_low)
    grad_bias_query = column_sums(query_low)
    grad_bias_value = column_sums(value_low)
    grad_inputs = (
        grad_resid_one
        + right_product(query_key_low, full_qk)
        + right_product(value_low, full_value)
    )
    summed = (
        lax.psum_scatter(grad_w_query_key, ("ctx", "fsdp"), scatter_dimension=0, tiled=True),
        lax.psum_scatter(grad_w_value, ("ctx", "fsdp"), scatter_dimension=0, tiled=True),
        lax.psum_scatter(grad_w_out, ("ctx", "fsdp"), scatter_dimension=0, tiled=True),
        lax.psum_scatter(grad_w_up, ("ctx", "fsdp"), scatter_dimension=0, tiled=True),
        lax.psum_scatter(grad_w_down, ("ctx", "fsdp"), scatter_dimension=0, tiled=True),
        lax.psum_scatter(grad_bias_query, ("ctx", "fsdp"), scatter_dimension=0, tiled=True),
        lax.psum_scatter(grad_bias_value, ("ctx", "fsdp"), scatter_dimension=0, tiled=True),
        lax.psum_scatter(grad_bias_out, ("ctx", "fsdp"), scatter_dimension=0, tiled=True),
        lax.psum_scatter(grad_gain_attn, ("ctx", "fsdp"), scatter_dimension=0, tiled=True),
        lax.psum_scatter(grad_shift_attn, ("ctx", "fsdp"), scatter_dimension=0, tiled=True),
        lax.psum_scatter(grad_bias_up, ("ctx", "fsdp"), scatter_dimension=0, tiled=True),
        lax.psum_scatter(grad_bias_down, ("ctx", "fsdp"), scatter_dimension=0, tiled=True),
        lax.psum_scatter(grad_gain_ffn, ("ctx", "fsdp"), scatter_dimension=0, tiled=True),
        lax.psum_scatter(grad_shift_ffn, ("ctx", "fsdp"), scatter_dimension=0, tiled=True),
    )
    return (
        output.astype(jnp.bfloat16).reshape(1, rows, width),
        grad_inputs.reshape(1, rows, width),
        summed[0],
        summed[1],
        summed[2],
        summed[3],
        summed[4],
        summed[5],
        summed[6],
        summed[7],
        summed[8],
        summed[9],
        summed[10],
        summed[11],
        summed[12],
        summed[13],
    )


BF = jnp.bfloat16
F32 = jnp.float32


COST = dict(attend=20, branch=20, feed=2, second=7.5, feed_back=3, first_back=9, attend_back=16, inner_weight=2.2, inner_input=7, feed_grad=5, turn=5, join_down=9, out_grad=2.0, input_sum=1, gather_out=8, pack_feed=9, half_feed_grad=8.5, settle_feed=8, finish_down=9, half_q=1)


def local_call(body, outs, args, name, scratch=(), mib=16, final=(), raw=0):
    vmem, hbm = pl.BlockSpec(memory_space=pltpu.VMEM), pl.BlockSpec(memory_space=pltpu.HBM)
    held = [pltpu.with_memory_space_constraint(a, pltpu.HBM if i < raw else pltpu.VMEM) for i, a in enumerate(args)]
    return pl.pallas_call(
        body,
        out_shape=tuple(jax.ShapeDtypeStruct(s, d) if i in final else pltpu.VMEM(s, d) for i, (s, d) in enumerate(outs)),
        in_specs=[hbm] * raw + [vmem] * (len(args) - raw),
        out_specs=tuple(vmem for _ in outs),
        scratch_shapes=list(scratch),
        compiler_params=pltpu.CompilerParams(vmem_limit_bytes=mib * 1024 * 1024),
        cost_estimate=pl.CostEstimate(flops=int(COST.get(name, 0) * 524e6), bytes_accessed=0, transcendentals=0),
        name=name,
    )(*held)


def fetch(sems, *pairs):
    copies = [pltpu.make_async_copy(src, dst, sems.at[i]) for i, (src, dst) in enumerate(pairs)]
    for copy in copies:
        copy.start()
    for copy in copies:
        copy.wait()


def place():
    c = lax.axis_index("ctx")
    return c // 2, c % 2, lax.axis_index("fsdp")


def chip(k, j):
    return k ^ j


def mm(a, b):
    return jnp.dot(a, b, preferred_element_type=F32)


def mm_nt(a, b):
    return lax.dot_general(a, b, (((1,), (1,)), ((), ())), preferred_element_type=F32)


def mm_tn(a, b):
    return lax.dot_general(a, b, (((0,), (0,)), ((), ())), preferred_element_type=F32)


def rows_at(start, size, step):
    return pl.ds(pl.multiple_of(start, step), size)


def pack_qkv(x_hbm, w_qk_hbm, w_v_hbm, w_out_hbm, *rest):
    raw, (own, other, x, w_qk, w_v, w_out), vecs, (tmp, wide, sems) = rest[:9], rest[9:15], rest[15:24], rest[24:]
    k, h, f = place()
    fetch(sems, (x_hbm, x), (w_qk_hbm, w_qk), (w_v_hbm, w_v), (w_out_hbm, w_out), *zip(raw, vecs))
    tmp[...] = jnp.zeros_like(tmp)
    for i in range(8):
        at = slice(192 * (i % 4), 192 * (i % 4) + 192)
        tmp[96 + i // 4 : 97 + i // 4, at] = vecs[i][...].astype(F32).reshape(1, 192)
    tmp[98:99, :] = vecs[8][...].astype(F32).reshape(1, 768)
    wide[...] = w_out[...].astype(F32)
    for out, half in ((own, h), (other, 1 - h)):
        rows = rows_at(half * 96, 96, 16)
        for t in range(4):
            tmp[24 * t : 24 * t + 24, 576:768] = wide[rows_at(48 * k + 24 * half, 24, 8), 192 * t : 192 * t + 192]
        out[...] = tmp[...].astype(BF)
        for kk in range(4):

            @pl.when(k == kk)
            def _():
                out[0:96, 0:192] = w_qk[rows, 192 * kk : 192 * kk + 192]
                out[0:96, 192:384] = w_qk[rows, 768 + 192 * kk : 960 + 192 * kk]
                out[0:96, 384:576] = w_v[rows, 192 * kk : 192 * kk + 192]


def pack_feed(w_up_hbm, w_down_hbm, token, own, other, w_up, w_down, sems):
    k, h, f = place()
    fetch(sems, (w_up_hbm, w_up), (w_down_hbm.at[rows_at(192 * k, 192, 16), :], w_down))
    for kk in range(4):
        for half in range(2):

            @pl.when(k == kk)
            def _():
                for which, out in enumerate((own, other)):

                    @pl.when(h == (half + which) % 2)
                    def _():
                        for g in range(4):
                            at = 768 * g + 192 * kk + 96 * half
                            out[0:192, 96 * g : 96 * g + 96] = w_up[:, at : at + 96]
                        out[192:288, :] = w_down[96 * half : 96 * half + 96, 0:384]
                        out[288:384, :] = w_down[96 * half : 96 * half + 96, 384:768]


def qkv_body(x0, x1, x2, x3, own, other, p1, p2, p3, m1, m2, m3, q, kv, w, vecs, up, tmp, vec, row, xs):
    k, h, f = place()
    for s, (mine, mate) in enumerate(((own, other), (p1, m1), (p2, m2), (p3, m3))):
        g = f ^ s
        w[rows_at(192 * g + 96 * h, 96, 16), :] = mine[0:96, 0:576]
        w[rows_at(192 * g + 96 * (1 - h), 96, 16), :] = mate[0:96, 0:576]
        tmp[g] = mine[96:112, :].astype(F32)
    for g in range(4):
        for i in range(8):
            at = 192 * (i % 4)
            vecs[i : i + 1, 192 * g : 192 * g + 192] = tmp[g, i // 4 : i // 4 + 1, at : at + 192]
    for kk in range(4):

        @pl.when(k == kk)
        def _():
            for half in range(2):
                for g in range(4):
                    at = 192 * kk + 96 * half
                    row[0:1, 384 * half + 96 * g : 384 * half + 96 * g + 96] = tmp[g, 2:3, at : at + 96]

    up[...] = row[0:1, :]
    for i in range(2):
        vec[i : i + 1, :] = tmp[k, 0:1, 192 * i : 192 * i + 192]
    for j, x in enumerate((x0, x1, x2, x3)):
        xs[128 * j : 128 * j + 128, :] = x[...]
    r = mm(xs[...], w[...])
    q[...] = ((r[:, 0:192] + vec[0:1, :]) * 0.125).astype(BF)
    kv[:, 0:192] = r[:, 192:384].astype(BF)
    kv[:, 192:384] = (r[:, 384:576] + vec[1:2, :]).astype(BF)


def gather_out_body(p0, p1, p2, p3, d):
    for s, p in enumerate((p0, p1, p2, p3)):
        d[:, 192 * s : 192 * s + 192] = p[0:96, 576:768]


def settle_out_body(d0, d1, d2, d3, e1, e2, e3, m0, m1, m2, m3, w_out, tmp):
    k, h, f = place()
    for half, parts in ((h, (d0, d1, d2, d3)), (1 - h, (None, e1, e2, e3))):
        for j, d in enumerate(parts):
            for s in range(4):
                rows = rows_at(192 * (f ^ s) + 48 * chip(k, j) + 24 * half, 24, 8)
                if d is None:
                    piece = (m0, m1, m2, m3)[s][0:96, 576:768].astype(F32)
                else:
                    piece = d[:, 192 * s : 192 * s + 192].astype(F32)
                for t in range(4):
                    tmp[rows, 192 * t : 192 * t + 192] = piece[24 * t : 24 * t + 24, :]
    w_out[...] = tmp[...].astype(BF)


def settle_feed_body(p0, p1, p2, p3, e0, e1, e2, e3, w_up, w_down):
    k, h, f = place()
    for half, parts in ((h, (p0, p1, p2, p3)), (1 - h, (e0, e1, e2, e3))):
        lanes = pl.ds(pl.multiple_of(384 * half, 128), 384)
        for s, part in enumerate(parts):
            g = f ^ s
            w_up[rows_at(192 * g, 192, 16), lanes] = part[0:192, :]
            rows = rows_at(384 * half + 96 * g, 96, 16)
            w_down[rows, 0:384] = part[192:288, :]
            w_down[rows, 384:768] = part[288:384, :]


def attend_body(q, kv, mate, packed, att, lse):
    for i in range(3):
        lanes, vlanes = slice(64 * i, 64 * i + 64), slice(192 + 64 * i, 256 + 64 * i)
        sa = mm_nt(q[:, lanes], kv[:, lanes])
        sb = mm_nt(q[:, lanes], mate[:, lanes])
        top = jnp.maximum(jnp.max(sa, axis=1, keepdims=True), jnp.max(sb, axis=1, keepdims=True))
        ea = jnp.exp(sa - top)
        eb = jnp.exp(sb - top)
        total = jnp.sum(ea, axis=1, keepdims=True) + jnp.sum(eb, axis=1, keepdims=True)
        out = (mm(ea.astype(BF), kv[:, vlanes]) + mm(eb.astype(BF), mate[:, vlanes])) / total
        att[i] = out
        lse[i] = top + jnp.log(total)
        low = out.astype(BF)
        packed[:, lanes] = low[0:256, :]
        packed[:, vlanes] = low[256:512, :]


def norm_parts(v):
    centre = v - jnp.mean(v, axis=1, keepdims=True)
    inv = lax.rsqrt(jnp.mean(centre * centre, axis=1, keepdims=True) + 1e-05)
    return centre * inv, inv


def branch_body(a0, a1, a2, a3, x0, x1, x2, x3, w_out, vecs, low, first, hat, inv, att, xs):
    k, h, f = place()
    parts = (a0, a1, a2, a3)
    for m, x in enumerate((x0, x1, x2, x3)):
        xs[128 * m : 128 * m + 128, :] = x[...]
        for j in range(4):
            b = j ^ m
            rows, lanes = 128 * (b % 2), 192 * (b // 2)
            att[j, 128 * m : 128 * m + 128, :] = parts[j][rows : rows + 128, lanes : lanes + 192]
    acc = xs[...].astype(F32) + vecs[2:3, :]
    for j in range(4):
        acc = acc + mm(att[j], w_out[rows_at(192 * chip(k, j), 192, 16), :])
    n, r = norm_parts(acc)
    y = n * vecs[3:4, :] + vecs[4:5, :]
    low[...] = y.astype(BF)
    first[...] = y[0:128, :]
    hat[...] = n[0:128, :]
    inv[...] = r[0:128, :]


def feed_body(low, w_up, w_down, up, own, s1, s2, s3, act, slope):
    hid = mm(low[...], w_up[...]) + up[...]
    cdf = 0.5 * (1.0 + lax.erf(hid * (2.0**-0.5)))
    pdf = jnp.exp(hid * hid * -0.5) * ((2.0 * math.pi) ** -0.5)
    a = (hid * cdf).astype(BF)
    act[...] = a
    slope[...] = (cdf + hid * pdf).astype(BF)
    part = mm(a, w_down[...])
    for m, out in enumerate((own, s1, s2, s3)):
        out[...] = part[128 * m : 128 * m + 128, :].astype(out.dtype)


def second_body(cot_hbm, own, r1, r2, r3, first, vecs, out, grad, low, sums, cot, sems):
    copy = pltpu.make_async_copy(cot_hbm, cot, sems.at[0])
    copy.start()
    v = own[...] + r1[...].astype(F32) + r2[...].astype(F32) + r3[...].astype(F32)
    n, inv = norm_parts(v + first[...] + vecs[5:6, :])
    out[...] = (n * vecs[6:7, :] + vecs[7:8, :]).astype(BF)
    copy.wait()
    dy = cot[...].astype(F32)
    g, lowered = norm_back(dy, n, inv, vecs[6:7, :])
    grad[...] = g
    low[...] = lowered
    sums[...] = jnp.zeros_like(sums)
    sums[0:1, :] = jnp.sum(dy * n, axis=0, keepdims=True)
    sums[1:2, :] = jnp.sum(dy, axis=0, keepdims=True)
    sums[2:3, :] = jnp.sum(lowered.astype(F32), axis=0, keepdims=True)


def norm_back(dy, n, inv, gain):
    d = dy * gain
    g = inv * (d - jnp.mean(d, axis=1, keepdims=True) - n * jnp.mean(d * n, axis=1, keepdims=True))
    return g, g.astype(BF)


def feed_back_body(d0, d1, d2, d3, w_up, w_down, slope, own, s1, s2, s3, dhid, ds):
    for m, d in enumerate((d0, d1, d2, d3)):
        ds[128 * m : 128 * m + 128, :] = d[...]
    dh = (mm_nt(ds[...], w_down[...]) * slope[...].astype(F32)).astype(BF)
    dhid[...] = dh
    part = mm_nt(dh, w_up[...])
    for m, out in enumerate((own, s1, s2, s3)):
        out[...] = part[128 * m : 128 * m + 128, :].astype(out.dtype)


def feed_grad_body(act, low, d0, d1, d2, d3, dhid, keep, send_a, send_b, send_c, send_d, full, ds):
    k, h, f = place()
    for m, d in enumerate((d0, d1, d2, d3)):
        ds[128 * m : 128 * m + 128, :] = d[...]
    full[...] = mm_tn(act[...], ds[...])
    keep[0:384, :] = full[rows_at(384 * h, 384, 8), :]
    send_a[...] = full[rows_at(384 * (1 - h), 192, 8), :].astype(BF)
    send_b[...] = full[rows_at(384 * (1 - h) + 192, 192, 8), :].astype(BF)
    full[...] = mm_tn(low[...], dhid[...])
    for kk in range(4):
        keep[384 + 96 * kk : 480 + 96 * kk, :] = full[rows_at(192 * kk + 96 * h, 96, 8), :]
        out = (send_c, send_d)[kk // 2]
        out[96 * (kk % 2) : 96 * (kk % 2) + 96, :] = full[rows_at(192 * kk + 96 * (1 - h), 96, 8), :].astype(BF)
    total = jnp.sum(dhid[...].astype(F32), axis=0, keepdims=True)
    lo, hi = total[:, 0:384], total[:, 384:768]
    keep[768:784, :] = jnp.zeros((16, 768), F32)
    keep[768:769, 0:384] = jnp.where(h == 0, lo, hi)
    full[0:16, :] = jnp.zeros((16, 768), F32)
    full[0:1, 0:384] = jnp.where(h == 0, hi, lo)
    send_d[192:208, :] = full[0:16, :].astype(BF)


def first_back_body(own, r1, r2, r3, grad, hat, inv, vecs, w_out, out, low, t0, t1, t2, t3, sums):
    k, h, f = place()
    dy = own[...] + r1[...].astype(F32) + r2[...].astype(F32) + r3[...].astype(F32) + grad[...]
    n = hat[...]
    g, lowered = norm_back(dy, n, inv[...], vecs[3:4, :])
    out[...] = g
    low[...] = lowered
    for j, t in enumerate((t0, t1, t2, t3)):
        t[...] = mm_nt(lowered, w_out[rows_at(192 * chip(k, j), 192, 16), :]).astype(BF)
    sums[...] = jnp.zeros_like(sums)
    sums[0:1, :] = jnp.sum(dy * n, axis=0, keepdims=True)
    sums[1:2, :] = jnp.sum(dy, axis=0, keepdims=True)
    sums[2:3, :] = jnp.sum(lowered.astype(F32), axis=0, keepdims=True)


def attend_back_body(d0, d1, d2, d3, q, kv, mate, att, lse, gq, keep, send_k, send_v, dat):
    for m, d in enumerate((d0, d1, d2, d3)):
        dat[128 * m : 128 * m + 128, :] = d[...]
    for i in range(3):
        lanes, vlanes = slice(64 * i, 64 * i + 64), slice(192 + 64 * i, 256 + 64 * i)
        qi = q[:, lanes]
        do = dat[:, lanes]
        delta = jnp.sum(do.astype(F32) * att[i], axis=1, keepdims=True)
        total = lse[i]
        gqi = None
        for keys in (kv, mate):
            p = jnp.exp(mm_nt(qi, keys[:, lanes]) - total)
            ds = (p * (mm_nt(do, keys[:, vlanes]) - delta)).astype(BF)
            part = mm(ds, keys[:, lanes])
            gqi = part if gqi is None else gqi + part
            gk, gv = mm_tn(ds, qi), mm_tn(p.astype(BF), do)
            if keys is kv:
                keep[:, lanes] = gk
                keep[:, vlanes] = gv
            else:
                send_k[:, lanes] = gk.astype(BF)
                send_v[:, lanes] = gv.astype(BF)
        gq[:, lanes] = (gqi * 0.125).astype(BF)


def out_grad_body(packed, d0, d1, d2, d3, keep, send, full, att, ds):
    k, h, f = place()
    for m, d in enumerate((d0, d1, d2, d3)):
        ds[128 * m : 128 * m + 128, :] = d[0:128, :]
    att[0:256, :] = packed[:, 0:192]
    att[256:512, :] = packed[:, 192:384]
    full[...] = mm_tn(att[...], ds[...])
    keep[...] = full[rows_at(96 * h, 96, 8), :]
    send[...] = full[rows_at(96 * (1 - h), 96, 8), :].astype(BF)


def inner_weight_body(gq, gk, got_k, got_v, x0, x1, x2, x3, sums_a, sums_b, g, keep, send_a, send_b, full, cols, xs):
    k, h, f = place()
    g[:, 0:192] = gq[...]
    g[:, 192:384] = (gk[:, 0:192] + got_k[...].astype(F32)).astype(BF)
    g[:, 384:576] = (gk[:, 192:384] + got_v[...].astype(F32)).astype(BF)
    for m, x in enumerate((x0, x1, x2, x3)):
        xs[128 * m : 128 * m + 128, :] = x[...]
    cols[...] = jnp.zeros_like(cols)
    bias = jnp.sum(g[...].astype(F32), axis=0, keepdims=True)
    for kk in range(4):

        @pl.when(k == kk)
        def _():
            cols[64:65, 192 * kk : 192 * kk + 192] = bias[:, 0:192]
            cols[65:66, 192 * kk : 192 * kk + 192] = bias[:, 384:576]

    cols[66:69, :] = sums_b[0:3, :]
    cols[69:72, :] = sums_a[0:3, :]
    full[:, 0:576] = mm_tn(xs[...], g[...])
    lane = lax.broadcasted_iota(jnp.int32, (768, 128), 1)
    full[:, 512:640] = jnp.where(lane < 64, full[:, 512:640], jnp.transpose(cols[...]))
    for kk in range(4):
        at = slice(96 * kk, 96 * kk + 96)
        keep[at, :] = full[rows_at(192 * kk + 96 * h, 96, 8), :]
        out = (send_a, send_b)[kk // 2]
        out[96 * (kk % 2) : 96 * (kk % 2) + 96, :] = full[rows_at(192 * kk + 96 * (1 - h), 96, 8), :].astype(BF)


def inner_input_body(g, w, own, s1, s2, s3):
    part = mm_nt(g[...], w[...])
    for m, out in enumerate((own, s1, s2, s3)):
        out[...] = part[128 * m : 128 * m + 128, :].astype(out.dtype)


def input_sum_body(grad, own, r1, r2, r3, out):
    n = r1.shape[0]
    total = grad[...] + own[...]
    for r in (r1, r2, r3):
        total = total + r[n - 128 : n, :].astype(F32)
    out[...] = total


def stage_feed_body(keep, got_a, got_b, got_c, got_d, held, sent, tmp, one):
    k, h, f = place()
    for at, n, got in ((0, 192, got_a), (192, 192, got_b), (384, 192, got_c), (576, 208, got_d)):
        tmp[at : at + n, :] = keep[at : at + n, :] + got[...].astype(F32)
    for g in range(4):
        one[g] = jnp.zeros((16, 768), F32)
        one[g, 0:1, 0:96] = tmp[768:769, 96 * g : 96 * g + 96]
    for s in range(4):
        out, g = (held, sent)[s % 2], f ^ s
        v = [tmp[rows_at(96 * g, 96, 8), :], one[g]] + [tmp[rows_at(384 + 96 * kk + 24 * g, 24, 8), :] for kk in range(4)]
        out[208 * (s // 2) : 208 * (s // 2) + 208, :] = jnp.concatenate(v, axis=0).astype(out.dtype)


def stage_q_body(keep, got_a, got_b, held, sent, tmp):
    k, h, f = place()
    tmp[0:192, :] = keep[0:192, :] + got_a[...].astype(F32)
    tmp[192:384, :] = keep[192:384, :] + got_b[...].astype(F32)
    for s in range(4):
        out = (held, sent)[s % 2]
        v = [tmp[rows_at(96 * kk + 24 * (f ^ s), 24, 8), :] for kk in range(4)]
        out[96 * (s // 2) : 96 * (s // 2) + 96, :] = jnp.concatenate(v, axis=0).astype(out.dtype)


def stage_out_body(keep, got, held, sent, tmp):
    k, h, f = place()
    tmp[...] = keep[...] + got[...].astype(F32)
    for half, out in enumerate((held, sent)):
        v = [tmp[rows_at(24 * (f ^ s), 24, 8), :] for s in (half, half + 2)]
        out[...] = jnp.concatenate(v, axis=0).astype(out.dtype)


def half_body(held, got, own, far):
    n = own.shape[0]
    own[...] = held[0:n, :] + got[0:n, :].astype(F32)
    far[...] = (held[n : 2 * n, :] + got[n : 2 * n, :].astype(F32)).astype(BF)


def half_out_body(held, got, own, far):
    v = held[...] + got[...].astype(F32)
    own[...] = v[0:24, :]
    far[...] = v[24:48, :].astype(BF)


def join_down_body(own, r, down, up):
    v = own[...] + r[...].astype(F32)
    down[...] = v[0:112, :].astype(BF)
    up[...] = v[112:208, :]


def turn_body(own, r, up, a0, a1, a2, a3, tmp):
    k, h, f = place()
    v = own[...] + r[...].astype(F32)
    u = up[...]
    for kk in range(4):
        tmp[kk, :, 0:768] = u[24 * kk : 24 * kk + 24, :]
        tmp[kk, :, 768:1408] = v[24 * kk : 24 * kk + 24, :]
    for j, out in enumerate((a0, a1, a2, a3)):
        out[...] = tmp[chip(k, j)].astype(out.dtype)


def finish_down_body(down, out, o1, w_down, w_out, bias_up):
    w_down[...] = down[0:96, :].astype(F32)
    bias_up[...] = down[96:112, :].astype(F32)[0:1, 0:96].reshape(96)
    w_out[...] = out[...] + o1[...].astype(F32)


def finish_body(own, r1, r2, r3, w_qk, w_v, w_up, *rest):
    vecs, tmp = rest[:8], rest[8]
    k, h, f = place()
    total = None
    for j, r in enumerate((own, r1, r2, r3)):
        v = r[...].astype(F32)
        tmp[chip(k, j)] = v
        part = v[:, 1280:1408]
        total = part if total is None else total + part
    for kk in range(4):
        v = tmp[kk]
        for half in range(2):
            for g in range(4):
                at = 768 * g + 192 * kk + 96 * half
                w_up[:, at : at + 96] = v[:, 384 * half + 96 * g : 384 * half + 96 * g + 96]
        w_qk[:, 192 * kk : 192 * kk + 192] = v[:, 768:960]
        w_qk[:, 768 + 192 * kk : 960 + 192 * kk] = v[:, 960:1152]
        w_v[:, 192 * kk : 192 * kk + 192] = v[:, 1152:1344]
    turned = jnp.transpose(jnp.concatenate([total, jnp.zeros((104, 128), F32)], axis=0))
    for i in range(8):
        vecs[i][...] = turned[64 + i : 65 + i, 0:24].reshape(24)


def swap(x):
    return lax.ppermute(x, "ctx", [(i, i ^ 1) for i in range(8)])


def to_chip(x, j):
    return lax.ppermute(x, "ctx", [(i, i ^ (2 * j)) for i in range(8)])


def to_plane(x, s):
    return lax.ppermute(x, "fsdp", [(i, i ^ s) for i in range(4)])


def send_plane(xs):
    return [to_chip(x, j) for j, x in enumerate(xs, 1)]


def send_back(xs):
    return [to_chip(x, 3 - j) for j, x in enumerate(xs[::-1])][::-1]


def gather_plane(x):
    return [x, *send_plane([x] * 3)]


def gather_back(x):
    return [x, *send_back([x] * 3)]


def relay_plane(x):
    a = to_chip(x, 1)
    return [x, a, to_chip(x, 2), to_chip(a, 2)]


def gather_z(x):
    return [x, to_plane(x, 1), to_plane(x, 2)]


def sum_z(body, mid, outs, args, name, scratch, gate=()):
    rows, lanes = outs
    held, sent = local_call(body, [((2 * rows, lanes), F32), ((2 * rows, lanes), BF)], args, "stage_" + name, scratch)
    own, far = local_call(mid, [((rows, lanes), F32), ((rows, lanes), BF)], [after(held, *gate), to_plane(sent, 1)], "half_" + name)
    return sent, far, own, to_plane(far, 2)


def after(value, *others):
    return lax.optimization_barrier((value, *others))[0]


def per_device_blocks(
    inputs, w_query_key, w_value, w_out, w_up, w_down, bias_query, bias_value, bias_out,
    gain_attn, shift_attn, bias_up, bias_down, gain_ffn, shift_ffn, cotangent,
):
    c = lax.axis_index("ctx")
    cot = cotangent.reshape(128, 768)
    block, wide = ((128, 768), BF), ((128, 768), F32)
    vectors = [bias_query, bias_value, bias_out, gain_attn, shift_attn, bias_down, gain_ffn, shift_ffn, bias_up]

    own, other, x0 = local_call(
        pack_qkv, [((112, 768), BF)] * 2 + [block], [inputs.reshape(128, 768), w_query_key, w_value, w_out] + vectors, "pack_qkv",
        [pltpu.VMEM((192, 1536), BF), pltpu.VMEM((192, 768), BF), pltpu.VMEM((192, 768), BF)]
        + [pltpu.VMEM((192,), BF)] * 8
        + [pltpu.VMEM((768,), BF), pltpu.VMEM((112, 768), F32), pltpu.VMEM((192, 768), F32), pltpu.SemaphoreType.DMA((13,))],
        raw=13,
    )
    pz_far = to_plane(own, 2)
    pz_near = to_plane(own, 1)
    part, mate_part = local_call(
        pack_feed, [((384, 384), BF)] * 2, [w_up, w_down, own], "pack_feed",
        [pltpu.VMEM((192, 3072), BF), pltpu.VMEM((192, 768), BF), pltpu.SemaphoreType.DMA((2,))],
        raw=2,
    )
    pz = [pz_near, pz_far, to_plane(after(pz_far, part), 1)]
    xs = gather_back(x0)
    parts = gather_z(after(part, pz[1]))
    pm = [swap(after(p, *xs[1:])) for p in pz]
    q, kv, w_qkv, vecs, up = local_call(
        qkv_body,
        [((512, 192), BF), ((512, 384), BF), ((768, 576), BF), ((8, 768), F32), ((1, 768), F32)],
        xs + [own, other] + pz + pm, "qkv",
        [pltpu.VMEM((4, 16, 768), F32), pltpu.VMEM((8, 192), F32), pltpu.VMEM((8, 768), F32), pltpu.VMEM((512, 768), BF)],
    )
    kv = [kv, swap(kv)]
    (piece,) = local_call(gather_out_body, [((96, 768), BF)], [own] + pz, "gather_out")
    ds = relay_plane(after(piece, q))
    both = parts[2]
    packed, att, lse = local_call(
        attend_body, [((256, 384), BF), ((3, 512, 64), F32), ((3, 512, 1), F32)], [q] + kv, "attend"
    )
    both = after(both, packed)
    parts.append(to_plane(both, 1))
    atts = relay_plane(packed)
    full_out, = local_call(settle_out_body, [((768, 768), BF)], ds + [swap(d) for d in ds[1:]] + [other] + pm, 'settle_out', [pltpu.VMEM((768, 768), F32)])
    full_up, full_down = local_call(
        settle_feed_body, [((768, 768), BF)] * 2, parts + [mate_part] + [swap(p) for p in parts[1:]], "settle_feed"
    )
    low, first, hat, inv = local_call(
        branch_body, [((512, 768), BF), wide, wide, ((128, 1), F32)], atts + xs + [full_out, vecs], "branch",
        [pltpu.VMEM((4, 512, 192), BF), pltpu.VMEM((512, 768), BF)]
    )
    sec, s1, s2, s3, act, slope = local_call(
        feed_body, [wide, block, block, block, ((512, 768), BF), ((512, 768), BF)], [low, full_up, full_down, up], "feed",

    )
    out, grad_two, dsec, sums_two = local_call(
        second_body, [block, wide, block, ((8, 768), F32)], [cot, sec] + send_plane([s1, s2, s3]) + [first, vecs], "second",
        [pltpu.VMEM((128, 768), BF), pltpu.SemaphoreType.DMA((1,))], final=(0,), raw=1,
    )
    dsecs = gather_back(dsec)
    gfo, s1, s2, s3, dhid = local_call(
        feed_back_body, [wide, block, block, block, ((512, 768), BF)],
        dsecs + [full_up, full_down, slope], "feed_back",
        [pltpu.VMEM((512, 768), BF)],
    )
    gfo = [gfo] + send_plane([s1, s2, s3])
    fkeep, *fsend = local_call(feed_grad_body, [((784, 768), F32)] + [((192, 768), BF)] * 3 + [((208, 768), BF)], [act, after(low, gfo[2])] + dsecs + [dhid], 'feed_grad', [pltpu.VMEM((768, 768), F32), pltpu.VMEM((512, 768), BF)])
    fsent, ffar, fown, fgot = sum_z(
        stage_feed_body, half_body, (208, 768), [fkeep] + [swap(x) for x in fsend], "feed_grad",
        [pltpu.VMEM((784, 768), F32), pltpu.VMEM((4, 16, 768), F32)],
    )
    grad_one, dbr, t0, t1, t2, t3, sums_one = local_call(first_back_body, [wide, block] + [((128, 192), BF)] * 4 + [((8, 768), F32)], [gfo[0]] + gfo[1:] + [grad_two, hat, inv, vecs, full_out], 'first_back')
    dats = [t0] + send_plane([t1, t2, t3])
    gq, gkeep, gk_send, gv_send = local_call(attend_back_body, [((512, 192), BF), ((512, 384), F32), ((512, 192), BF), ((512, 192), BF)], dats + [after(q, fsent)] + kv + [att, lse], 'attend_back', [pltpu.VMEM((512, 192), BF)], mib=24)
    gk_got, gv_got = (swap(gk_send), swap(gv_send))
    g, qkeep, qsend_a, qsend_b = local_call(inner_weight_body, [((512, 576), BF), ((384, 640), F32), ((192, 640), BF), ((192, 640), BF)], [gq, gkeep, gk_got, gv_got] + xs + [sums_two, sums_one], 'inner_weight', [pltpu.VMEM((768, 640), F32), pltpu.VMEM((128, 768), F32), pltpu.VMEM((512, 768), BF)])
    qsent, qfar_sent, qown, qfar = sum_z(stage_q_body, half_body, (96, 640), [qkeep, swap(qsend_a), swap(qsend_b)], 'q', [pltpu.VMEM((384, 640), F32)])
    dbrs = gather_plane(after(dbr, gq))
    gin, s1, s2, s3 = local_call(inner_input_body, [wide, block, block, block], [after(g, qsent), w_qkv], 'inner_input')
    gin = [gin] + send_plane([s1, s2, s3])
    okeep, osend = local_call(
        out_grad_body, [((96, 768), F32), ((96, 768), BF)], [packed] + dbrs, "out_grad",
        [pltpu.VMEM((192, 768), F32), pltpu.VMEM((512, 192), BF), pltpu.VMEM((512, 768), BF)],
    )
    _, _, oown, ofar = sum_z(stage_out_body, half_out_body, (24, 768), [after(okeep, qsent), swap(after(osend, qsent))], 'out', [pltpu.VMEM((96, 768), F32)], [qfar_sent] + [gin[1]])
    down, up_sum = local_call(join_down_body, [((112, 768), BF), ((96, 768), F32)], [after(fown, gin[1]), fgot], 'join_down')
    down = lax.ppermute(down, ("ctx", "fsdp"), [(4 * i + z, 8 * z + i) for i in range(8) for z in range(4)])
    a0, a1, a2, a3 = local_call(turn_body, [((24, 1408), F32)] + [((24, 1408), BF)] * 3, [qown, qfar, up_sum], 'turn', scratch=[pltpu.VMEM((4, 24, 1408), F32)])
    aa = send_plane([a1, a2, a3])
    g_qk, g_v, g_up, *small = local_call(
        finish_body, [((24, 1536), F32), ((24, 768), F32), ((24, 3072), F32)] + [((24,), F32)] * 8, [a0] + aa, "finish",
        [pltpu.VMEM((4, 24, 1408), F32)], final=range(11),
    )
    g_down, g_out, g_bias_up = local_call(
        finish_down_body, [((96, 768), F32), ((24, 768), F32), ((96,), F32)], [down, oown, ofar], "finish_down",
        final=range(3),
    )
    grad_inputs, = local_call(input_sum_body, [wide], [grad_one] + gin, 'input_sum', final=(0,))
    return (
        out.reshape(1, 128, 768), grad_inputs.reshape(1, 128, 768), g_qk, g_v, g_out, g_up, g_down,
        small[0], small[1], small[4], small[2], small[3], g_bias_up, small[7], small[5], small[6],
    )


def solution(mesh):
    blocks = mesh.shape["ctx"] == 8 and mesh.shape["fsdp"] == 4
    return jax.shard_map(
        per_device_blocks if blocks else per_device,
        mesh=mesh,
        in_specs=(
            P("fsdp", "ctx", None),
            P("fsdp", None),
            P("fsdp", None),
            P("fsdp", None),
            P("fsdp", None),
            P("fsdp", None),
            P("fsdp"),
            P("fsdp"),
            P("fsdp"),
            P("fsdp"),
            P("fsdp"),
            P("fsdp"),
            P("fsdp"),
            P("fsdp"),
            P("fsdp"),
            P("fsdp", "ctx", None),
        ),
        out_specs=(
            P("fsdp", "ctx", None),
            P("fsdp", "ctx", None),
            P(("ctx", "fsdp"), None),
            P(("ctx", "fsdp"), None),
            P(("ctx", "fsdp"), None),
            P(("ctx", "fsdp"), None),
            P(("ctx", "fsdp"), None),
            P(("ctx", "fsdp")),
            P(("ctx", "fsdp")),
            P(("ctx", "fsdp")),
            P(("ctx", "fsdp")),
            P(("ctx", "fsdp")),
            P(("ctx", "fsdp")),
            P(("ctx", "fsdp")),
            P(("ctx", "fsdp")),
            P(("ctx", "fsdp")),
        ),
        check_vma=False,
    )
```

```python
import functools
import math

import jax
import jax.numpy as jnp
from jax import lax
from jax.experimental import pallas as pl
from jax.experimental.pallas import tpu as pltpu
from jax.sharding import PartitionSpec as P

HEADS = 12
HEAD = 64


def norm_apply(inputs, norm_gain, norm_shift):
    centre = inputs - jnp.mean(inputs, axis=-1, keepdims=True)
    spread = jnp.mean(centre * centre, axis=-1, keepdims=True)
    return centre * lax.rsqrt(spread + 1e-05) * norm_gain + norm_shift


def left_product(left, right):
    return lax.dot_general(
        left, right, (((0,), (0,)), ((), ())), preferred_element_type=jnp.float32
    )


def right_product(left, right):
    return lax.dot_general(
        left, right, (((1,), (1,)), ((), ())), preferred_element_type=jnp.float32
    )


def column_sums(matrix):
    return jnp.sum(matrix.astype(jnp.float32), axis=0)


def per_device(
    inputs,
    w_query_key,
    w_value,
    w_out,
    w_up,
    w_down,
    bias_query,
    bias_value,
    bias_out,
    gain_attn,
    shift_attn,
    bias_up,
    bias_down,
    gain_ffn,
    shift_ffn,
    cotangent,
):
    gathered = (
        lax.all_gather(w_query_key, "fsdp", axis=0, tiled=True),
        lax.all_gather(w_value, "fsdp", axis=0, tiled=True),
        lax.all_gather(w_out, "fsdp", axis=0, tiled=True),
        lax.all_gather(w_up, "fsdp", axis=0, tiled=True),
        lax.all_gather(w_down, "fsdp", axis=0, tiled=True),
        lax.all_gather(bias_query, "fsdp", axis=0, tiled=True),
        lax.all_gather(bias_value, "fsdp", axis=0, tiled=True),
        lax.all_gather(bias_out, "fsdp", axis=0, tiled=True),
        lax.all_gather(gain_attn, "fsdp", axis=0, tiled=True),
        lax.all_gather(shift_attn, "fsdp", axis=0, tiled=True),
        lax.all_gather(bias_up, "fsdp", axis=0, tiled=True),
        lax.all_gather(bias_down, "fsdp", axis=0, tiled=True),
        lax.all_gather(gain_ffn, "fsdp", axis=0, tiled=True),
        lax.all_gather(shift_ffn, "fsdp", axis=0, tiled=True),
    )
    full_qk, full_value, full_out, full_up, full_down = (
        gathered[0],
        gathered[1],
        gathered[2],
        gathered[3],
        gathered[4],
    )
    smalls = [piece.astype(jnp.float32) for piece in gathered[5:]]
    (
        vec_query,
        vec_value,
        vec_out,
        vec_gain_one,
        vec_shift_one,
        vec_up,
        vec_down,
        vec_gain_two,
        vec_shift_two,
    ) = smalls
    rows = inputs.shape[1]
    width = inputs.shape[2]
    heads = HEADS
    head = HEAD
    tokens = inputs.reshape(rows, width)
    tok_float = tokens.astype(jnp.float32)
    query_key = jnp.dot(tokens, full_qk, preferred_element_type=jnp.float32)
    queries = (query_key[:, :width] + vec_query).astype(jnp.bfloat16)
    keys = query_key[:, width:].astype(jnp.bfloat16)
    values = (jnp.dot(tokens, full_value, preferred_element_type=jnp.float32) + vec_value).astype(
        jnp.bfloat16
    )
    query_heads = queries.reshape(rows, heads, head)
    start_state = (
        jnp.full((heads, rows), -1e30, jnp.float32),
        jnp.zeros((heads, rows), jnp.float32),
        jnp.zeros((rows, heads, head), jnp.float32),
    )
    carry = start_state
    key_piece = lax.all_gather(keys, "ctx", axis=0, tiled=True)
    value_piece = lax.all_gather(values, "ctx", axis=0, tiled=True)
    count = key_piece.shape[0]
    block = math.gcd(count, 2048)
    key_split = key_piece.reshape(count // block, block, heads, head)
    value_split = value_piece.reshape(count // block, block, heads, head)

    def step_block(state, pair):
        running_max, running_sum, running_acc = state
        key_block, value_block = pair
        scores = (
            jnp.einsum("qhd,khd->hqk", query_heads, key_block, preferred_element_type=jnp.float32)
            * 0.125
        )
        new_max = jnp.maximum(running_max, jnp.max(scores, axis=-1))
        factor = jnp.exp(running_max - new_max)
        weights = jnp.exp(scores - new_max[:, :, None])
        running_sum = running_sum * factor + jnp.sum(weights, axis=-1)
        update = jnp.einsum(
            "hqk,khd->qhd",
            weights.astype(jnp.bfloat16),
            value_block,
            preferred_element_type=jnp.float32,
        )
        running_acc = running_acc * jnp.transpose(factor)[:, :, None] + update
        return ((new_max, running_sum, running_acc), None)

    carry, unused = lax.scan(step_block, carry, (key_split, value_split))
    final_max, final_sum, final_acc = carry
    attended_heads = final_acc / jnp.transpose(final_sum)[:, :, None]
    log_total = final_max + jnp.log(final_sum)
    attended_low = attended_heads.reshape(rows, width).astype(jnp.bfloat16)
    branch = jnp.dot(attended_low, full_out, preferred_element_type=jnp.float32) + vec_out
    first, norm_one_pull = jax.vjp(norm_apply, tok_float + branch, vec_gain_one, vec_shift_one)
    first_low = first.astype(jnp.bfloat16)
    hidden = jnp.dot(first_low, full_up, preferred_element_type=jnp.float32) + vec_up
    activ, gelu_pull = jax.vjp(functools.partial(jax.nn.gelu, approximate=False), hidden)
    activ_low = activ.astype(jnp.bfloat16)
    second = jnp.dot(activ_low, full_down, preferred_element_type=jnp.float32) + vec_down
    output, norm_two_pull = jax.vjp(norm_apply, first + second, vec_gain_two, vec_shift_two)
    grad_resid_two, grad_gain_ffn, grad_shift_ffn = norm_two_pull(
        cotangent.reshape(rows, width).astype(jnp.float32)
    )
    second_low = grad_resid_two.astype(jnp.bfloat16)
    grad_w_down = left_product(activ_low, second_low)
    grad_bias_down = column_sums(second_low)
    grad_activ = right_product(second_low, full_down)
    hidden_low = gelu_pull(grad_activ)[0].astype(jnp.bfloat16)
    grad_w_up = left_product(first_low, hidden_low)
    grad_bias_up = column_sums(hidden_low)
    grad_first = grad_resid_two + right_product(hidden_low, full_up)
    grad_resid_one, grad_gain_attn, grad_shift_attn = norm_one_pull(grad_first)
    branch_low = grad_resid_one.astype(jnp.bfloat16)
    grad_w_out = left_product(attended_low, branch_low)
    grad_bias_out = column_sums(branch_low)
    dout_low = right_product(branch_low, full_out).astype(jnp.bfloat16)
    dout_heads = dout_low.reshape(rows, heads, head)
    delta = jnp.einsum("qhd,qhd->hq", dout_heads.astype(jnp.float32), attended_heads)
    all_keys, all_values = (
        lax.all_gather(keys, "ctx", axis=0, tiled=True),
        lax.all_gather(values, "ctx", axis=0, tiled=True),
    )
    total = all_keys.shape[0]
    key_total = all_keys.shape[0]
    block = math.gcd(key_total, 2048)

    def back_block(grad_query, pair):
        key_block, value_block = pair
        scores = (
            jnp.einsum("qhd,khd->hqk", query_heads, key_block, preferred_element_type=jnp.float32)
            * 0.125
        )
        weights = jnp.exp(scores - log_total[:, :, None])
        weight_grad = jnp.einsum(
            "qhd,khd->hqk", dout_heads, value_block, preferred_element_type=jnp.float32
        )
        score_grad = (weights * (weight_grad - delta[:, :, None]) * 0.125).astype(jnp.bfloat16)
        grad_query = grad_query + jnp.einsum(
            "hqk,khd->qhd", score_grad, key_block, preferred_element_type=jnp.float32
        )
        value_grad = jnp.einsum(
            "hqk,qhd->khd",
            weights.astype(jnp.bfloat16),
            dout_heads,
            preferred_element_type=jnp.float32,
        )
        key_grad = jnp.einsum(
            "hqk,qhd->khd", score_grad, query_heads, preferred_element_type=jnp.float32
        )
        return (grad_query, (key_grad, value_grad))

    grad_query, terms = lax.scan(
        back_block,
        jnp.zeros((rows, heads, head), jnp.float32),
        (
            all_keys.reshape(key_total // block, block, heads, head),
            all_values.reshape(key_total // block, block, heads, head),
        ),
    )
    grad_keys, grad_values = (
        lax.psum_scatter(terms[0].reshape(total, width), "ctx", scatter_dimension=0, tiled=True),
        lax.psum_scatter(terms[1].reshape(total, width), "ctx", scatter_dimension=0, tiled=True),
    )
    grad_queries = grad_query.reshape(rows, width)
    query_low = grad_queries.astype(jnp.bfloat16)
    key_low = grad_keys.astype(jnp.bfloat16)
    value_low = grad_values.astype(jnp.bfloat16)
    query_key_low = jnp.concatenate([query_low, key_low], axis=1)
    grad_w_query_key = left_product(tokens, query_key_low)
    grad_w_value = left_product(tokens, value_low)
    grad_bias_query = column_sums(query_low)
    grad_bias_value = column_sums(value_low)
    grad_inputs = (
        grad_resid_one
        + right_product(query_key_low, full_qk)
        + right_product(value_low, full_value)
    )
    summed = (
        lax.psum_scatter(grad_w_query_key, ("ctx", "fsdp"), scatter_dimension=0, tiled=True),
        lax.psum_scatter(grad_w_value, ("ctx", "fsdp"), scatter_dimension=0, tiled=True),
        lax.psum_scatter(grad_w_out, ("ctx", "fsdp"), scatter_dimension=0, tiled=True),
        lax.psum_scatter(grad_w_up, ("ctx", "fsdp"), scatter_dimension=0, tiled=True),
        lax.psum_scatter(grad_w_down, ("ctx", "fsdp"), scatter_dimension=0, tiled=True),
        lax.psum_scatter(grad_bias_query, ("ctx", "fsdp"), scatter_dimension=0, tiled=True),
        lax.psum_scatter(grad_bias_value, ("ctx", "fsdp"), scatter_dimension=0, tiled=True),
        lax.psum_scatter(grad_bias_out, ("ctx", "fsdp"), scatter_dimension=0, tiled=True),
        lax.psum_scatter(grad_gain_attn, ("ctx", "fsdp"), scatter_dimension=0, tiled=True),
        lax.psum_scatter(grad_shift_attn, ("ctx", "fsdp"), scatter_dimension=0, tiled=True),
        lax.psum_scatter(grad_bias_up, ("ctx", "fsdp"), scatter_dimension=0, tiled=True),
        lax.psum_scatter(grad_bias_down, ("ctx", "fsdp"), scatter_dimension=0, tiled=True),
        lax.psum_scatter(grad_gain_ffn, ("ctx", "fsdp"), scatter_dimension=0, tiled=True),
        lax.psum_scatter(grad_shift_ffn, ("ctx", "fsdp"), scatter_dimension=0, tiled=True),
    )
    return (
        output.astype(jnp.bfloat16).reshape(1, rows, width),
        grad_inputs.reshape(1, rows, width),
        summed[0],
        summed[1],
        summed[2],
        summed[3],
        summed[4],
        summed[5],
        summed[6],
        summed[7],
        summed[8],
        summed[9],
        summed[10],
        summed[11],
        summed[12],
        summed[13],
    )


BF = jnp.bfloat16
F32 = jnp.float32


COST = dict(attend=20, branch=20, feed=2, second=7.5, feed_back=3, first_back=9, attend_back=16, inner_weight=2.2, inner_input=7, feed_grad=5, turn=5, join_down=9, out_grad=2.0, input_sum=1, gather_out=8, pack_feed=9, half_feed_grad=8.5, settle_feed=8, finish_down=9, half_q=1)


def local_call(body, outs, args, name, scratch=(), mib=16, final=(), raw=0):
    vmem, hbm = pl.BlockSpec(memory_space=pltpu.VMEM), pl.BlockSpec(memory_space=pltpu.HBM)
    held = [pltpu.with_memory_space_constraint(a, pltpu.HBM if i < raw else pltpu.VMEM) for i, a in enumerate(args)]
    return pl.pallas_call(
        body,
        out_shape=tuple(jax.ShapeDtypeStruct(s, d) if i in final else pltpu.VMEM(s, d) for i, (s, d) in enumerate(outs)),
        in_specs=[hbm] * raw + [vmem] * (len(args) - raw),
        out_specs=tuple(vmem for _ in outs),
        scratch_shapes=list(scratch),
        compiler_params=pltpu.CompilerParams(vmem_limit_bytes=mib * 1024 * 1024),
        cost_estimate=pl.CostEstimate(flops=int(COST.get(name, 0) * 524e6), bytes_accessed=0, transcendentals=0),
        name=name,
    )(*held)


def fetch(sems, *pairs):
    copies = [pltpu.make_async_copy(src, dst, sems.at[i]) for i, (src, dst) in enumerate(pairs)]
    for copy in copies:
        copy.start()
    for copy in copies:
        copy.wait()


def place():
    c = lax.axis_index("ctx")
    return c // 2, c % 2, lax.axis_index("fsdp")


def chip(k, j):
    return k ^ j


def mm(a, b):
    return jnp.dot(a, b, preferred_element_type=F32)


def mm_nt(a, b):
    return lax.dot_general(a, b, (((1,), (1,)), ((), ())), preferred_element_type=F32)


def mm_tn(a, b):
    return lax.dot_general(a, b, (((0,), (0,)), ((), ())), preferred_element_type=F32)


def rows_at(start, size, step):
    return pl.ds(pl.multiple_of(start, step), size)


def pack_qkv(x_hbm, w_qk_hbm, w_v_hbm, w_out_hbm, *rest):
    raw, (own, other, x, w_qk, w_v, w_out), vecs, (tmp, wide, sems) = rest[:9], rest[9:15], rest[15:24], rest[24:]
    k, h, f = place()
    fetch(sems, (x_hbm, x), (w_qk_hbm, w_qk), (w_v_hbm, w_v), (w_out_hbm.at[rows_at(48 * k, 48, 16), :], w_out), *zip(raw, vecs))
    tmp[...] = jnp.zeros_like(tmp)
    for i in range(8):
        at = slice(192 * (i % 4), 192 * (i % 4) + 192)
        tmp[i // 4 : 1 + i // 4, at] = vecs[i][...].astype(F32).reshape(1, 192)
    tmp[2:3, :] = vecs[8][...].astype(F32).reshape(1, 768)
    small = tmp[...].astype(BF)
    wide[...] = w_out[...].astype(F32)
    for out, half in ((own, h), (other, 1 - h)):
        rows = rows_at(half * 96, 96, 16)
        piece = wide[rows_at(24 * half, 24, 8), :]
        parts = [piece[:, 192 * t : 192 * t + 192] for t in range(4)]
        out[0:96, 576:768] = jnp.concatenate(parts, axis=0).astype(BF)
        out[96:112, :] = small
        for kk in range(4):

            @pl.when(k == kk)
            def _():
                out[0:96, 0:192] = w_qk[rows, 192 * kk : 192 * kk + 192]
                out[0:96, 192:384] = w_qk[rows, 768 + 192 * kk : 960 + 192 * kk]
                out[0:96, 384:576] = w_v[rows, 192 * kk : 192 * kk + 192]


def pack_feed(w_up_hbm, w_down_hbm, token, own, other, w_up, w_down, sems):
    k, h, f = place()
    fetch(sems, (w_up_hbm, w_up), (w_down_hbm.at[rows_at(192 * k, 192, 16), :], w_down))
    for kk in range(4):
        for half in range(2):

            @pl.when(k == kk)
            def _():
                for which, out in enumerate((own, other)):

                    @pl.when(h == (half + which) % 2)
                    def _():
                        for g in range(4):
                            at = 768 * g + 192 * kk + 96 * half
                            out[0:192, 96 * g : 96 * g + 96] = w_up[:, at : at + 96]
                        out[192:288, :] = w_down[96 * half : 96 * half + 96, 0:384]
                        out[288:384, :] = w_down[96 * half : 96 * half + 96, 384:768]


def qkv_body(x0, x1, x2, x3, own, other, p1, p2, p3, m1, m2, m3, q, kv, w, vecs, up, tmp, vec, row, xs):
    k, h, f = place()
    for s, (mine, mate) in enumerate(((own, other), (p1, m1), (p2, m2), (p3, m3))):
        g = f ^ s
        w[rows_at(192 * g + 96 * h, 96, 16), :] = mine[0:96, 0:576]
        w[rows_at(192 * g + 96 * (1 - h), 96, 16), :] = mate[0:96, 0:576]
        tmp[g] = mine[96:112, :].astype(F32)
    for g in range(4):
        for i in range(8):
            at = 192 * (i % 4)
            vecs[i : i + 1, 192 * g : 192 * g + 192] = tmp[g, i // 4 : i // 4 + 1, at : at + 192]
    for kk in range(4):

        @pl.when(k == kk)
        def _():
            for half in range(2):
                for g in range(4):
                    at = 192 * kk + 96 * half
                    row[0:1, 384 * half + 96 * g : 384 * half + 96 * g + 96] = tmp[g, 2:3, at : at + 96]

    up[...] = row[0:1, :]
    for i in range(2):
        vec[i : i + 1, :] = tmp[k, 0:1, 192 * i : 192 * i + 192]
    for j, x in enumerate((x0, x1, x2, x3)):
        xs[128 * j : 128 * j + 128, :] = x[...]
    r = mm(xs[...], w[...])
    q[...] = ((r[:, 0:192] + vec[0:1, :]) * 0.125).astype(BF)
    kv[:, 0:192] = r[:, 192:384].astype(BF)
    kv[:, 192:384] = (r[:, 384:576] + vec[1:2, :]).astype(BF)


def gather_out_body(p0, p1, p2, p3, d):
    for s, p in enumerate((p0, p1, p2, p3)):
        d[:, 192 * s : 192 * s + 192] = p[0:96, 576:768]


def settle_out_body(d0, d1, d2, d3, e1, e2, e3, m0, m1, m2, m3, w_out, tmp):
    k, h, f = place()
    for half, parts in ((h, (d0, d1, d2, d3)), (1 - h, (None, e1, e2, e3))):
        for j, d in enumerate(parts):
            for s in range(4):
                rows = rows_at(192 * (f ^ s) + 48 * chip(k, j) + 24 * half, 24, 8)
                if d is None:
                    piece = (m0, m1, m2, m3)[s][0:96, 576:768].astype(F32)
                else:
                    piece = d[:, 192 * s : 192 * s + 192].astype(F32)
                for t in range(4):
                    tmp[rows, 192 * t : 192 * t + 192] = piece[24 * t : 24 * t + 24, :]
    w_out[...] = tmp[...].astype(BF)


def settle_feed_body(p0, p1, p2, p3, e0, e1, e2, e3, w_up, w_down):
    k, h, f = place()
    for half, parts in ((h, (p0, p1, p2, p3)), (1 - h, (e0, e1, e2, e3))):
        lanes = pl.ds(pl.multiple_of(384 * half, 128), 384)
        for s, part in enumerate(parts):
            g = f ^ s
            w_up[rows_at(192 * g, 192, 16), lanes] = part[0:192, :]
            rows = rows_at(384 * half + 96 * g, 96, 16)
            w_down[rows, 0:384] = part[192:288, :]
            w_down[rows, 384:768] = part[288:384, :]


def attend_body(q, kv, mate, packed, att, lse):
    for i in range(3):
        lanes, vlanes = slice(64 * i, 64 * i + 64), slice(192 + 64 * i, 256 + 64 * i)
        sa = mm_nt(q[:, lanes], kv[:, lanes])
        sb = mm_nt(q[:, lanes], mate[:, lanes])
        top = jnp.maximum(jnp.max(sa, axis=1, keepdims=True), jnp.max(sb, axis=1, keepdims=True))
        ea = jnp.exp(sa - top)
        eb = jnp.exp(sb - top)
        total = jnp.sum(ea, axis=1, keepdims=True) + jnp.sum(eb, axis=1, keepdims=True)
        out = (mm(ea.astype(BF), kv[:, vlanes]) + mm(eb.astype(BF), mate[:, vlanes])) / total
        att[i] = out
        lse[i] = top + jnp.log(total)
        low = out.astype(BF)
        packed[:, lanes] = low[0:256, :]
        packed[:, vlanes] = low[256:512, :]


def norm_parts(v):
    centre = v - jnp.mean(v, axis=1, keepdims=True)
    inv = lax.rsqrt(jnp.mean(centre * centre, axis=1, keepdims=True) + 1e-05)
    return centre * inv, inv


def branch_body(a0, a1, a2, a3, x0, x1, x2, x3, w_out, vecs, low, first, hat, inv, att, xs):
    k, h, f = place()
    parts = (a0, a1, a2, a3)
    for m, x in enumerate((x0, x1, x2, x3)):
        xs[128 * m : 128 * m + 128, :] = x[...]
        for j in range(4):
            b = j ^ m
            rows, lanes = 128 * (b % 2), 192 * (b // 2)
            att[j, 128 * m : 128 * m + 128, :] = parts[j][rows : rows + 128, lanes : lanes + 192]
    acc = xs[...].astype(F32) + vecs[2:3, :]
    for j in range(4):
        acc = acc + mm(att[j], w_out[rows_at(192 * chip(k, j), 192, 16), :])
    n, r = norm_parts(acc)
    y = n * vecs[3:4, :] + vecs[4:5, :]
    low[...] = y.astype(BF)
    first[...] = y[0:128, :]
    hat[...] = n[0:128, :]
    inv[...] = r[0:128, :]


def feed_body(low, w_up, w_down, up, own, s1, s2, s3, act, slope):
    hid = mm(low[...], w_up[...]) + up[...]
    cdf = 0.5 * (1.0 + lax.erf(hid * (2.0**-0.5)))
    pdf = jnp.exp(hid * hid * -0.5) * ((2.0 * math.pi) ** -0.5)
    a = (hid * cdf).astype(BF)
    act[...] = a
    slope[...] = (cdf + hid * pdf).astype(BF)
    part = mm(a, w_down[...])
    for m, out in enumerate((own, s1, s2, s3)):
        out[...] = part[128 * m : 128 * m + 128, :].astype(out.dtype)


def second_body(cot_hbm, own, r1, r2, r3, first, vecs, out, grad, low, sums, cot, sems):
    copy = pltpu.make_async_copy(cot_hbm, cot, sems.at[0])
    copy.start()
    v = own[...] + r1[...].astype(F32) + r2[...].astype(F32) + r3[...].astype(F32)
    n, inv = norm_parts(v + first[...] + vecs[5:6, :])
    out[...] = (n * vecs[6:7, :] + vecs[7:8, :]).astype(BF)
    copy.wait()
    dy = cot[...].astype(F32)
    g, lowered = norm_back(dy, n, inv, vecs[6:7, :])
    grad[...] = g
    low[...] = lowered
    sums[...] = jnp.zeros_like(sums)
    sums[0:1, :] = jnp.sum(dy * n, axis=0, keepdims=True)
    sums[1:2, :] = jnp.sum(dy, axis=0, keepdims=True)
    sums[2:3, :] = jnp.sum(lowered.astype(F32), axis=0, keepdims=True)


def norm_back(dy, n, inv, gain):
    d = dy * gain
    g = inv * (d - jnp.mean(d, axis=1, keepdims=True) - n * jnp.mean(d * n, axis=1, keepdims=True))
    return g, g.astype(BF)


def feed_back_body(d0, d1, d2, d3, w_up, w_down, slope, own, s1, s2, s3, dhid, ds):
    for m, d in enumerate((d0, d1, d2, d3)):
        ds[128 * m : 128 * m + 128, :] = d[...]
    dh = (mm_nt(ds[...], w_down[...]) * slope[...].astype(F32)).astype(BF)
    dhid[...] = dh
    part = mm_nt(dh, w_up[...])
    for m, out in enumerate((own, s1, s2, s3)):
        out[...] = part[128 * m : 128 * m + 128, :].astype(out.dtype)


def feed_grad_body(act, low, d0, d1, d2, d3, dhid, keep, send_a, send_b, send_c, send_d, full, ds):
    k, h, f = place()
    for m, d in enumerate((d0, d1, d2, d3)):
        ds[128 * m : 128 * m + 128, :] = d[...]
    full[...] = mm_tn(act[...], ds[...])
    keep[0:384, :] = full[rows_at(384 * h, 384, 8), :]
    send_a[...] = full[rows_at(384 * (1 - h), 192, 8), :].astype(BF)
    send_b[...] = full[rows_at(384 * (1 - h) + 192, 192, 8), :].astype(BF)
    full[...] = mm_tn(low[...], dhid[...])
    for kk in range(4):
        keep[384 + 96 * kk : 480 + 96 * kk, :] = full[rows_at(192 * kk + 96 * h, 96, 8), :]
        out = (send_c, send_d)[kk // 2]
        out[96 * (kk % 2) : 96 * (kk % 2) + 96, :] = full[rows_at(192 * kk + 96 * (1 - h), 96, 8), :].astype(BF)
    total = jnp.sum(dhid[...].astype(F32), axis=0, keepdims=True)
    lo, hi = total[:, 0:384], total[:, 384:768]
    keep[768:784, :] = jnp.zeros((16, 768), F32)
    keep[768:769, 0:384] = jnp.where(h == 0, lo, hi)
    full[0:16, :] = jnp.zeros((16, 768), F32)
    full[0:1, 0:384] = jnp.where(h == 0, hi, lo)
    send_d[192:208, :] = full[0:16, :].astype(BF)


def first_back_body(own, r1, r2, r3, grad, hat, inv, vecs, w_out, out, low, t0, t1, t2, t3, sums):
    k, h, f = place()
    dy = own[...] + r1[...].astype(F32) + r2[...].astype(F32) + r3[...].astype(F32) + grad[...]
    n = hat[...]
    g, lowered = norm_back(dy, n, inv[...], vecs[3:4, :])
    out[...] = g
    low[...] = lowered
    for j, t in enumerate((t0, t1, t2, t3)):
        t[...] = mm_nt(lowered, w_out[rows_at(192 * chip(k, j), 192, 16), :]).astype(BF)
    sums[...] = jnp.zeros_like(sums)
    sums[0:1, :] = jnp.sum(dy * n, axis=0, keepdims=True)
    sums[1:2, :] = jnp.sum(dy, axis=0, keepdims=True)
    sums[2:3, :] = jnp.sum(lowered.astype(F32), axis=0, keepdims=True)


def attend_back_body(d0, d1, d2, d3, q, kv, mate, att, lse, gq, keep, send_k, send_v, dat):
    for m, d in enumerate((d0, d1, d2, d3)):
        dat[128 * m : 128 * m + 128, :] = d[...]
    for i in range(3):
        lanes, vlanes = slice(64 * i, 64 * i + 64), slice(192 + 64 * i, 256 + 64 * i)
        qi = q[:, lanes]
        do = dat[:, lanes]
        delta = jnp.sum(do.astype(F32) * att[i], axis=1, keepdims=True)
        total = lse[i]
        gqi = None
        for keys in (kv, mate):
            p = jnp.exp(mm_nt(qi, keys[:, lanes]) - total)
            ds = (p * (mm_nt(do, keys[:, vlanes]) - delta)).astype(BF)
            part = mm(ds, keys[:, lanes])
            gqi = part if gqi is None else gqi + part
            gk, gv = mm_tn(ds, qi), mm_tn(p.astype(BF), do)
            if keys is kv:
                keep[:, lanes] = gk
                keep[:, vlanes] = gv
            else:
                send_k[:, lanes] = gk.astype(BF)
                send_v[:, lanes] = gv.astype(BF)
        gq[:, lanes] = (gqi * 0.125).astype(BF)


def out_grad_body(packed, d0, d1, d2, d3, keep, send, full, att, ds):
    k, h, f = place()
    for m, d in enumerate((d0, d1, d2, d3)):
        ds[128 * m : 128 * m + 128, :] = d[0:128, :]
    att[0:256, :] = packed[:, 0:192]
    att[256:512, :] = packed[:, 192:384]
    full[...] = mm_tn(att[...], ds[...])
    keep[...] = full[rows_at(96 * h, 96, 8), :]
    send[...] = full[rows_at(96 * (1 - h), 96, 8), :].astype(BF)


def inner_weight_body(gq, gk, got_k, got_v, x0, x1, x2, x3, sums_a, sums_b, g, keep, send_a, send_b, full, cols, xs):
    k, h, f = place()
    g[:, 0:192] = gq[...]
    g[:, 192:384] = (gk[:, 0:192] + got_k[...].astype(F32)).astype(BF)
    g[:, 384:576] = (gk[:, 192:384] + got_v[...].astype(F32)).astype(BF)
    for m, x in enumerate((x0, x1, x2, x3)):
        xs[128 * m : 128 * m + 128, :] = x[...]
    cols[...] = jnp.zeros_like(cols)
    bias = jnp.sum(g[...].astype(F32), axis=0, keepdims=True)
    for kk in range(4):

        @pl.when(k == kk)
        def _():
            cols[64:65, 192 * kk : 192 * kk + 192] = bias[:, 0:192]
            cols[65:66, 192 * kk : 192 * kk + 192] = bias[:, 384:576]

    cols[66:69, :] = sums_b[0:3, :]
    cols[69:72, :] = sums_a[0:3, :]
    full[:, 0:576] = mm_tn(xs[...], g[...])
    lane = lax.broadcasted_iota(jnp.int32, (768, 128), 1)
    full[:, 512:640] = jnp.where(lane < 64, full[:, 512:640], jnp.transpose(cols[...]))
    for kk in range(4):
        at = slice(96 * kk, 96 * kk + 96)
        keep[at, :] = full[rows_at(192 * kk + 96 * h, 96, 8), :]
        out = (send_a, send_b)[kk // 2]
        out[96 * (kk % 2) : 96 * (kk % 2) + 96, :] = full[rows_at(192 * kk + 96 * (1 - h), 96, 8), :].astype(BF)


def inner_input_body(g, w, own, s1, s2, s3):
    part = mm_nt(g[...], w[...])
    for m, out in enumerate((own, s1, s2, s3)):
        out[...] = part[128 * m : 128 * m + 128, :].astype(out.dtype)


def input_sum_body(grad, own, r1, r2, r3, out):
    n = r1.shape[0]
    total = grad[...] + own[...]
    for r in (r1, r2, r3):
        total = total + r[n - 128 : n, :].astype(F32)
    out[...] = total


def stage_feed_body(keep, got_a, got_b, got_c, got_d, held, sent, tmp, one):
    k, h, f = place()
    for at, n, got in ((0, 192, got_a), (192, 192, got_b), (384, 192, got_c), (576, 208, got_d)):
        tmp[at : at + n, :] = keep[at : at + n, :] + got[...].astype(F32)
    for g in range(4):
        one[g] = jnp.zeros((16, 768), F32)
        one[g, 0:1, 0:96] = tmp[768:769, 96 * g : 96 * g + 96]
    for s in range(4):
        out, g = (held, sent)[s % 2], f ^ s
        v = [tmp[rows_at(96 * g, 96, 8), :], one[g]] + [tmp[rows_at(384 + 96 * kk + 24 * g, 24, 8), :] for kk in range(4)]
        out[208 * (s // 2) : 208 * (s // 2) + 208, :] = jnp.concatenate(v, axis=0).astype(out.dtype)


def stage_q_body(keep, got_a, got_b, held, sent, tmp):
    k, h, f = place()
    tmp[0:192, :] = keep[0:192, :] + got_a[...].astype(F32)
    tmp[192:384, :] = keep[192:384, :] + got_b[...].astype(F32)
    for s in range(4):
        out = (held, sent)[s % 2]
        v = [tmp[rows_at(96 * kk + 24 * (f ^ s), 24, 8), :] for kk in range(4)]
        out[96 * (s // 2) : 96 * (s // 2) + 96, :] = jnp.concatenate(v, axis=0).astype(out.dtype)


def stage_out_body(keep, got, held, sent, tmp):
    k, h, f = place()
    tmp[...] = keep[...] + got[...].astype(F32)
    for half, out in enumerate((held, sent)):
        v = [tmp[rows_at(24 * (f ^ s), 24, 8), :] for s in (half, half + 2)]
        out[...] = jnp.concatenate(v, axis=0).astype(out.dtype)


def half_body(held, got, own, far):
    n = own.shape[0]
    own[...] = held[0:n, :] + got[0:n, :].astype(F32)
    far[...] = (held[n : 2 * n, :] + got[n : 2 * n, :].astype(F32)).astype(BF)


def half_out_body(held, got, own, far):
    v = held[...] + got[...].astype(F32)
    own[...] = v[0:24, :]
    far[...] = v[24:48, :].astype(BF)


def join_down_body(own, r, down, up):
    v = own[...] + r[...].astype(F32)
    down[...] = v[0:112, :].astype(BF)
    up[...] = v[112:208, :]


def turn_body(own, r, up, a0, a1, a2, a3, tmp):
    k, h, f = place()
    v = own[...] + r[...].astype(F32)
    u = up[...]
    for kk in range(4):
        tmp[kk, :, 0:768] = u[24 * kk : 24 * kk + 24, :]
        tmp[kk, :, 768:1408] = v[24 * kk : 24 * kk + 24, :]
    for j, out in enumerate((a0, a1, a2, a3)):
        out[...] = tmp[chip(k, j)].astype(out.dtype)


def finish_down_body(down, out, o1, w_down, w_out, bias_up):
    w_down[...] = down[0:96, :].astype(F32)
    bias_up[...] = down[96:112, :].astype(F32)[0:1, 0:96].reshape(96)
    w_out[...] = out[...] + o1[...].astype(F32)


def finish_body(own, r1, r2, r3, w_qk, w_v, w_up, *rest):
    vecs, tmp = rest[:8], rest[8]
    k, h, f = place()
    total = None
    for j, r in enumerate((own, r1, r2, r3)):
        v = r[...].astype(F32)
        tmp[chip(k, j)] = v
        part = v[:, 1280:1408]
        total = part if total is None else total + part
    for kk in range(4):
        v = tmp[kk]
        for half in range(2):
            for g in range(4):
                at = 768 * g + 192 * kk + 96 * half
                w_up[:, at : at + 96] = v[:, 384 * half + 96 * g : 384 * half + 96 * g + 96]
        w_qk[:, 192 * kk : 192 * kk + 192] = v[:, 768:960]
        w_qk[:, 768 + 192 * kk : 960 + 192 * kk] = v[:, 960:1152]
        w_v[:, 192 * kk : 192 * kk + 192] = v[:, 1152:1344]
    turned = jnp.transpose(jnp.concatenate([total, jnp.zeros((104, 128), F32)], axis=0))
    for i in range(8):
        vecs[i][...] = turned[64 + i : 65 + i, 0:24].reshape(24)


def swap(x):
    return lax.ppermute(x, "ctx", [(i, i ^ 1) for i in range(8)])


def to_chip(x, j):
    return lax.ppermute(x, "ctx", [(i, i ^ (2 * j)) for i in range(8)])


def to_plane(x, s):
    return lax.ppermute(x, "fsdp", [(i, i ^ s) for i in range(4)])


def send_plane(xs):
    return [to_chip(x, j) for j, x in enumerate(xs, 1)]


def send_back(xs):
    return [to_chip(x, 3 - j) for j, x in enumerate(xs[::-1])][::-1]


def gather_plane(x):
    return [x, *send_plane([x] * 3)]


def gather_back(x):
    return [x, *send_back([x] * 3)]


def relay_plane(x):
    a = to_chip(x, 1)
    return [x, a, to_chip(x, 2), to_chip(a, 2)]


def gather_z(x):
    return [x, to_plane(x, 1), to_plane(x, 2)]


def sum_z(body, mid, outs, args, name, scratch, gate=()):
    rows, lanes = outs
    held, sent = local_call(body, [((2 * rows, lanes), F32), ((2 * rows, lanes), BF)], args, "stage_" + name, scratch)
    own, far = local_call(mid, [((rows, lanes), F32), ((rows, lanes), BF)], [after(held, *gate), to_plane(sent, 1)], "half_" + name)
    return sent, far, own, to_plane(far, 2)


def after(value, *others):
    return lax.optimization_barrier((value, *others))[0]


def per_device_blocks(
    inputs, w_query_key, w_value, w_out, w_up, w_down, bias_query, bias_value, bias_out,
    gain_attn, shift_attn, bias_up, bias_down, gain_ffn, shift_ffn, cotangent,
):
    c = lax.axis_index("ctx")
    cot = cotangent.reshape(128, 768)
    block, wide = ((128, 768), BF), ((128, 768), F32)
    vectors = [bias_query, bias_value, bias_out, gain_attn, shift_attn, bias_down, gain_ffn, shift_ffn, bias_up]

    own, other, x0 = local_call(
        pack_qkv, [((112, 768), BF)] * 2 + [block], [inputs.reshape(128, 768), w_query_key, w_value, w_out] + vectors, "pack_qkv",
        [pltpu.VMEM((192, 1536), BF), pltpu.VMEM((192, 768), BF), pltpu.VMEM((48, 768), BF)]
        + [pltpu.VMEM((192,), BF)] * 8
        + [pltpu.VMEM((768,), BF), pltpu.VMEM((16, 768), F32), pltpu.VMEM((48, 768), F32), pltpu.SemaphoreType.DMA((13,))],
        raw=13,
    )
    pz_far = to_plane(own, 2)
    pz_near = to_plane(own, 1)
    part, mate_part = local_call(
        pack_feed, [((384, 384), BF)] * 2, [w_up, w_down, own], "pack_feed",
        [pltpu.VMEM((192, 3072), BF), pltpu.VMEM((192, 768), BF), pltpu.SemaphoreType.DMA((2,))],
        raw=2,
    )
    pz = [pz_near, pz_far, to_plane(after(pz_far, part), 1)]
    xs = gather_back(x0)
    parts = gather_z(after(part, pz[1]))
    pm = [swap(after(p, *xs[1:])) for p in pz]
    q, kv, w_qkv, vecs, up = local_call(
        qkv_body,
        [((512, 192), BF), ((512, 384), BF), ((768, 576), BF), ((8, 768), F32), ((1, 768), F32)],
        xs + [own, other] + pz + pm, "qkv",
        [pltpu.VMEM((4, 16, 768), F32), pltpu.VMEM((8, 192), F32), pltpu.VMEM((8, 768), F32), pltpu.VMEM((512, 768), BF)],
    )
    kv = [kv, swap(kv)]
    (piece,) = local_call(gather_out_body, [((96, 768), BF)], [own] + pz, "gather_out")
    ds = relay_plane(after(piece, q))
    both = parts[2]
    packed, att, lse = local_call(
        attend_body, [((256, 384), BF), ((3, 512, 64), F32), ((3, 512, 1), F32)], [q] + kv, "attend"
    )
    both = after(both, packed)
    parts.append(to_plane(both, 1))
    atts = relay_plane(packed)
    full_out, = local_call(settle_out_body, [((768, 768), BF)], ds + [swap(d) for d in ds[1:]] + [other] + pm, 'settle_out', [pltpu.VMEM((768, 768), F32)])
    full_up, full_down = local_call(
        settle_feed_body, [((768, 768), BF)] * 2, parts + [mate_part] + [swap(p) for p in parts[1:]], "settle_feed"
    )
    low, first, hat, inv = local_call(
        branch_body, [((512, 768), BF), wide, wide, ((128, 1), F32)], atts + xs + [full_out, vecs], "branch",
        [pltpu.VMEM((4, 512, 192), BF), pltpu.VMEM((512, 768), BF)]
    )
    sec, s1, s2, s3, act, slope = local_call(
        feed_body, [wide, block, block, block, ((512, 768), BF), ((512, 768), BF)], [low, full_up, full_down, up], "feed",

    )
    out, grad_two, dsec, sums_two = local_call(
        second_body, [block, wide, block, ((8, 768), F32)], [cot, sec] + send_plane([s1, s2, s3]) + [first, vecs], "second",
        [pltpu.VMEM((128, 768), BF), pltpu.SemaphoreType.DMA((1,))], final=(0,), raw=1,
    )
    dsecs = gather_back(dsec)
    gfo, s1, s2, s3, dhid = local_call(
        feed_back_body, [wide, block, block, block, ((512, 768), BF)],
        dsecs + [full_up, full_down, slope], "feed_back",
        [pltpu.VMEM((512, 768), BF)],
    )
    gfo = [gfo] + send_plane([s1, s2, s3])
    fkeep, *fsend = local_call(feed_grad_body, [((784, 768), F32)] + [((192, 768), BF)] * 3 + [((208, 768), BF)], [act, after(low, gfo[2])] + dsecs + [dhid], 'feed_grad', [pltpu.VMEM((768, 768), F32), pltpu.VMEM((512, 768), BF)])
    fsent, ffar, fown, fgot = sum_z(
        stage_feed_body, half_body, (208, 768), [fkeep] + [swap(x) for x in fsend], "feed_grad",
        [pltpu.VMEM((784, 768), F32), pltpu.VMEM((4, 16, 768), F32)],
    )
    grad_one, dbr, t0, t1, t2, t3, sums_one = local_call(first_back_body, [wide, block] + [((128, 192), BF)] * 4 + [((8, 768), F32)], [gfo[0]] + gfo[1:] + [grad_two, hat, inv, vecs, full_out], 'first_back')
    dats = [t0] + send_plane([t1, t2, t3])
    gq, gkeep, gk_send, gv_send = local_call(attend_back_body, [((512, 192), BF), ((512, 384), F32), ((512, 192), BF), ((512, 192), BF)], dats + [after(q, fsent)] + kv + [att, lse], 'attend_back', [pltpu.VMEM((512, 192), BF)], mib=24)
    gk_got, gv_got = (swap(gk_send), swap(gv_send))
    g, qkeep, qsend_a, qsend_b = local_call(inner_weight_body, [((512, 576), BF), ((384, 640), F32), ((192, 640), BF), ((192, 640), BF)], [gq, gkeep, gk_got, gv_got] + xs + [sums_two, sums_one], 'inner_weight', [pltpu.VMEM((768, 640), F32), pltpu.VMEM((128, 768), F32), pltpu.VMEM((512, 768), BF)])
    qsent, qfar_sent, qown, qfar = sum_z(stage_q_body, half_body, (96, 640), [qkeep, swap(qsend_a), swap(qsend_b)], 'q', [pltpu.VMEM((384, 640), F32)])
    dbrs = gather_plane(after(dbr, gq))
    gin, s1, s2, s3 = local_call(inner_input_body, [wide, block, block, block], [after(g, qsent), w_qkv], 'inner_input')
    gin = [gin] + send_plane([s1, s2, s3])
    okeep, osend = local_call(
        out_grad_body, [((96, 768), F32), ((96, 768), BF)], [packed] + dbrs, "out_grad",
        [pltpu.VMEM((192, 768), F32), pltpu.VMEM((512, 192), BF), pltpu.VMEM((512, 768), BF)],
    )
    _, _, oown, ofar = sum_z(stage_out_body, half_out_body, (24, 768), [after(okeep, qsent), swap(after(osend, qsent))], 'out', [pltpu.VMEM((96, 768), F32)], [qfar_sent] + [gin[1]])
    down, up_sum = local_call(join_down_body, [((112, 768), BF), ((96, 768), F32)], [after(fown, gin[1]), fgot], 'join_down')
    down = lax.ppermute(down, ("ctx", "fsdp"), [(4 * i + z, 8 * z + i) for i in range(8) for z in range(4)])
    a0, a1, a2, a3 = local_call(turn_body, [((24, 1408), F32)] + [((24, 1408), BF)] * 3, [qown, qfar, up_sum], 'turn', scratch=[pltpu.VMEM((4, 24, 1408), F32)])
    aa = send_plane([a1, a2, a3])
    g_qk, g_v, g_up, *small = local_call(
        finish_body, [((24, 1536), F32), ((24, 768), F32), ((24, 3072), F32)] + [((24,), F32)] * 8, [a0] + aa, "finish",
        [pltpu.VMEM((4, 24, 1408), F32)], final=range(11),
    )
    g_down, g_out, g_bias_up = local_call(
        finish_down_body, [((96, 768), F32), ((24, 768), F32), ((96,), F32)], [down, oown, ofar], "finish_down",
        final=range(3),
    )
    grad_inputs, = local_call(input_sum_body, [wide], [grad_one] + gin, 'input_sum', final=(0,))
    return (
        out.reshape(1, 128, 768), grad_inputs.reshape(1, 128, 768), g_qk, g_v, g_out, g_up, g_down,
        small[0], small[1], small[4], small[2], small[3], g_bias_up, small[7], small[5], small[6],
    )


def solution(mesh):
    blocks = mesh.shape["ctx"] == 8 and mesh.shape["fsdp"] == 4
    return jax.shard_map(
        per_device_blocks if blocks else per_device,
        mesh=mesh,
        in_specs=(
            P("fsdp", "ctx", None),
            P("fsdp", None),
            P("fsdp", None),
            P("fsdp", None),
            P("fsdp", None),
            P("fsdp", None),
            P("fsdp"),
            P("fsdp"),
            P("fsdp"),
            P("fsdp"),
            P("fsdp"),
            P("fsdp"),
            P("fsdp"),
            P("fsdp"),
            P("fsdp"),
            P("fsdp", "ctx", None),
        ),
        out_specs=(
            P("fsdp", "ctx", None),
            P("fsdp", "ctx", None),
            P(("ctx", "fsdp"), None),
            P(("ctx", "fsdp"), None),
            P(("ctx", "fsdp"), None),
            P(("ctx", "fsdp"), None),
            P(("ctx", "fsdp"), None),
            P(("ctx", "fsdp")),
            P(("ctx", "fsdp")),
            P(("ctx", "fsdp")),
            P(("ctx", "fsdp")),
            P(("ctx", "fsdp")),
            P(("ctx", "fsdp")),
            P(("ctx", "fsdp")),
            P(("ctx", "fsdp")),
            P(("ctx", "fsdp")),
        ),
        check_vma=False,
    )
```
